256 devices in a mesh: gx: 8 (over x, core), gy: 32 (over y, z).
Axes of the slice: x: 4, y: 4, z: 8, core: 2. Of those that a mesh axis runs over, the one named last changes fastest.
Arguments:
- tokens: bfloat16 [256, 8192], P('gy', 'gx'), may hold values from -6 to 6
- norm_gain: float32 [8192], P('gx'), may hold values from 0.5 to 1.5
- query_matrix: bfloat16 [8192, 8192], P('gx', 'gy'), may hold values from -0.0625 to 0.0625
- key_matrix: bfloat16 [8192, 1024], P('gx', 'gy'), may hold values from -0.0625 to 0.0625
- value_matrix: bfloat16 [8192, 1024], P('gx', 'gy'), may hold values from -0.0625 to 0.0625
- output_matrix: bfloat16 [8192, 8192], P('gx', 'gy'), may hold values from -0.0625 to 0.0625
- adapter_down: bfloat16 [64, 8192, 48], P('gy', 'gx'), may hold values from -0.0625 to 0.0625
- query_lift: bfloat16 [64, 16, 8192], P('gx', None, 'gy'), may hold values from -0.75 to 0.75
- key_value_lift: bfloat16 [64, 2, 16, 1024], P('gx', None, None, 'gy'), may hold values from -2.25 to 2.25
- mixer_down: bfloat16 [64, 8192, 16], P('gy', 'gx'), may hold values from -0.0625 to 0.0625
- mixer_lift: bfloat16 [64, 16, 8192], P('gx', None, 'gy'), may hold values from -0.75 to 0.75
- adapter_index: int32 [256], replicated, may hold values from 0 to 63
- suffix_lengths: int32 [256], P(('gx', 'gy')), may hold values from 1 to 2048, 262144 in all
- shared_prefix_keys: bfloat16 [16384, 1024], P('gy'), may hold values from -1000 to 1000
- shared_prefix_values: bfloat16 [16384, 1024], P('gy'), may hold values from -6 to 6
- private_suffix_keys: bfloat16 [256, 2048, 1024], P(('gx', 'gy')), may hold values from -40 to 40
- private_suffix_values: bfloat16 [256, 2048, 1024], P(('gx', 'gy')), may hold values from -6 to 6
Outputs:
- output: bfloat16 [256, 8192], P(('gx', 'gy'))
The draws below stay inside these ranges and needn't reach their ends.
Inputs may be any that keep to these rules, and one draw needn't show every extreme that they name: `adapter_index`: each agent's adapter. `suffix_lengths`: the agents' lengths add up to 262144, and some agent has exactly 2048.
All inputs are finite; a program needn't handle non-finite values. No bound on the sum of `suffix_lengths` on one device may be relied on, other than what follows from the above.
Results may differ from the reference program's by a relative error of at most 0.024.
Values may be sent and summed in bfloat16 or wider, within the bound.
A program may use at most 64 MiB of HBM per device.

```python
import math
import jax
import jax.numpy as jnp
import numpy as np
from jax import lax

MODEL_WIDTH = 8192
QUERY_HEADS = 64
KEY_HEADS = 8
HEAD_SIZE = 128
ADAPTER_RANK = 16
ADAPTER_COUNT = 64
PREFIX_LENGTH = 16384
SUFFIX_LENGTH = 2048
AGENT_COUNT = 256


def draw_scaled_keys(key, shape):
    base_key, scale_key = jax.random.split(key, 2)
    normal_part = jax.random.normal(base_key, shape, jnp.float32)
    row_shape = shape[:-1] + (1,)
    row_scale = jnp.exp(jax.random.uniform(scale_key, row_shape, jnp.float32, math.log(0.3), math.log(1.5)))
    return jnp.clip(normal_part * row_scale, -8.0, 8.0)


def draw_shared_prefix_keys(key, part):
    folded = jax.random.fold_in(key, 3)
    base_rows = draw_scaled_keys(folded, (PREFIX_LENGTH, KEY_HEADS * HEAD_SIZE))
    return jnp.clip(base_rows, -1000.0, 1000.0).astype(jnp.bfloat16)


def draw_private_suffix_keys(key, part):
    return draw_scaled_keys(jax.random.fold_in(key, 7), (AGENT_COUNT, SUFFIX_LENGTH, KEY_HEADS * HEAD_SIZE)).astype(jnp.bfloat16)


def place_ends(values, rng, smallest, high):
    longest = values.shape.index(max(values.shape))
    spots = []
    for shift in (0, 1):
        where = [jax.random.randint(jax.random.fold_in(rng, axis), (), 0, length) for axis, length in enumerate(values.shape)]
        where[longest] = (where[longest] + shift) % values.shape[longest]
        spots.append(tuple(where))
    return values.at[spots[0]].set(smallest).at[spots[1]].set(high)


def block_scale(rng, extent, cuts, low, largest):
    gain = 1.0
    for position, blocks in cuts:
        draws = jax.random.uniform(jax.random.fold_in(jax.random.fold_in(rng, 6), position), (blocks,), jnp.float32, low / len(cuts), largest / len(cuts))
        gain = gain * jnp.repeat(jnp.exp(draws), extent[position] // blocks).reshape((-1,) + (1,) * (len(extent) - 1 - position))
    return gain


def split_up(count, total, bound, slope):
    portions = [(1 << 20) // math.isqrt(rank ** slope) + 1 for rank in range(2, count + 1)]
    surplus, counts = total - bound - (count - 1), [1] * (count - 1)
    while surplus > 0:
        free = [i for i in range(count - 1) if counts[i] < bound]
        whole, budget = sum([portions[i] for i in free]), surplus
        for i in free:
            extra = min(bound - counts[i], max(1, budget * portions[i] // whole), surplus)
            counts[i] = counts[i] + extra
            surplus = surplus - extra
    return np.array([bound] + counts)


def ragged_sizes(rng, count, total, limit, lean):
    if count == 2:
        one = jax.random.randint(rng, (), max(1, total - limit), min(limit, total - 1) + 1)
        return jnp.stack([one, total - one])
    lengths = jnp.asarray(split_up(count, total, limit, lean), jnp.int32)
    couples = (count - 1) // 2
    giver, sink = lengths[1:1 + 2 * couples:2], lengths[2:2 + 2 * couples:2]
    slack = jnp.minimum(giver - 1, limit - sink)
    shifted = jax.random.randint(jax.random.fold_in(rng, 1), (couples,), 0, 1 << 20) % (slack + 1)
    lengths = lengths.at[1:1 + 2 * couples:2].set(giver - shifted).at[2:2 + 2 * couples:2].set(sink + shifted)
    return lengths[jax.random.permutation(jax.random.fold_in(rng, 2), count)]


def scatter_about(rng, dims, scale, bound, shards=(), kind=jnp.bfloat16):
    entries = jax.random.normal(rng, dims, jnp.float32) * scale
    if len(shards) > 0:
        entries = block_scale(rng, dims, shards, -0.22, 0.18) * entries
    return jnp.clip(entries, min=-bound, max=bound).astype(kind)


def setup_inputs(seed: int = 0) -> dict:
    seeds = jax.random.split(jax.random.key(seed), 18)
    return {
        "tokens": scatter_about(seeds[0], (AGENT_COUNT, MODEL_WIDTH), 1.0, 6.0, ((0, 32), (1, 8))),
        "norm_gain": jnp.clip(0.5 + 1.0 * jax.random.uniform(seeds[1], (MODEL_WIDTH,), jnp.float32) ** block_scale(seeds[1], (MODEL_WIDTH,), ((0, 8),), -0.2, 0.2), 0.5, 1.5),
        "query_matrix": scatter_about(seeds[2], (MODEL_WIDTH, QUERY_HEADS * HEAD_SIZE), MODEL_WIDTH ** -0.5, 0.0625, ((0, 8), (1, 32))),
        "key_matrix": scatter_about(seeds[3], (MODEL_WIDTH, KEY_HEADS * HEAD_SIZE), MODEL_WIDTH ** -0.5, 0.0625, ((0, 8), (1, 32))),
        "value_matrix": scatter_about(seeds[4], (MODEL_WIDTH, KEY_HEADS * HEAD_SIZE), MODEL_WIDTH ** -0.5, 0.0625, ((0, 8), (1, 32))),
        "output_matrix": scatter_about(seeds[5], (QUERY_HEADS * HEAD_SIZE, MODEL_WIDTH), (QUERY_HEADS * HEAD_SIZE) ** -0.5, 0.0625, ((0, 8), (1, 32))),
        "adapter_down": scatter_about(seeds[6], (ADAPTER_COUNT, MODEL_WIDTH, 3 * ADAPTER_RANK), MODEL_WIDTH ** -0.5, 0.0625, ((0, 32), (1, 8))),
        "query_lift": scatter_about(seeds[7], (ADAPTER_COUNT, ADAPTER_RANK, QUERY_HEADS * HEAD_SIZE), 0.125, 0.75, ((0, 8), (2, 32))),
        "key_value_lift": scatter_about(seeds[8], (ADAPTER_COUNT, 2, ADAPTER_RANK, KEY_HEADS * HEAD_SIZE), 0.375, 2.25, ((0, 8), (3, 32))),
        "mixer_down": scatter_about(seeds[9], (ADAPTER_COUNT, QUERY_HEADS * HEAD_SIZE, ADAPTER_RANK), (QUERY_HEADS * HEAD_SIZE) ** -0.5, 0.0625, ((0, 32), (1, 8))),
        "mixer_lift": scatter_about(seeds[10], (ADAPTER_COUNT, ADAPTER_RANK, MODEL_WIDTH), 0.125, 0.75, ((0, 8), (2, 32))),
        "adapter_index": place_ends(jax.random.randint(seeds[11], (AGENT_COUNT,), 0, ADAPTER_COUNT), jax.random.fold_in(seeds[11], 1), 0, ADAPTER_COUNT - 1).astype(jnp.int32),
        "suffix_lengths": ragged_sizes(seeds[12], AGENT_COUNT, AGENT_COUNT * SUFFIX_LENGTH // 2, SUFFIX_LENGTH, 2).astype(jnp.int32),
        "shared_prefix_keys": draw_shared_prefix_keys(jax.random.fold_in(seeds[17], 71), 0),
        "shared_prefix_values": scatter_about(seeds[14], (PREFIX_LENGTH, KEY_HEADS * HEAD_SIZE), 1.0, 6.0, ((0, 32),)),
        "private_suffix_keys": draw_private_suffix_keys(jax.random.fold_in(seeds[17], 71), 0),
        "private_suffix_values": scatter_about(seeds[16], (AGENT_COUNT, SUFFIX_LENGTH, KEY_HEADS * HEAD_SIZE), 1.0, 6.0, ((0, 256),)),
    }


EPSILON = 1e-05
ADAPTER_SCALE = 2.0
ROPE_BASE = 500000.0

def apply_rotary(vectors, token_position):
    half_dim = vectors.shape[-1] // 2
    steps = jnp.arange(half_dim).astype(jnp.float32)
    frequency = jnp.power(jnp.float32(ROPE_BASE), -2.0 * steps / vectors.shape[-1])
    angles = token_position[..., None] * frequency
    cosine = jnp.cos(angles)
    sine_part = jnp.sin(angles)
    front_half = vectors[..., :half_dim]
    back_half = vectors[..., half_dim:]
    return jnp.concatenate([front_half * cosine - back_half * sine_part, back_half * cosine + front_half * sine_part], axis=-1)

def spread_token_rows(adapter_update, owners, slots_here):
    selected = (owners[:, None] == jnp.arange(slots_here).astype(jnp.int32)[None, :]).astype(adapter_update.dtype)
    return (selected[:, :, None] * adapter_update[:, None, :]).reshape(adapter_update.shape[0], slots_here * adapter_update.shape[1])

def reference(tokens, norm_gain, query_matrix, key_matrix, value_matrix, output_matrix, adapter_down, query_lift, key_value_lift, mixer_down, mixer_lift, adapter_index, suffix_lengths, shared_prefix_keys, shared_prefix_values, private_suffix_keys, private_suffix_values):
    tokens_f = tokens.astype(jnp.float32)
    squares = lax.optimization_barrier(jnp.sum(tokens_f * tokens_f, axis=1))
    scale_factor = lax.rsqrt(squares / MODEL_WIDTH + EPSILON)
    scaled_scores = (tokens_f * norm_gain[None, :]).astype(jnp.bfloat16)
    chosen = (adapter_index[:, None] == jnp.arange(ADAPTER_COUNT).astype(jnp.int32)[None, :]).astype(jnp.float32)
    down_flat = jnp.transpose(adapter_down, (1, 0, 2)).reshape(MODEL_WIDTH, ADAPTER_COUNT * 3 * ADAPTER_RANK)
    down_all = jnp.dot(scaled_scores, down_flat, preferred_element_type=jnp.float32).reshape(AGENT_COUNT, ADAPTER_COUNT, 3 * ADAPTER_RANK)
    adapter_update = lax.optimization_barrier(jnp.sum(down_all * chosen[:, :, None], axis=1)).astype(jnp.bfloat16)
    query_lifted = jnp.dot(spread_token_rows(adapter_update[:, :ADAPTER_RANK], adapter_index, ADAPTER_COUNT), query_lift.reshape(ADAPTER_COUNT * ADAPTER_RANK, QUERY_HEADS * HEAD_SIZE), preferred_element_type=jnp.float32)
    key_lifted = jnp.dot(spread_token_rows(adapter_update[:, ADAPTER_RANK:2 * ADAPTER_RANK], adapter_index, ADAPTER_COUNT), key_value_lift[:, 0].reshape(ADAPTER_COUNT * ADAPTER_RANK, KEY_HEADS * HEAD_SIZE), preferred_element_type=jnp.float32)
    value_lifted = jnp.dot(spread_token_rows(adapter_update[:, 2 * ADAPTER_RANK:], adapter_index, ADAPTER_COUNT), key_value_lift[:, 1].reshape(ADAPTER_COUNT * ADAPTER_RANK, KEY_HEADS * HEAD_SIZE), preferred_element_type=jnp.float32)
    prefix_query = (jnp.dot(scaled_scores, query_matrix, preferred_element_type=jnp.float32) + ADAPTER_SCALE * query_lifted) * scale_factor[:, None]
    prefix_key_block = (jnp.dot(scaled_scores, key_matrix, preferred_element_type=jnp.float32) + ADAPTER_SCALE * key_lifted) * scale_factor[:, None]
    prefix_value_block = (jnp.dot(scaled_scores, value_matrix, preferred_element_type=jnp.float32) + ADAPTER_SCALE * value_lifted) * scale_factor[:, None]
    token_position = (PREFIX_LENGTH + suffix_lengths).astype(jnp.float32)
    query_vectors = apply_rotary(prefix_query.reshape(AGENT_COUNT, QUERY_HEADS, HEAD_SIZE), token_position[:, None]).astype(jnp.bfloat16)
    fresh_keys = apply_rotary(prefix_key_block.reshape(AGENT_COUNT, KEY_HEADS, HEAD_SIZE), token_position[:, None]).astype(jnp.bfloat16)
    fresh_values = prefix_value_block.reshape(AGENT_COUNT, KEY_HEADS, HEAD_SIZE).astype(jnp.bfloat16)
    group_width = math.gcd(AGENT_COUNT, 16)
    groups_total = AGENT_COUNT // group_width
    heads_per_group = QUERY_HEADS // KEY_HEADS
    inv_root = 1.0 / math.sqrt(HEAD_SIZE)
    prefix_key_rows = shared_prefix_keys.reshape(PREFIX_LENGTH, KEY_HEADS, HEAD_SIZE).astype(jnp.float32)
    prefix_value_rows = shared_prefix_values.reshape(PREFIX_LENGTH, KEY_HEADS, HEAD_SIZE).astype(jnp.float32)

    def attend_token(pieces):
        group_query, group_k, group_v, group_len, agent_keys, agent_values = pieces
        query_float = group_query.reshape(group_width, KEY_HEADS, heads_per_group, HEAD_SIZE).astype(jnp.float32)
        suffix_keys_float = agent_keys.reshape(group_width, SUFFIX_LENGTH, KEY_HEADS, HEAD_SIZE).astype(jnp.float32)
        suffix_values_float = agent_values.reshape(group_width, SUFFIX_LENGTH, KEY_HEADS, HEAD_SIZE).astype(jnp.float32)
        prefix_scores = jnp.einsum('akgd,pkd->akgp', query_float, prefix_key_rows) * inv_root
        suffix_scores = jnp.einsum('akgd,apkd->akgp', query_float, suffix_keys_float) * inv_root
        live_mask = jnp.arange(SUFFIX_LENGTH).astype(jnp.int32)[None, :] < group_len[:, None]
        suffix_scores = jnp.where(live_mask[:, None, None, :], suffix_scores, -jnp.inf)
        new_scores = jnp.einsum('akgd,akd->akg', query_float, group_k.astype(jnp.float32))[..., None] * inv_root
        scores = jnp.concatenate([prefix_scores, suffix_scores, new_scores], axis=-1)
        peak = lax.optimization_barrier(jnp.max(scores, axis=-1, keepdims=True))
        weights = jnp.exp(scores - peak)
        mass = lax.optimization_barrier(jnp.sum(weights, axis=-1))
        rounded = lax.optimization_barrier(weights.astype(jnp.bfloat16)).astype(jnp.float32)
        mixed = jnp.einsum('akgp,pkd->akgd', rounded[..., :PREFIX_LENGTH], prefix_value_rows)
        mixed = mixed + jnp.einsum('akgp,apkd->akgd', rounded[..., PREFIX_LENGTH:PREFIX_LENGTH + SUFFIX_LENGTH], suffix_values_float)
        mixed = mixed + rounded[..., PREFIX_LENGTH + SUFFIX_LENGTH:] * group_v.astype(jnp.float32)[:, :, None, :]
        result = mixed / mass[..., None]
        return result.reshape(group_width, QUERY_HEADS * HEAD_SIZE).astype(jnp.bfloat16)
    decode_attention = lax.map(attend_token, (query_vectors.reshape(groups_total, group_width, QUERY_HEADS, HEAD_SIZE), fresh_keys.reshape(groups_total, group_width, KEY_HEADS, HEAD_SIZE), fresh_values.reshape(groups_total, group_width, KEY_HEADS, HEAD_SIZE), suffix_lengths.reshape(groups_total, group_width), private_suffix_keys.reshape(groups_total, group_width, SUFFIX_LENGTH, KEY_HEADS * HEAD_SIZE), private_suffix_values.reshape(groups_total, group_width, SUFFIX_LENGTH, KEY_HEADS * HEAD_SIZE))).reshape(AGENT_COUNT, QUERY_HEADS * HEAD_SIZE)
    mixer_flat = jnp.transpose(mixer_down, (1, 0, 2)).reshape(QUERY_HEADS * HEAD_SIZE, ADAPTER_COUNT * ADAPTER_RANK)
    mixer_all = jnp.dot(decode_attention, mixer_flat, preferred_element_type=jnp.float32).reshape(AGENT_COUNT, ADAPTER_COUNT, ADAPTER_RANK)
    lowmix = lax.optimization_barrier(jnp.sum(mixer_all * chosen[:, :, None], axis=1)).astype(jnp.bfloat16)
    output_lifted = jnp.dot(spread_token_rows(lowmix, adapter_index, ADAPTER_COUNT), mixer_lift.reshape(ADAPTER_COUNT * ADAPTER_RANK, MODEL_WIDTH), preferred_element_type=jnp.float32)
    output = jnp.dot(decode_attention, output_matrix, preferred_element_type=jnp.float32) + ADAPTER_SCALE * output_lifted
    return output.astype(jnp.bfloat16)
```

```python
import math

import jax
import jax.numpy as jnp
from jax import lax
from jax.experimental import pallas as pl
from jax.experimental.pallas import tpu as pltpu
from jax.sharding import PartitionSpec as P

MODEL_WIDTH = 8192
HEAD_SIZE = 128
PREFIX_LENGTH = 16384
EPSILON = 1e-05
ADAPTER_SCALE = 2.0
ROPE_BASE = 500000.0
RANK = 16

MESH = pl.DeviceIdType.MESH
F32 = jnp.float32
BF16 = jnp.bfloat16
NEG = -1e30


def iota(shape, dim):
    return lax.broadcasted_iota(jnp.int32, shape, dim)


def one_hot(cond):
    return jnp.where(cond, 1.0, 0.0).astype(BF16)


def dot(a, b):
    return jnp.dot(a, b, preferred_element_type=F32)


def dot_t(a, b):
    return lax.dot_general(a, b, (((1,), (1,)), ((), ())), preferred_element_type=F32)


class Net:
    def __init__(self, gx_count, gy_count):
        self.nx, self.ny = gx_count, gy_count
        self.gx, self.gy = lax.axis_index("gx"), lax.axis_index("gy")

    def along(self, axis):
        if axis == "gy":
            return self.gy, self.ny, lambda p: (self.gx, p)
        return self.gx, self.nx, lambda p: (p, self.gy)

    def barrier(self, axes):
        sem = pltpu.get_barrier_semaphore()
        total = 0
        for axis in axes:
            me, n, dev = self.along(axis)
            total += n - 1

            def one(s, c):
                pl.semaphore_signal(sem, inc=1, device_id=dev(lax.rem(me + s, n)), device_id_type=MESH)
                return c

            lax.fori_loop(1, n, one, 0)
        pl.semaphore_wait(sem, total)

    def exchange(self, axis, src_at, dst, slot, ssem, rsem):
        me, n, dev = self.along(axis)

        def copy(peer, target):
            return pltpu.make_async_remote_copy(
                src_ref=src_at(peer), dst_ref=dst.at[slot(target)],
                send_sem=ssem.at[peer], recv_sem=rsem.at[target],
                device_id=dev(peer), device_id_type=MESH)

        def start():
            def one(s, c):
                copy(lax.rem(me + s, n), me).start()
                return c
            lax.fori_loop(1, n, one, 0)

        def wait_recv():
            def one(s, c):
                peer = lax.rem(me + n - s, n)
                copy(peer, peer).wait_recv()
                return c
            lax.fori_loop(1, n, one, 0)

        def wait_send():
            def one(s, c):
                copy(lax.rem(me + s, n), me).wait_send()
                return c
            lax.fori_loop(1, n, one, 0)

        return start, wait_recv, wait_send

    def gather(self, axis, buf, ssem, rsem):
        me, _, _ = self.along(axis)
        return self.exchange(axis, lambda p: buf.at[me], buf, lambda i: i, ssem, rsem)

    def scatter(self, axis, src, dst, ssem, rsem):
        return self.exchange(axis, lambda p: src.at[p], dst, lambda i: i, ssem, rsem)


def index_columns(idx_ref):
    count = idx_ref.shape[1]
    row = jnp.broadcast_to(idx_ref[...].astype(F32), (count, count))
    diagonal = iota((count, count), 0) == iota((count, count), 1)
    return jnp.sum(jnp.where(diagonal, row, 0.0), axis=1, keepdims=True)


def spread(low, pattern, adapter_column):
    wide = dot(low, pattern)
    owner = (iota(wide.shape, 1) // RANK).astype(F32)
    return jnp.where(owner == adapter_column, wide, 0.0).astype(BF16)


def project_body(net, r, q_out, kv_out):
    nx, ny, gx, gy = net.nx, net.ny, net.gx, net.gy
    agents = nx * ny
    tok, lift = r["tok"], r["lift"]
    tok[gy, :, 0:1024] = r["tokens"][...]
    cs = jnp.broadcast_to(r["cs"][...], (nx, 128))
    high = cs.astype(BF16).astype(F32)
    mid = (cs - high).astype(BF16).astype(F32)
    row = iota((nx, 128), 0)
    if nx >= 3:
        low3 = cs - high - mid
        parts = jnp.where(row == 0, high, jnp.where(row == 1, mid, jnp.where(row == 2, low3, 0.0)))
    else:
        parts = jnp.where(row == 0, high, mid)
    tok[gy, :, 1024:1152] = parts.astype(BF16)
    lift[gx] = r["lift_in"][...]
    t_start, t_recv, t_send = net.gather("gy", tok, r["tok_s"], r["tok_r"])
    l_start, l_recv, l_send = net.gather("gx", lift, r["lift_s"], r["lift_r"])
    t_start()
    l_start()
    adapters = index_columns(r["idx"])
    r["cols"][...] = jnp.broadcast_to(adapters, (agents, 128))
    t_recv()
    x = tok[:, :, 0:1024].astype(F32).reshape(agents, 1024)
    squares = jnp.sum(x * x, axis=1, keepdims=True)
    scaled = (x * r["gain"][...]).astype(BF16)
    first = dot(scaled, r["wcat"][...])
    lane = iota((agents, 128), 1)
    base = (gy * 2).astype(F32)
    down = jnp.where(adapters == base, first[:, 0:128],
                     jnp.where(adapters == base + 1.0, first[:, 128:256], 0.0))
    down = jnp.where(lane < 3 * RANK, down, jnp.where(lane == 127, squares, 0.0))
    rows = agents // nx
    r["rl_src"][...] = down.reshape(nx, rows, 128)
    r["rl"][gx] = r["rl_src"][gx]
    rl_start, rl_recv, rl_send = net.scatter("gx", r["rl_src"], r["rl"], r["rl_s"], r["rl_r"])
    rl_start()
    r["rm_src"][:, :, 256:384] = first[:, 0:128].reshape(nx, rows, 128)
    r["rm_src"][:, :, 0:256] = dot(scaled, r["wq"][...]).reshape(nx, rows, 256)
    r["rm"][gx] = r["rm_src"][gx]
    rm_start, rm_recv, rm_send = net.scatter("gx", r["rm_src"], r["rm"], r["rm_s"], r["rm_r"])
    rm_start()
    rl_recv()
    low = jnp.sum(r["rl"][...], axis=0)
    factor = lax.rsqrt(low[:, 127:128] / (nx * 1024) + EPSILON)
    al = r["al"]
    al[gy] = jnp.where(iota((rows, 128), 1) < 3 * RANK, low, 0.0).astype(BF16)
    al_start, al_recv, al_send = net.gather("gy", al, r["al_s"], r["al_r"])
    al_start()
    width = nx * 128
    pattern_row, pattern_rank = iota((128, width), 0), iota((128, width), 1) & (RANK - 1)
    patterns = [one_hot(pattern_row == pattern_rank + part * RANK) for part in range(3)]
    ctab = jnp.sum(tok[:, :, 1024:1152].astype(F32), axis=1)
    turned = pltpu.roll(ctab, 64, 1)
    front = iota(ctab.shape, 1) < 64
    cosines = jnp.where(front, ctab, turned)
    sines = jnp.where(front, -turned, ctab)
    own_adapter = r["cols"][pl.ds(pl.multiple_of(gx * rows, 8), rows), 0:1]
    rm_recv()
    summed = jnp.sum(r["rm"][...], axis=0)
    l_recv()
    lift_all = lift[...].reshape(width, 384)
    al_recv()
    lowrank = jnp.sum(al[...].astype(F32), axis=0).astype(BF16)
    q_up = dot(spread(lowrank, patterns[0], own_adapter), lift_all[:, 0:256])
    k_up = dot(spread(lowrank, patterns[1], own_adapter), lift_all[:, 256:384])
    v_up = dot(spread(lowrank, patterns[2], own_adapter), lift_all[:, 256:384])
    q = (summed[:, 0:256] + ADAPTER_SCALE * q_up) * factor
    kv_up = jnp.where(iota((rows, 128), 1) < 96, k_up, v_up)
    kv_out[...] = (summed[:, 256:384] + ADAPTER_SCALE * kv_up) * factor
    for t in range(2):
        u = q[:, t * 128:(t + 1) * 128]
        q_out[:, t * 128:(t + 1) * 128] = (u * cosines + pltpu.roll(u, 64, 1) * sines).astype(BF16)
    return [t_send, l_send, rl_send, rm_send, al_send]


def attend_body(net, r, q_in, kv_in, att_out):
    nx, ny, gx, gy = net.nx, net.ny, net.gx, net.gy
    rows = ny
    kv_heads = nx
    parts = ny // kv_heads
    inv_root = 1.0 / math.sqrt(HEAD_SIZE)
    qbuf, kvs, kvb, osend, obuf, qp = r["qbuf"], r["kvs"], r["kvb"], r["osend"], r["obuf"], r["qp"]
    qbuf[gy] = q_in[...]
    q_start, q_recv, q_send = net.gather("gy", qbuf, r["q_s"], r["q_r"])
    q_start()
    for i in range(rows):
        kvs[i] = kv_in[i:i + 1, :]

    def place(i):
        return lax.rem(i, parts) * kv_heads + i // parts

    kvb[place(gy)] = kvs[gy]
    k_start, k_recv, k_send = net.exchange("gy", lambda p: kvs.at[p], kvb, place, r["kv_s"], r["kv_r"])
    k_start()
    count = rows * 8
    target, source = iota((count, count), 0), iota((count, count), 1)
    perm = one_hot(source == (target & 7) * rows + (target >> 3))
    lane3 = iota((rows, 8, 128), 2)
    stats = jnp.zeros((rows, 8, 128), F32)
    q_recv()
    for h in range(kv_heads):
        blocks = [qbuf[h * parts + j, :, t * 128:(t + 1) * 128] for j in range(parts) for t in range(2)]
        qh = dot(perm, jnp.concatenate(blocks, axis=0))
        qp[h] = qh.reshape(rows, 8, 128)
        scores = dot_t(qh.astype(BF16), r["pk"][:, h * 128:(h + 1) * 128]) * inv_root
        peak = jnp.max(scores, axis=1, keepdims=True)
        weights = jnp.exp(scores - peak)
        mass = jnp.sum(weights, axis=1, keepdims=True)
        out = dot(weights.astype(BF16), r["pv"][:, h * 128:(h + 1) * 128]) / mass
        osend[h] = out.reshape(rows, 8, 128).astype(BF16)
        here = (lane3 & 7) == h
        stats = jnp.where(here & (lane3 < 24), peak.reshape(rows, 8, 1), stats)
        stats = jnp.where(here & (lane3 >= 24) & (lane3 < 48), mass.reshape(rows, 8, 1), stats)
    high = stats.astype(BF16).astype(F32)
    mid = (stats - high).astype(BF16).astype(F32)
    low = stats - high - mid
    third = (lane3 >> 3)
    third = jnp.where(third >= 3, third - 3, third)
    coded = jnp.where(third == 0, high, jnp.where(third == 1, mid, low))
    osend[kv_heads] = jnp.where(lane3 < 48, coded, 0.0).astype(BF16)
    for h in range(kv_heads + 1):
        obuf[gy, h] = osend[h, gy]
    o_start, o_recv, o_send = net.exchange(
        "gy", lambda p: osend.at[:, p], obuf, lambda i: i, r["o_s"], r["o_r"])
    o_start()
    span = r["sk"].shape[1]
    live = iota((8, span), 1) < r["len"][0]
    lane = iota((8, 128), 1)
    own_peak = jnp.zeros((8, 128), F32)
    own_mass = jnp.zeros((8, 128), F32)
    own_out = []
    for h in range(kv_heads):
        qh = qp[h, gy].astype(BF16)
        scores = dot_t(qh, r["sk"][0, :, h * 128:(h + 1) * 128]) * inv_root
        scores = jnp.where(live, scores, NEG)
        peak = jnp.max(scores, axis=1, keepdims=True)
        weights = jnp.exp(scores - peak)
        mass = jnp.sum(weights, axis=1, keepdims=True)
        own_out.append(dot(weights.astype(BF16), r["sv"][0, :, h * 128:(h + 1) * 128]) / mass)
        own_peak = jnp.where(lane == h, peak, own_peak)
        own_mass = jnp.where(lane == h, mass, own_mass)
    k_recv()
    head_row = iota((kv_heads, 128), 0)
    head_lane = iota((kv_heads, 128), 1)
    new_k = jnp.zeros((kv_heads, 128), F32)
    new_v = jnp.zeros((kv_heads, 128), F32)
    for p in range(parts):
        piece = jnp.zeros((kv_heads, 128), F32)
        for h in range(kv_heads):
            piece = jnp.where(head_row == h, kvb[p * kv_heads + h], piece)
        here = (head_lane >> 5) == p
        new_k = jnp.where(here, pltpu.roll(piece, (32 * p - 64) % 128, 1), new_k)
        new_v = jnp.where(here, pltpu.roll(piece, (32 * p - 96) % 128, 1), new_v)
    ctab = jnp.broadcast_to(r["cs"][...], (kv_heads, 128))
    turned = pltpu.roll(ctab, 64, 1)
    front = head_lane < 64
    cosines = jnp.where(front, ctab, turned)
    sines = jnp.where(front, -turned, ctab)
    new_k = (new_k * cosines + pltpu.roll(new_k, 64, 1) * sines).astype(BF16).astype(F32)
    new_v = new_v.astype(BF16).astype(F32)
    new_score = jnp.zeros((8, 128), F32)
    for h in range(kv_heads):
        s = jnp.sum(qp[h, gy] * new_k[h:h + 1, :], axis=1, keepdims=True) * inv_root
        new_score = jnp.where(lane == h, s, new_score)
    o_recv()
    t = obuf[:, kv_heads].astype(F32)
    flat = t.reshape(ny * 8, 128)
    joined = flat + pltpu.roll(flat, 120, 1) + pltpu.roll(flat, 112, 1)
    valid = iota((ny * 8, 128), 1) < kv_heads
    peaks = jnp.where(valid, joined, 0.0).reshape(ny, 8, 128)
    masses = jnp.where(valid, pltpu.roll(joined, 104, 1), 0.0).reshape(ny, 8, 128)
    top = jnp.maximum(jnp.maximum(jnp.max(peaks, axis=0), own_peak), new_score)
    share = masses * jnp.exp(peaks - top[None])
    own_share = own_mass * jnp.exp(own_peak - top)
    new_share = jnp.exp(new_score - top)
    whole = jnp.sum(share, axis=0) + own_share + new_share
    inverse = 1.0 / jnp.where(lane < kv_heads, whole, 1.0)
    for h in range(kv_heads):
        got = jnp.sum(obuf[:, h].astype(F32) * share[:, :, h:h + 1], axis=0)
        got = got + own_out[h] * own_share[:, h:h + 1] + new_share[:, h:h + 1] * new_v[h:h + 1, :]
        att_out[h] = (got * inverse[:, h:h + 1]).astype(BF16)
    return [q_send, k_send, o_send]


def output_body(net, r, att_in, y_out):
    nx, ny, gx, gy = net.nx, net.ny, net.gx, net.gy
    agents, rows = nx * ny, ny
    ab, arow, ml = r["ab"], r["arow"], r["ml"]
    ab[gx] = att_in[gx]
    a_start, a_recv, a_send = net.exchange("gx", lambda p: att_in.at[p], ab, lambda i: i, r["ab_s"], r["ab_r"])
    a_start()
    ml[gx] = r["ml_in"][...]
    ml_start, ml_recv, ml_send = net.gather("gx", ml, r["ml_s"], r["ml_r"])
    ml_start()
    count = nx * 8
    target, source = iota((count, count), 0), iota((count, count), 1)
    turn = one_hot(source == lax.rem(target, nx) * 8 + target // nx)
    target, source = iota((agents, agents), 0), iota((agents, agents), 1)
    sort_rows = one_hot(source == lax.rem(target, ny) * nx + target // ny)
    adapters = index_columns(r["idx"])
    r["cols2"][...] = jnp.broadcast_to(adapters, (agents, 128))
    a_recv()
    turned = dot(turn, ab[...].astype(F32).reshape(count, 128).astype(BF16))
    for g in range(8):
        arow[gy, :, g * 128:(g + 1) * 128] = turned[g * nx:(g + 1) * nx, :].astype(BF16)
    g_start, g_recv, g_send = net.gather("gy", arow, r["ar_s"], r["ar_r"])
    g_start()
    width = nx * 128
    pattern_row, pattern_rank = iota((128, width), 0), iota((128, width), 1) & (RANK - 1)
    pattern = one_hot(((pattern_row & (RANK - 1)) == pattern_rank) & (pattern_row < 2 * RANK))
    g_recv()
    gathered = arow[...].astype(F32).reshape(agents, 1024).astype(BF16)
    attention = dot(sort_rows, gathered).astype(BF16)
    mixed = dot(attention, r["md"][...])
    lane = iota((agents, 128), 1)
    base = (gy * 2).astype(F32)
    first = (adapters == base) & (lane < RANK)
    second = (adapters == base + 1.0) & (lane >= RANK) & (lane < 2 * RANK)
    r["xl_src"][...] = jnp.where(first | second, mixed, 0.0).reshape(nx, rows, 128)
    r["xl"][gx] = r["xl_src"][gx]
    x_start, x_recv, x_send = net.scatter("gx", r["xl_src"], r["xl"], r["xl_s"], r["xl_r"])
    x_start()
    r["xm_src"][...] = dot(attention, r["wo"][...]).reshape(nx, rows, 256)
    r["xm"][gx] = r["xm_src"][gx]
    m_start, m_recv, m_send = net.scatter("gx", r["xm_src"], r["xm"], r["xm_s"], r["xm_r"])
    m_start()
    x_recv()
    zl = r["zl"]
    zl[gy] = jnp.sum(r["xl"][...], axis=0).astype(BF16)
    z_start, z_recv, z_send = net.gather("gy", zl, r["zl_s"], r["zl_r"])
    z_start()
    own_adapter = r["cols2"][pl.ds(pl.multiple_of(gx * rows, 8), rows), 0:1]
    m_recv()
    summed = jnp.sum(r["xm"][...], axis=0)
    ml_recv()
    lift_all = ml[...].reshape(width, 256)
    z_recv()
    lowmix = jnp.sum(zl[...].astype(F32), axis=0).astype(BF16)
    y = summed + ADAPTER_SCALE * dot(spread(lowmix, pattern, own_adapter), lift_all)
    ys, yb = r["ys"], r["yb"]
    for i in range(rows):
        ys[i] = y[i:i + 1, :]
    yb[gy] = ys[gy]
    y_start, y_recv, y_send = net.scatter("gy", ys, yb, r["y_s"], r["y_r"])
    y_start()
    y_recv()
    for i in range(ny):
        y_out[:, i * 256:(i + 1) * 256] = yb[i].astype(BF16)
    return [a_send, ml_send, g_send, x_send, m_send, z_send, y_send]


def vm(shape, dtype):
    return pltpu.VMEM(shape, dtype)


def pair(names, sizes):
    out = {}
    for name, n in zip(names, sizes):
        out[name + "_s"] = pltpu.SemaphoreType.DMA((n,))
        out[name + "_r"] = pltpu.SemaphoreType.DMA((n,))
    return out


def call(body, inputs, outs, scratch, net_args, axes, collective_id, in_specs=None):
    names_in, names_out, names_scratch = list(inputs), list(outs), list(scratch)

    def kernel(*refs):
        r = dict(zip(names_in + names_out + names_scratch, refs))
        net = Net(*net_args)
        net.barrier(axes)
        for wait in body(net, r):
            wait()

    specs = {n: pl.BlockSpec(memory_space=pltpu.VMEM) for n in names_in}
    specs.update(in_specs or {})
    return pl.pallas_call(
        kernel,
        out_shape=[outs[n] for n in names_out],
        in_specs=[specs[n] for n in names_in],
        out_specs=[pl.BlockSpec(memory_space=pltpu.VMEM)] * len(names_out),
        scratch_shapes=[scratch[n] for n in names_scratch],
        compiler_params=pltpu.CompilerParams(
            collective_id=collective_id, has_side_effects=True, vmem_limit_bytes=40 * 1024 * 1024),
    )(*[inputs[n] for n in names_in])


def make_local(nx, ny):
    agents, rows, width = nx * ny, ny, nx * 128

    def local(tokens, norm_gain, query_matrix, key_matrix, value_matrix, output_matrix, adapter_down,
              query_lift, key_value_lift, mixer_down, mixer_lift, adapter_index, suffix_lengths,
              shared_prefix_keys, shared_prefix_values, private_suffix_keys, private_suffix_values):
        zeros = lambda n, w: jnp.zeros((n, w), BF16)
        wcat = jnp.concatenate(
            [adapter_down[0], zeros(1024, 16), key_matrix, value_matrix, adapter_down[1], zeros(1024, 80)], axis=1)
        lift_in = jnp.concatenate(
            [query_lift.reshape(128, 256), zeros(128, 64),
             key_value_lift[:, 0].reshape(128, 32), key_value_lift[:, 1].reshape(128, 32)], axis=1)
        md = jnp.concatenate([mixer_down[0], mixer_down[1], zeros(1024, 96)], axis=1)
        position = (PREFIX_LENGTH + suffix_lengths).astype(F32)
        steps = jnp.arange(HEAD_SIZE // 2).astype(F32)
        frequency = jnp.power(F32(ROPE_BASE), -2.0 * steps / HEAD_SIZE)
        angles = position[:, None] * frequency[None, :]
        cs = jnp.concatenate([jnp.cos(angles), jnp.sin(angles)], axis=1)
        idx = adapter_index.reshape(1, agents)

        q, kv = call(
            lambda net, r: project_body(net, r, r["q"], r["kv"]),
            dict(tokens=tokens, gain=norm_gain.reshape(1, 1024), wq=query_matrix, wcat=wcat, lift_in=lift_in,
                 idx=idx, cs=cs),
            dict(q=jax.ShapeDtypeStruct((rows, 256), BF16), kv=jax.ShapeDtypeStruct((rows, 128), F32)),
            dict(tok=vm((ny, nx, 1152), BF16), lift=vm((nx, 128, 384), BF16), cols=vm((agents, 128), F32),
                 rl_src=vm((nx, rows, 128), F32), rl=vm((nx, rows, 128), F32),
                 rm_src=vm((nx, rows, 384), F32), rm=vm((nx, rows, 384), F32), al=vm((ny, rows, 128), BF16),
                 **pair(["tok", "lift", "rl", "rm", "al"], [ny, nx, nx, nx, ny])),
            (nx, ny), ("gy", "gx"), 0)
        (att,) = call(
            lambda net, r: attend_body(net, r, r["q"], r["kv"], r["att"]),
            dict(q=q, kv=kv, cs=cs, len=suffix_lengths, pk=shared_prefix_keys, pv=shared_prefix_values,
                 sk=private_suffix_keys, sv=private_suffix_values),
            dict(att=jax.ShapeDtypeStruct((nx, 8, 128), BF16)),
            dict(qbuf=vm((ny, rows, 256), BF16), kvs=vm((rows, 1, 128), F32), kvb=vm((rows, 1, 128), F32),
                 osend=vm((nx + 1, rows, 8, 128), BF16), obuf=vm((ny, nx + 1, 8, 128), BF16),
                 qp=vm((nx, rows, 8, 128), F32), **pair(["q", "kv", "o"], [ny, ny, ny])),
            (nx, ny), ("gy",), 1, dict(len=pl.BlockSpec(memory_space=pltpu.SMEM)))
        (y,) = call(
            lambda net, r: output_body(net, r, r["att"], r["y"]),
            dict(att=att, wo=output_matrix, md=md, ml_in=mixer_lift.reshape(128, 256), idx=idx),
            dict(y=jax.ShapeDtypeStruct((1, ny * 256), BF16)),
            dict(ab=vm((nx, 8, 128), BF16), arow=vm((ny, nx, 1024), BF16), ml=vm((nx, 128, 256), BF16),
                 cols2=vm((agents, 128), F32), xl_src=vm((nx, rows, 128), F32), xl=vm((nx, rows, 128), F32),
                 xm_src=vm((nx, rows, 256), F32), xm=vm((nx, rows, 256), F32), zl=vm((ny, rows, 128), BF16),
                 ys=vm((rows, 1, 256), F32), yb=vm((rows, 1, 256), F32),
                 **pair(["ab", "ml", "ar", "xl", "xm", "zl", "y"], [nx, nx, ny, nx, nx, ny, ny])),
            (nx, ny), ("gy", "gx"), 2)
        return y

    return local


def solution(mesh):
    return jax.shard_map(
        make_local(mesh.shape["gx"], mesh.shape["gy"]),
        mesh=mesh,
        in_specs=(
            P("gy", "gx"),
            P("gx"),
            P("gx", "gy"),
            P("gx", "gy"),
            P("gx", "gy"),
            P("gx", "gy"),
            P("gy", "gx", None),
            P("gx", None, "gy"),
            P("gx", None, None, "gy"),
            P("gy", "gx", None),
            P("gx", None, "gy"),
            P(),
            P(("gx", "gy")),
            P("gy", None),
            P("gy", None),
            P(("gx", "gy"), None, None),
            P(("gx", "gy"), None, None),
        ),
        out_specs=P(("gx", "gy"), None),
        check_vma=False,
    )
```

```python
import math

import jax
import jax.numpy as jnp
from jax import lax
from jax.experimental import pallas as pl
from jax.experimental.pallas import tpu as pltpu
from jax.sharding import PartitionSpec as P

MODEL_WIDTH = 8192
HEAD_SIZE = 128
PREFIX_LENGTH = 16384
EPSILON = 1e-05
ADAPTER_SCALE = 2.0
ROPE_BASE = 500000.0
RANK = 16

MESH = pl.DeviceIdType.MESH
F32 = jnp.float32
BF16 = jnp.bfloat16
NEG = -1e30


def iota(shape, dim):
    return lax.broadcasted_iota(jnp.int32, shape, dim)


def one_hot(cond):
    return jnp.where(cond, 1.0, 0.0).astype(BF16)


def dot(a, b):
    return jnp.dot(a, b, preferred_element_type=F32)


def dot_t(a, b):
    return lax.dot_general(a, b, (((1,), (1,)), ((), ())), preferred_element_type=F32)


class Net:
    def __init__(self, gx_count, gy_count):
        self.nx, self.ny = gx_count, gy_count
        self.gx, self.gy = lax.axis_index("gx"), lax.axis_index("gy")
        self.nz = min(8, gy_count // 2)

    def along(self, axis):
        if axis == "gy":
            return self.gy, self.ny, lambda p: (self.gx, p)
        return self.gx, self.nx, lambda p: (p, self.gy)

    def signal_all(self):
        sem = pltpu.get_barrier_semaphore()
        for axis in ("gy", "gx"):
            me, n, dev = self.along(axis)

            def one(s, c):
                pl.semaphore_signal(sem, inc=1, device_id=dev(lax.rem(me + s, n)), device_id_type=MESH)
                return c

            lax.fori_loop(1, n, one, 0)

    def wait_all(self):
        pl.semaphore_wait(pltpu.get_barrier_semaphore(), self.nx + self.ny - 2)

    def exchange(self, axis, src_at, dst, slot, sems, all_src, all_dst):
        me, n, dev = self.along(axis)

        def start():
            def one(s, c):
                peer = lax.rem(me + s, n)
                pltpu.make_async_remote_copy(
                    src_ref=src_at(peer), dst_ref=dst.at[slot(me)], send_sem=sems.at[0], recv_sem=sems.at[1],
                    device_id=dev(peer), device_id_type=MESH).start()
                return c
            lax.fori_loop(1, n, one, 0)

        def whole():
            return pltpu.make_async_remote_copy(
                src_ref=all_src, dst_ref=all_dst, send_sem=sems.at[0], recv_sem=sems.at[1],
                device_id=dev(lax.rem(me + 1, n)), device_id_type=MESH)

        return start, lambda: whole().wait_recv(), lambda: whole().wait_send()

    def gather(self, axis, buf, sems):
        me, n, _ = self.along(axis)
        part = buf.at[pl.ds(0, n - 1)]
        return self.exchange(axis, lambda p: buf.at[me], buf, lambda i: i, sems, part, part)

    def scatter(self, axis, src, dst, sems):
        _, n, _ = self.along(axis)
        return self.exchange(axis, lambda p: src.at[p], dst, lambda i: i, sems,
                             src.at[pl.ds(0, n - 1)], dst.at[pl.ds(0, n - 1)])

    def relay(self, buf, sems, first_sems):
        nz = self.nz
        ny = self.ny // nz
        y, z = self.gy // nz, lax.rem(self.gy, nz)

        def copy(slot, recv, device):
            return pltpu.make_async_remote_copy(
                src_ref=buf.at[slot], dst_ref=buf.at[slot], send_sem=sems.at[0], recv_sem=recv,
                device_id=(self.gx, device), device_id_type=MESH)

        def send_on(slot):
            def one(t, c):
                copy(slot, sems.at[1], lax.rem(y + t, ny) * nz + z).start()
                return c
            lax.fori_loop(1, ny, one, 0)

        def start():
            def one(t, c):
                copy(self.gy, first_sems.at[z], y * nz + lax.rem(z + t, nz)).start()
                return c
            lax.fori_loop(1, nz, one, 0)
            send_on(self.gy)

        def wait_recv():
            def one(t, c):
                other = lax.rem(z + nz - t, nz)
                copy(y * nz + other, first_sems.at[other], y * nz + other).wait_recv()
                send_on(y * nz + other)
                return c
            lax.fori_loop(1, nz, one, 0)
            far = buf.at[pl.ds(0, (ny - 1) * nz)]
            pltpu.make_async_remote_copy(
                src_ref=far, dst_ref=far, send_sem=sems.at[0], recv_sem=sems.at[1],
                device_id=(self.gx, y * nz + lax.rem(z + 1, nz)), device_id_type=MESH).wait_recv()

        def wait_send():
            part = buf.at[pl.ds(0, self.ny - 1)]
            pltpu.make_async_remote_copy(
                src_ref=part, dst_ref=part, send_sem=sems.at[0], recv_sem=sems.at[1],
                device_id=(self.gx, y * nz + lax.rem(z + 1, nz)), device_id_type=MESH).wait_send()

        return start, wait_recv, wait_send


def index_columns(idx_ref):
    count = idx_ref.shape[1]
    row = jnp.broadcast_to(idx_ref[...].astype(F32), (count, count))
    diagonal = iota((count, count), 0) == iota((count, count), 1)
    return jnp.sum(jnp.where(diagonal, row, 0.0), axis=1, keepdims=True)


def spread(low, pattern, adapter_column):
    wide = dot(low, pattern)
    owner = (iota(wide.shape, 1) // RANK).astype(F32)
    return jnp.where(owner == adapter_column, wide, 0.0).astype(BF16)


def prepare(net, r, load):
    nx, ny, gx, gy = net.nx, net.ny, net.gx, net.gy
    agents = nx * ny
    tok, lift = r["tok"], r["lift"]
    lane = iota((8, 128), 1)
    frequency = jnp.exp((lane & 63).astype(F32) * (-2.0 * math.log(ROPE_BASE) / HEAD_SIZE))
    angles = (PREFIX_LENGTH + r["len"][0]).astype(F32) * frequency
    cs = jnp.where(lane < 64, jnp.cos(angles), jnp.sin(angles))
    r["cs"][...] = cs
    high = cs.astype(BF16).astype(F32)
    mid = (cs - high).astype(BF16).astype(F32)
    row = iota((8, 128), 0)
    parts = jnp.where(row == 0, high, jnp.where(row == 1, mid, jnp.where(row == 2, cs - high - mid, 0.0)))
    load("tokens")
    tok[gy, :, 0:1024] = r["tokens_v"][...]
    tok[gy, :, 1024:1152] = parts[0:nx].astype(BF16)
    ml = r["ml"]
    load("ml_in")
    ml[gx] = r["ml_in_v"][...]
    load("ql")
    load("kvl")
    place = iota((32, 128), 1) - iota((32, 128), 0)
    kvl = r["kvl_v"][...]
    lift[gx, :, 0:256] = r["ql_v"][...]
    lift[gx, :, 256:384] = (dot(kvl[:, 0].reshape(128, 32), one_hot(place == 64))
                            + dot(kvl[:, 1].reshape(128, 32), one_hot(place == 96))).astype(BF16)
    load("idx")
    r["cols"][...] = jnp.broadcast_to(index_columns(r["idx_v"]), (agents, 128))
    wc, md = r["wc"], r["md"]
    for name in ("down", "kt", "vt", "mdt"):
        load(name)
    wc[...] = jnp.zeros(wc.shape, BF16)
    wc[0:48] = r["down_v"][0]
    wc[128:176] = r["down_v"][1]
    wc[64:96] = r["kt_v"][...]
    wc[96:128] = r["vt_v"][...]
    md[...] = jnp.zeros(md.shape, BF16)
    md[0:16] = r["mdt_v"][0]
    md[16:32] = r["mdt_v"][1]


def project(net, r, load):
    nx, ny, gx, gy = net.nx, net.ny, net.gx, net.gy
    agents = nx * ny
    tok, lift = r["tok"], r["lift"]
    t_start, t_recv, t_send = net.relay(tok, r["tok_s"], r["tok_z"])
    l_start, l_recv, l_send = net.gather("gx", lift, r["lift_s"])
    t_start()
    l_start()
    load("gain")
    load("wq")
    t_recv()
    adapters = r["cols"][:, 0:1]
    x = tok[:, :, 0:1024].astype(F32).reshape(agents, 1024)
    scaled = (x * r["gain_v"][...]).astype(BF16)
    first = dot_t(scaled, r["wc"][...])
    squares = jnp.sum(x * x, axis=1, keepdims=True)
    lane = iota((agents, 128), 1)
    base = (gy * 2).astype(F32)
    down = jnp.where(adapters == base, first[:, 0:128],
                     jnp.where(adapters == base + 1.0, first[:, 128:256], 0.0))
    down = jnp.where(lane < 3 * RANK, down, jnp.where(lane == 127, squares, 0.0))
    rows = agents // nx
    r["rl_src"][...] = down.reshape(nx, rows, 128)
    rl_start, rl_recv, rl_send = net.scatter("gx", r["rl_src"], r["rl"], r["rl_s"])
    rl_start()
    r["rl"][gx] = r["rl_src"][gx]
    r["rm_src"][:, :, 256:384] = first[:, 0:128].reshape(nx, rows, 128)
    r["rm_src"][:, :, 0:256] = dot(scaled, r["wq_v"][...]).reshape(nx, rows, 256)
    rm_start, rm_recv, rm_send = net.scatter("gx", r["rm_src"], r["rm"], r["rm_s"])
    rm_start()
    r["rm"][gx] = r["rm_src"][gx]
    rl_recv()
    low = jnp.sum(r["rl"][...], axis=0)
    factor = lax.rsqrt(low[:, 127:128] / (nx * 1024) + EPSILON)
    al = r["al"]
    narrow = jnp.where(iota((rows, 128), 1) < 3 * RANK, low, 0.0)
    half = rows // 2
    al[gy] = (narrow[0:half] + pltpu.roll(narrow[half:rows], 64, 1)).astype(BF16)
    al_start, al_recv, al_send = net.gather("gy", al, r["al_s"])
    al_start()
    width = nx * 128
    pattern_row, pattern_rank = iota((128, width), 0), iota((128, width), 1) & (RANK - 1)
    patterns = [one_hot(pattern_row == pattern_rank + part * RANK) for part in range(3)]
    ctab = jnp.sum(tok[:, :, 1024:1152].astype(F32), axis=1)
    turned = pltpu.roll(ctab, 64, 1)
    front = iota(ctab.shape, 1) < 64
    cosines = jnp.where(front, ctab, turned)
    sines = jnp.where(front, -turned, ctab)
    own_adapter = r["cols"][pl.ds(pl.multiple_of(gx * rows, 8), rows), 0:1]
    rm_recv()
    summed = jnp.sum(r["rm"][...], axis=0)
    l_recv()
    ml_start, ml_recv, ml_send = net.gather("gx", r["ml"], r["ml_s"])
    ml_start()
    lift_all = lift[...].reshape(width, 384)
    al_recv()
    packed = jnp.sum(al[...].astype(F32), axis=0)
    lowrank = jnp.concatenate([packed, pltpu.roll(packed, 64, 1)], axis=0)
    lowrank = jnp.where(iota((rows, 128), 1) < 3 * RANK, lowrank, 0.0).astype(BF16)
    q_up = dot(spread(lowrank, patterns[0], own_adapter), lift_all[:, 0:256])
    k_up = dot(spread(lowrank, patterns[1], own_adapter), lift_all[:, 256:384])
    v_up = dot(spread(lowrank, patterns[2], own_adapter), lift_all[:, 256:384])
    q = (summed[:, 0:256] + ADAPTER_SCALE * q_up) * factor
    kv_up = jnp.where(iota((rows, 128), 1) < 96, k_up, v_up)
    kv = (summed[:, 256:384] + ADAPTER_SCALE * kv_up) * factor
    qbuf = r["qbuf"]
    for t in range(2):
        u = q[:, t * 128:(t + 1) * 128]
        qbuf[gy, :, t * 128:(t + 1) * 128] = (u * cosines + pltpu.roll(u, 64, 1) * sines).astype(BF16)
    return kv, ml_recv, [t_send, l_send, rl_send, rm_send, al_send, ml_send]


def attend(net, r, load, kv):
    nx, ny, gx, gy = net.nx, net.ny, net.gx, net.gy
    rows = ny
    kv_heads = nx
    parts = ny // kv_heads
    inv_root = 1.0 / math.sqrt(HEAD_SIZE)
    qbuf, kvs, kvb, osend, obuf, qp = r["qbuf"], r["kvs"], r["kvb"], r["osend"], r["obuf"], r["qp"]
    att_out = r["att"]
    q_start, q_recv, q_send = net.relay(qbuf, r["q_s"], r["q_z"])
    q_start()
    for i in range(rows):
        kvs[i] = kv[i:i + 1, :]

    def place(i):
        return lax.rem(i, parts) * kv_heads + i // parts

    kvb[place(gy)] = kvs[gy]
    k_start, k_recv, k_send = net.exchange("gy", lambda p: kvs.at[p], kvb, place, r["kv_s"],
                                           kvs.at[pl.ds(0, ny - 1)], kvb.at[pl.ds(0, ny - 1)])
    k_start()
    count = rows * 8
    target, source = iota((count, count), 0), iota((count, count), 1)
    perm = one_hot(source == (target & 7) * rows + (target >> 3))
    lane3 = iota((rows, 8, 128), 2)
    stats = jnp.zeros((rows, 8, 128), F32)
    for name in ("pk", "pv"):
        load(name)
    q_recv()
    for h in range(kv_heads):
        blocks = [qbuf[h * parts + j, :, t * 128:(t + 1) * 128] for j in range(parts) for t in range(2)]
        qh = dot(perm, jnp.concatenate(blocks, axis=0))
        qp[h] = qh.reshape(rows, 8, 128)
        scores = dot_t(qh.astype(BF16), r["pk_v"][:, h * 128:(h + 1) * 128]) * inv_root
        peak = jnp.max(scores, axis=1, keepdims=True)
        weights = jnp.exp(scores - peak)
        mass = jnp.sum(weights, axis=1, keepdims=True)
        out = dot(weights.astype(BF16), r["pv_v"][:, h * 128:(h + 1) * 128]) / mass
        osend[h] = out.reshape(rows, 8, 128).astype(BF16)
        here = (lane3 & 7) == h
        stats = jnp.where(here & (lane3 < 24), peak.reshape(rows, 8, 1), stats)
        stats = jnp.where(here & (lane3 >= 24) & (lane3 < 48), mass.reshape(rows, 8, 1), stats)
    high = stats.astype(BF16).astype(F32)
    mid = (stats - high).astype(BF16).astype(F32)
    low = stats - high - mid
    third = (lane3 >> 3)
    third = jnp.where(third >= 3, third - 3, third)
    coded = jnp.where(third == 0, high, jnp.where(third == 1, mid, low))
    osend[kv_heads] = jnp.where(lane3 < 48, coded, 0.0).astype(BF16)
    for h in range(kv_heads + 1):
        obuf[gy, h] = osend[h, gy]
    o_start, o_recv, o_send = net.exchange(
        "gy", lambda p: osend.at[:, p], obuf, lambda i: i, r["o_s"],
        osend.at[:, pl.ds(0, ny - 1)], obuf.at[pl.ds(0, ny - 1)])
    o_start()
    for name in ("sk", "sv"):
        load(name)
    span = r["sk_v"].shape[1]
    live = iota((8, span), 1) < r["len"][0]
    lane = iota((8, 128), 1)
    own_peak = jnp.zeros((8, 128), F32)
    own_mass = jnp.zeros((8, 128), F32)
    own_out = []
    for h in range(kv_heads):
        qh = qp[h, gy].astype(BF16)
        scores = dot_t(qh, r["sk_v"][0, :, h * 128:(h + 1) * 128]) * inv_root
        scores = jnp.where(live, scores, NEG)
        peak = jnp.max(scores, axis=1, keepdims=True)
        weights = jnp.exp(scores - peak)
        mass = jnp.sum(weights, axis=1, keepdims=True)
        own_out.append(dot(weights.astype(BF16), r["sv_v"][0, :, h * 128:(h + 1) * 128]) / mass)
        own_peak = jnp.where(lane == h, peak, own_peak)
        own_mass = jnp.where(lane == h, mass, own_mass)
    k_recv()
    head_row = iota((kv_heads, 128), 0)
    head_lane = iota((kv_heads, 128), 1)
    new_k = jnp.zeros((kv_heads, 128), F32)
    new_v = jnp.zeros((kv_heads, 128), F32)
    for p in range(parts):
        piece = jnp.zeros((kv_heads, 128), F32)
        for h in range(kv_heads):
            piece = jnp.where(head_row == h, kvb[p * kv_heads + h], piece)
        here = (head_lane >> 5) == p
        new_k = jnp.where(here, pltpu.roll(piece, (32 * p - 64) % 128, 1), new_k)
        new_v = jnp.where(here, pltpu.roll(piece, (32 * p - 96) % 128, 1), new_v)
    ctab = r["cs"][0:kv_heads]
    turned = pltpu.roll(ctab, 64, 1)
    front = head_lane < 64
    cosines = jnp.where(front, ctab, turned)
    sines = jnp.where(front, -turned, ctab)
    new_k = (new_k * cosines + pltpu.roll(new_k, 64, 1) * sines).astype(BF16).astype(F32)
    new_v = new_v.astype(BF16).astype(F32)
    new_score = jnp.zeros((8, 128), F32)
    for h in range(kv_heads):
        s = jnp.sum(qp[h, gy] * new_k[h:h + 1, :], axis=1, keepdims=True) * inv_root
        new_score = jnp.where(lane == h, s, new_score)
    o_recv()
    t = obuf[:, kv_heads].astype(F32)
    flat = t.reshape(ny * 8, 128)
    joined = flat + pltpu.roll(flat, 120, 1) + pltpu.roll(flat, 112, 1)
    valid = iota((ny * 8, 128), 1) < kv_heads
    peaks = jnp.where(valid, joined, 0.0).reshape(ny, 8, 128)
    masses = jnp.where(valid, pltpu.roll(joined, 104, 1), 0.0).reshape(ny, 8, 128)
    top = jnp.maximum(jnp.maximum(jnp.max(peaks, axis=0), own_peak), new_score)
    share = masses * jnp.exp(peaks - top[None])
    own_share = own_mass * jnp.exp(own_peak - top)
    new_share = jnp.exp(new_score - top)
    whole = jnp.sum(share, axis=0) + own_share + new_share
    inverse = 1.0 / jnp.where(lane < kv_heads, whole, 1.0)
    for h in range(kv_heads):
        got = jnp.sum(obuf[:, h].astype(F32) * share[:, :, h:h + 1], axis=0)
        got = got + own_out[h] * own_share[:, h:h + 1] + new_share[:, h:h + 1] * new_v[h:h + 1, :]
        att_out[h] = (got * inverse[:, h:h + 1]).astype(BF16)
    return [q_send, k_send, o_send]


def project_out(net, r, load, ml_recv, y_out):
    nx, ny, gx, gy = net.nx, net.ny, net.gx, net.gy
    agents, rows = nx * ny, ny
    ab, arow, ml = r["ab"], r["arow"], r["ml"]
    att_in = r["att"]
    ab[gx] = att_in[gx]
    a_start, a_recv, a_send = net.scatter("gx", att_in, ab, r["ab_s"])
    a_start()
    count = nx * 8
    target, source = iota((count, count), 0), iota((count, count), 1)
    turn = one_hot(source == lax.rem(target, nx) * 8 + target // nx)
    target, source = iota((agents, agents), 0), iota((agents, agents), 1)
    sort_rows = one_hot(source == lax.rem(target, ny) * nx + target // ny)
    adapters = r["cols"][:, 0:1]
    load("wo")
    a_recv()
    turned = dot(turn, ab[...].astype(F32).reshape(count, 128).astype(BF16))
    for g in range(8):
        arow[gy, :, g * 128:(g + 1) * 128] = turned[g * nx:(g + 1) * nx, :].astype(BF16)
    g_start, g_recv, g_send = net.relay(arow, r["ar_s"], r["ar_z"])
    g_start()
    width = nx * 128
    pattern_row, pattern_rank = iota((128, width), 0), iota((128, width), 1) & (RANK - 1)
    pattern = one_hot(((pattern_row & (RANK - 1)) == pattern_rank) & (pattern_row < 2 * RANK))
    g_recv()
    gathered = arow[...].astype(F32).reshape(agents, 1024).astype(BF16)
    attention = dot(sort_rows, gathered).astype(BF16)
    mixed = dot_t(attention, r["md"][...])
    lane = iota((agents, 128), 1)
    base = (gy * 2).astype(F32)
    first = (adapters == base) & (lane < RANK)
    second = (adapters == base + 1.0) & (lane >= RANK) & (lane < 2 * RANK)
    r["xl_src"][...] = jnp.where(first | second, mixed, 0.0).reshape(nx, rows, 128)
    r["xl"][gx] = r["xl_src"][gx]
    x_start, x_recv, x_send = net.scatter("gx", r["xl_src"], r["xl"], r["xl_s"])
    x_start()
    r["xm_src"][...] = dot(attention, r["wo_v"][...]).reshape(nx, rows, 256)
    r["xm"][gx] = r["xm_src"][gx]
    m_start, m_recv, m_send = net.scatter("gx", r["xm_src"], r["xm"], r["xm_s"])
    m_start()
    x_recv()
    zl = r["zl"]
    zl[gy] = jnp.sum(r["xl"][...], axis=0).astype(BF16)
    z_start, z_recv, z_send = net.gather("gy", zl, r["zl_s"])
    z_start()
    own_adapter = r["cols"][pl.ds(pl.multiple_of(gx * rows, 8), rows), 0:1]
    m_recv()
    summed = jnp.sum(r["xm"][...], axis=0)
    ml_recv()
    lift_all = ml[...].reshape(width, 256)
    z_recv()
    lowmix = jnp.sum(zl[...].astype(F32), axis=0).astype(BF16)
    y = summed + ADAPTER_SCALE * dot(spread(lowmix, pattern, own_adapter), lift_all)
    ys, yb = r["ys"], r["yb"]
    for i in range(rows):
        ys[i] = y[i:i + 1, :]
    yb[gy] = ys[gy]
    y_start, y_recv, y_send = net.scatter("gy", ys, yb, r["y_s"])
    y_start()
    y_recv()
    for i in range(ny):
        y_out[:, i * 256:(i + 1) * 256] = yb[i].astype(BF16)
    return [a_send, g_send, x_send, m_send, z_send, y_send]


def make_local(nx, ny):
    agents, rows = nx * ny, ny
    nz = min(8, ny // 2)
    sem = pltpu.SemaphoreType.DMA

    def local(tokens, norm_gain, query_matrix, key_matrix, value_matrix, output_matrix, adapter_down,
              query_lift, key_value_lift, mixer_down, mixer_lift, adapter_index, suffix_lengths,
              shared_prefix_keys, shared_prefix_values, private_suffix_keys, private_suffix_values):
        arrays = dict(
            tokens=tokens, ml_in=mixer_lift.reshape(128, 256), ql=query_lift.reshape(128, 256), kvl=key_value_lift,
            idx=adapter_index.reshape(1, agents), down=adapter_down.transpose(0, 2, 1), kt=key_matrix.T,
            vt=value_matrix.T, mdt=mixer_down.transpose(0, 2, 1), gain=norm_gain.reshape(1, 1024), wq=query_matrix,
            pk=shared_prefix_keys, pv=shared_prefix_values, sk=private_suffix_keys, sv=private_suffix_values,
            wo=output_matrix)
        scratch = {name + "_v": pltpu.VMEM(a.shape, a.dtype) for name, a in arrays.items()}
        scratch.update({name: pltpu.VMEM(shape, dtype) for name, shape, dtype in [
            ("tok", (ny, nx, 1152), BF16), ("lift", (nx, 128, 384), BF16), ("cols", (agents, 128), F32),
            ("cs", (8, 128), F32), ("wc", (256, 1024), BF16), ("md", (128, 1024), BF16),
            ("rl_src", (nx, rows, 128), F32), ("rl", (nx, rows, 128), F32),
            ("rm_src", (nx, rows, 384), F32), ("rm", (nx, rows, 384), F32), ("al", (ny, rows // 2, 128), BF16),
            ("qbuf", (ny, rows, 256), BF16), ("kvs", (rows, 1, 128), F32), ("kvb", (rows, 1, 128), F32),
            ("osend", (nx + 1, rows, 8, 128), BF16), ("obuf", (ny, nx + 1, 8, 128), BF16),
            ("qp", (nx, rows, 8, 128), F32), ("att", (nx, 8, 128), BF16),
            ("ab", (nx, 8, 128), BF16), ("arow", (ny, nx, 1024), BF16), ("ml", (nx, 128, 256), BF16),
            ("xl_src", (nx, rows, 128), F32), ("xl", (nx, rows, 128), F32),
            ("xm_src", (nx, rows, 256), F32), ("xm", (nx, rows, 256), F32), ("zl", (ny, rows, 128), BF16),
            ("ys", (rows, 1, 256), F32), ("yb", (rows, 1, 256), F32)]})
        phases = ["tok", "lift", "rl", "rm", "al", "q", "kv", "o", "ab", "ar", "ml", "xl", "xm", "zl", "y"]
        scratch.update({name + "_s": sem((2,)) for name in phases})
        scratch.update({name + "_z": sem((nz,)) for name in ("tok", "q", "ar")})
        scratch["loads"] = sem((len(arrays),))
        names, extra = list(arrays), list(scratch)

        def kernel(*refs):
            r = dict(zip(names + ["len", "y_out"] + extra, refs))
            copies = {name: pltpu.make_async_copy(r[name], r[name + "_v"], r["loads"].at[i])
                      for i, name in enumerate(names)}
            net = Net(nx, ny)
            net.signal_all()
            for name in names:
                copies[name].start()
            load = lambda name: copies[name].wait()
            prepare(net, r, load)
            net.wait_all()
            kv, ml_recv, waits = project(net, r, load)
            waits = waits + attend(net, r, load, kv)
            waits = waits + project_out(net, r, load, ml_recv, r["y_out"])
            for wait in waits:
                wait()

        any_space = pl.BlockSpec(memory_space=pl.ANY)
        return pl.pallas_call(
            kernel,
            out_shape=jax.ShapeDtypeStruct((1, ny * 256), BF16),
            in_specs=[any_space] * len(names) + [pl.BlockSpec(memory_space=pltpu.SMEM)],
            out_specs=pl.BlockSpec(memory_space=pltpu.VMEM),
            scratch_shapes=[scratch[n] for n in extra],
            compiler_params=pltpu.CompilerParams(
                collective_id=0, has_side_effects=True, vmem_limit_bytes=48 * 1024 * 1024),
        )(*arrays.values(), suffix_lengths)

    return local


def solution(mesh):
    return jax.shard_map(
        make_local(mesh.shape["gx"], mesh.shape["gy"]),
        mesh=mesh,
        in_specs=(
            P("gy", "gx"),
            P("gx"),
            P("gx", "gy"),
            P("gx", "gy"),
            P("gx", "gy"),
            P("gx", "gy"),
            P("gy", "gx", None),
            P("gx", None, "gy"),
            P("gx", None, None, "gy"),
            P("gy", "gx", None),
            P("gx", None, "gy"),
            P(),
            P(("gx", "gy")),
            P("gy", None),
            P("gy", None),
            P(("gx", "gy"), None, None),
            P(("gx", "gy"), None, None),
        ),
        out_specs=P(("gx", "gy"), None),
        check_vma=False,
    )
```

```python
import math

import jax
import jax.numpy as jnp
from jax import lax
from jax.experimental import pallas as pl
from jax.experimental.pallas import tpu as pltpu
from jax.sharding import PartitionSpec as P

MODEL_WIDTH = 8192
HEAD_SIZE = 128
PREFIX_LENGTH = 16384
EPSILON = 1e-05
ADAPTER_SCALE = 2.0
ROPE_BASE = 500000.0
RANK = 16

MESH = pl.DeviceIdType.MESH
F32 = jnp.float32
BF16 = jnp.bfloat16
NEG = -1e30


def iota(shape, dim):
    return lax.broadcasted_iota(jnp.int32, shape, dim)


def one_hot(cond):
    return jnp.where(cond, 1.0, 0.0).astype(BF16)


def dot(a, b):
    return jnp.dot(a, b, preferred_element_type=F32)


def dot_t(a, b):
    return lax.dot_general(a, b, (((1,), (1,)), ((), ())), preferred_element_type=F32)


class Net:
    def __init__(self, gx_count, gy_count):
        self.nx, self.ny = gx_count, gy_count
        self.gx, self.gy = lax.axis_index("gx"), lax.axis_index("gy")
        self.nz = min(8, gy_count // 2)

    def along(self, axis):
        if axis == "gy":
            return self.gy, self.ny, lambda p: (self.gx, p)
        return self.gx, self.nx, lambda p: (p, self.gy)

    def signal_all(self):
        sem = pltpu.get_barrier_semaphore()
        for axis in ("gy", "gx"):
            me, n, dev = self.along(axis)

            def one(s, c):
                pl.semaphore_signal(sem, inc=1, device_id=dev(lax.rem(me + s, n)), device_id_type=MESH)
                return c

            lax.fori_loop(1, n, one, 0)

    def wait_all(self):
        pl.semaphore_wait(pltpu.get_barrier_semaphore(), self.nx + self.ny - 2)

    def exchange(self, axis, src_at, dst, slot, sems, all_src, all_dst):
        me, n, dev = self.along(axis)

        def start():
            def one(s, c):
                peer = lax.rem(me + s, n)
                pltpu.make_async_remote_copy(
                    src_ref=src_at(peer), dst_ref=dst.at[slot(me)], send_sem=sems.at[0], recv_sem=sems.at[1],
                    device_id=dev(peer), device_id_type=MESH).start()
                return c
            lax.fori_loop(1, n, one, 0)

        def whole():
            return pltpu.make_async_remote_copy(
                src_ref=all_src, dst_ref=all_dst, send_sem=sems.at[0], recv_sem=sems.at[1],
                device_id=dev(lax.rem(me + 1, n)), device_id_type=MESH)

        return start, lambda: whole().wait_recv(), lambda: whole().wait_send()

    def gather(self, axis, buf, sems):
        me, n, _ = self.along(axis)
        part = buf.at[pl.ds(0, n - 1)]
        return self.exchange(axis, lambda p: buf.at[me], buf, lambda i: i, sems, part, part)

    def scatter(self, axis, src, dst, sems):
        _, n, _ = self.along(axis)
        return self.exchange(axis, lambda p: src.at[p], dst, lambda i: i, sems,
                             src.at[pl.ds(0, n - 1)], dst.at[pl.ds(0, n - 1)])

    def relay(self, buf, sems, first_sems):
        nz = self.nz
        ny = self.ny // nz
        y, z = self.gy // nz, lax.rem(self.gy, nz)

        def copy(slot, recv, device):
            return pltpu.make_async_remote_copy(
                src_ref=buf.at[slot], dst_ref=buf.at[slot], send_sem=sems.at[0], recv_sem=recv,
                device_id=(self.gx, device), device_id_type=MESH)

        def send_on(slot):
            def one(t, c):
                copy(slot, sems.at[1], lax.rem(y + t, ny) * nz + z).start()
                return c
            lax.fori_loop(1, ny, one, 0)

        def start():
            def one(t, c):
                copy(self.gy, first_sems.at[z], y * nz + lax.rem(z + t, nz)).start()
                return c
            lax.fori_loop(1, nz, one, 0)
            send_on(self.gy)

        def wait_recv():
            def one(t, c):
                other = lax.rem(z + nz - t, nz)
                copy(y * nz + other, first_sems.at[other], y * nz + other).wait_recv()
                send_on(y * nz + other)
                return c
            lax.fori_loop(1, nz, one, 0)
            far = buf.at[pl.ds(0, (ny - 1) * nz)]
            pltpu.make_async_remote_copy(
                src_ref=far, dst_ref=far, send_sem=sems.at[0], recv_sem=sems.at[1],
                device_id=(self.gx, y * nz + lax.rem(z + 1, nz)), device_id_type=MESH).wait_recv()

        def wait_send():
            part = buf.at[pl.ds(0, self.ny - 1)]
            pltpu.make_async_remote_copy(
                src_ref=part, dst_ref=part, send_sem=sems.at[0], recv_sem=sems.at[1],
                device_id=(self.gx, y * nz + lax.rem(z + 1, nz)), device_id_type=MESH).wait_send()

        return start, wait_recv, wait_send


def index_columns(idx_ref):
    count = idx_ref.shape[1]
    row = jnp.broadcast_to(idx_ref[...].astype(F32), (count, count))
    diagonal = iota((count, count), 0) == iota((count, count), 1)
    return jnp.sum(jnp.where(diagonal, row, 0.0), axis=1, keepdims=True)


def spread(low, pattern, adapter_column):
    wide = dot(low, pattern)
    owner = (iota(wide.shape, 1) // RANK).astype(F32)
    return jnp.where(owner == adapter_column, wide, 0.0).astype(BF16)


def prepare(net, r, load):
    nx, ny, gx, gy = net.nx, net.ny, net.gx, net.gy
    agents = nx * ny
    tok, lift = r["tok"], r["lift"]
    lane = iota((8, 128), 1)
    frequency = jnp.exp((lane & 63).astype(F32) * (-2.0 * math.log(ROPE_BASE) / HEAD_SIZE))
    angles = (PREFIX_LENGTH + r["len"][0]).astype(F32) * frequency
    cs = jnp.where(lane < 64, jnp.cos(angles), jnp.sin(angles))
    r["cs"][...] = cs
    high = cs.astype(BF16).astype(F32)
    mid = (cs - high).astype(BF16).astype(F32)
    row = iota((8, 128), 0)
    parts = jnp.where(row == 0, high, jnp.where(row == 1, mid, jnp.where(row == 2, cs - high - mid, 0.0)))
    load("tokens")
    tok[gy, :, 0:1024] = r["tokens_v"][...]
    tok[gy, :, 1024:1152] = parts[0:nx].astype(BF16)
    ml = r["ml"]
    load("ml_in")
    ml[gx] = r["ml_in_v"][...]
    load("ql")
    load("kvl")
    place = iota((32, 128), 1) - iota((32, 128), 0)
    kvl = r["kvl_v"][...]
    lift[gx, :, 0:256] = r["ql_v"][...]
    lift[gx, :, 256:384] = (dot(kvl[:, 0].reshape(128, 32), one_hot(place == 64))
                            + dot(kvl[:, 1].reshape(128, 32), one_hot(place == 96))).astype(BF16)
    load("idx")
    r["cols"][...] = jnp.broadcast_to(index_columns(r["idx_v"]), (agents, 128))
    wc, md = r["wc"], r["md"]
    for name in ("down", "kt", "vt", "mdt"):
        load(name)
    wc[...] = jnp.zeros(wc.shape, BF16)
    wc[0:48] = r["down_v"][0]
    wc[128:176] = r["down_v"][1]
    wc[64:96] = r["kt_v"][...]
    wc[96:128] = r["vt_v"][...]
    md[...] = jnp.zeros(md.shape, BF16)
    md[0:16] = r["mdt_v"][0]
    md[16:32] = r["mdt_v"][1]


def project(net, r, load):
    nx, ny, gx, gy = net.nx, net.ny, net.gx, net.gy
    agents = nx * ny
    tok, lift = r["tok"], r["lift"]
    t_start, t_recv, t_send = net.relay(tok, r["tok_s"], r["tok_z"])
    l_start, l_recv, l_send = net.gather("gx", lift, r["lift_s"])
    t_start()
    l_start()
    load("gain")
    load("wq")
    t_recv()
    adapters = r["cols"][:, 0:1]
    x = tok[:, :, 0:1024].astype(F32).reshape(agents, 1024)
    scaled = (x * r["gain_v"][...]).astype(BF16)
    first = dot_t(scaled, r["wc"][...])
    squares = jnp.sum(x * x, axis=1, keepdims=True)
    lane = iota((agents, 128), 1)
    base = (gy * 2).astype(F32)
    down = jnp.where(adapters == base, first[:, 0:128],
                     jnp.where(adapters == base + 1.0, first[:, 128:256], 0.0))
    down = jnp.where(lane < 3 * RANK, down, jnp.where(lane == 127, squares, 0.0))
    rows = agents // nx
    r["rl_src"][...] = down.reshape(nx, rows, 128)
    rl_start, rl_recv, rl_send = net.scatter("gx", r["rl_src"], r["rl"], r["rl_s"])
    rl_start()
    r["rl"][gx] = r["rl_src"][gx]
    r["rm_src"][:, :, 256:384] = first[:, 0:128].reshape(nx, rows, 128)
    r["rm_src"][:, :, 0:256] = dot(scaled, r["wq_v"][...]).reshape(nx, rows, 256)
    rm_start, rm_recv, rm_send = net.scatter("gx", r["rm_src"], r["rm"], r["rm_s"])
    rm_start()
    r["rm"][gx] = r["rm_src"][gx]
    rl_recv()
    low = jnp.sum(r["rl"][...], axis=0)
    factor = lax.rsqrt(low[:, 127:128] / (nx * 1024) + EPSILON)
    al = r["al"]
    narrow = jnp.where(iota((rows, 128), 1) < 3 * RANK, low, 0.0)
    half = rows // 2
    al[gy] = (narrow[0:half] + pltpu.roll(narrow[half:rows], 64, 1)).astype(BF16)
    al_start, al_recv, al_send = net.gather("gy", al, r["al_s"])
    al_start()
    width = nx * 128
    pattern_row, pattern_rank = iota((128, width), 0), iota((128, width), 1) & (RANK - 1)
    patterns = [one_hot(pattern_row == pattern_rank + part * RANK) for part in range(3)]
    ctab = jnp.sum(tok[:, :, 1024:1152].astype(F32), axis=1)
    turned = pltpu.roll(ctab, 64, 1)
    front = iota(ctab.shape, 1) < 64
    cosines = jnp.where(front, ctab, turned)
    sines = jnp.where(front, -turned, ctab)
    own_adapter = r["cols"][pl.ds(pl.multiple_of(gx * rows, 8), rows), 0:1]
    rm_recv()
    summed = jnp.sum(r["rm"][...], axis=0)
    l_recv()
    ml_start, ml_recv, ml_send = net.gather("gx", r["ml"], r["ml_s"])
    ml_start()
    lift_all = lift[...].reshape(width, 384)
    al_recv()
    packed = jnp.sum(al[...].astype(F32), axis=0)
    lowrank = jnp.concatenate([packed, pltpu.roll(packed, 64, 1)], axis=0)
    lowrank = jnp.where(iota((rows, 128), 1) < 3 * RANK, lowrank, 0.0).astype(BF16)
    q_up = dot(spread(lowrank, patterns[0], own_adapter), lift_all[:, 0:256])
    k_up = dot(spread(lowrank, patterns[1], own_adapter), lift_all[:, 256:384])
    v_up = dot(spread(lowrank, patterns[2], own_adapter), lift_all[:, 256:384])
    q = (summed[:, 0:256] + ADAPTER_SCALE * q_up) * factor
    kv_up = jnp.where(iota((rows, 128), 1) < 96, k_up, v_up)
    kv = (summed[:, 256:384] + ADAPTER_SCALE * kv_up) * factor
    qbuf = r["qbuf"]
    for t in range(2):
        u = q[:, t * 128:(t + 1) * 128]
        qbuf[gy, :, t * 128:(t + 1) * 128] = (u * cosines + pltpu.roll(u, 64, 1) * sines).astype(BF16)
    return kv, ml_recv, [t_send, l_send, rl_send, rm_send, al_send, ml_send]


def attend(net, r, load, kv):
    nx, ny, gx, gy = net.nx, net.ny, net.gx, net.gy
    rows = ny
    kv_heads = nx
    parts = ny // kv_heads
    inv_root = 1.0 / math.sqrt(HEAD_SIZE)
    qbuf, kvs, kvb, osend, obuf, qp = r["qbuf"], r["kvs"], r["kvb"], r["osend"], r["obuf"], r["qp"]
    att_out = r["att"]
    q_start, q_recv, q_send = net.relay(qbuf, r["q_s"], r["q_z"])
    q_start()
    for i in range(rows):
        kvs[i] = kv[i:i + 1, :]

    def place(i):
        return lax.rem(i, parts) * kv_heads + i // parts

    kvb[place(gy)] = kvs[gy]
    k_start, k_recv, k_send = net.exchange("gy", lambda p: kvs.at[p], kvb, place, r["kv_s"],
                                           kvs.at[pl.ds(0, ny - 1)], kvb.at[pl.ds(0, ny - 1)])
    k_start()
    count = rows * 8
    target, source = iota((count, count), 0), iota((count, count), 1)
    perm = one_hot(source == (target & 7) * rows + (target >> 3))
    lane3 = iota((rows, 8, 128), 2)
    stats = jnp.zeros((rows, 8, 128), F32)
    for name in ("pk", "pv"):
        load(name)
    q_recv()
    for h in range(kv_heads):
        blocks = [qbuf[h * parts + j, :, t * 128:(t + 1) * 128] for j in range(parts) for t in range(2)]
        qh = dot(perm, jnp.concatenate(blocks, axis=0))
        qp[h] = qh.reshape(rows, 8, 128)
        scores = dot_t(qh.astype(BF16), r["pk_v"][:, h * 128:(h + 1) * 128]) * inv_root
        peak = jnp.max(scores, axis=1, keepdims=True)
        weights = jnp.exp(scores - peak)
        mass = jnp.sum(weights, axis=1, keepdims=True)
        out = dot(weights.astype(BF16), r["pv_v"][:, h * 128:(h + 1) * 128]) / mass
        osend[h] = out.reshape(rows, 8, 128).astype(BF16)
        here = (lane3 & 7) == h
        stats = jnp.where(here & (lane3 < 24), peak.reshape(rows, 8, 1), stats)
        stats = jnp.where(here & (lane3 >= 24) & (lane3 < 48), mass.reshape(rows, 8, 1), stats)
    high = stats.astype(BF16).astype(F32)
    mid = (stats - high).astype(BF16).astype(F32)
    low = stats - high - mid
    third = (lane3 >> 3)
    third = jnp.where(third >= 3, third - 3, third)
    coded = jnp.where(third == 0, high, jnp.where(third == 1, mid, low))
    osend[kv_heads] = jnp.where(lane3 < 48, coded, 0.0).astype(BF16)
    for h in range(kv_heads + 1):
        obuf[gy, h] = osend[h, gy]
    o_start, o_recv, o_send = net.exchange(
        "gy", lambda p: osend.at[:, p], obuf, lambda i: i, r["o_s"],
        osend.at[:, pl.ds(0, ny - 1)], obuf.at[pl.ds(0, ny - 1)])
    o_start()
    for name in ("sk", "sv"):
        load(name)
    span = r["sk_v"].shape[1]
    live = iota((8, span), 1) < r["len"][0]
    lane = iota((8, 128), 1)
    own_peak = jnp.zeros((8, 128), F32)
    own_mass = jnp.zeros((8, 128), F32)
    own_out = []
    for h in range(kv_heads):
        qh = qp[h, gy].astype(BF16)
        scores = dot_t(qh, r["sk_v"][0, :, h * 128:(h + 1) * 128]) * inv_root
        scores = jnp.where(live, scores, NEG)
        peak = jnp.max(scores, axis=1, keepdims=True)
        weights = jnp.exp(scores - peak)
        mass = jnp.sum(weights, axis=1, keepdims=True)
        own_out.append(dot(weights.astype(BF16), r["sv_v"][0, :, h * 128:(h + 1) * 128]) / mass)
        own_peak = jnp.where(lane == h, peak, own_peak)
        own_mass = jnp.where(lane == h, mass, own_mass)
    k_recv()
    head_row = iota((kv_heads, 128), 0)
    head_lane = iota((kv_heads, 128), 1)
    new_k = jnp.zeros((kv_heads, 128), F32)
    new_v = jnp.zeros((kv_heads, 128), F32)
    for p in range(parts):
        piece = jnp.zeros((kv_heads, 128), F32)
        for h in range(kv_heads):
            piece = jnp.where(head_row == h, kvb[p * kv_heads + h], piece)
        here = (head_lane >> 5) == p
        new_k = jnp.where(here, pltpu.roll(piece, (32 * p - 64) % 128, 1), new_k)
        new_v = jnp.where(here, pltpu.roll(piece, (32 * p - 96) % 128, 1), new_v)
    ctab = r["cs"][0:kv_heads]
    turned = pltpu.roll(ctab, 64, 1)
    front = head_lane < 64
    cosines = jnp.where(front, ctab, turned)
    sines = jnp.where(front, -turned, ctab)
    new_k = (new_k * cosines + pltpu.roll(new_k, 64, 1) * sines).astype(BF16).astype(F32)
    new_v = new_v.astype(BF16).astype(F32)
    new_score = jnp.zeros((8, 128), F32)
    for h in range(kv_heads):
        s = jnp.sum(qp[h, gy] * new_k[h:h + 1, :], axis=1, keepdims=True) * inv_root
        new_score = jnp.where(lane == h, s, new_score)
    o_recv()
    t = obuf[:, kv_heads].astype(F32)
    flat = t.reshape(ny * 8, 128)
    joined = flat + pltpu.roll(flat, 120, 1) + pltpu.roll(flat, 112, 1)
    valid = iota((ny * 8, 128), 1) < kv_heads
    peaks = jnp.where(valid, joined, 0.0).reshape(ny, 8, 128)
    masses = jnp.where(valid, pltpu.roll(joined, 104, 1), 0.0).reshape(ny, 8, 128)
    top = jnp.maximum(jnp.maximum(jnp.max(peaks, axis=0), own_peak), new_score)
    share = masses * jnp.exp(peaks - top[None])
    own_share = own_mass * jnp.exp(own_peak - top)
    new_share = jnp.exp(new_score - top)
    whole = jnp.sum(share, axis=0) + own_share + new_share
    inverse = 1.0 / jnp.where(lane < kv_heads, whole, 1.0)
    for h in range(kv_heads):
        got = jnp.sum(obuf[:, h].astype(F32) * share[:, :, h:h + 1], axis=0)
        got = got + own_out[h] * own_share[:, h:h + 1] + new_share[:, h:h + 1] * new_v[h:h + 1, :]
        att_out[h] = (got * inverse[:, h:h + 1]).astype(BF16)
    return [q_send, k_send, o_send]


def project_out(net, r, load, ml_recv, y_out):
    nx, ny, gx, gy = net.nx, net.ny, net.gx, net.gy
    agents, rows = nx * ny, ny
    ab, arow, ml = r["ab"], r["arow"], r["ml"]
    att_in = r["att"]
    ab[gx] = att_in[gx]
    a_start, a_recv, a_send = net.scatter("gx", att_in, ab, r["ab_s"])
    a_start()
    count = nx * 8
    target, source = iota((count, count), 0), iota((count, count), 1)
    turn = one_hot(source == lax.rem(target, nx) * 8 + target // nx)
    target, source = iota((agents, agents), 0), iota((agents, agents), 1)
    sort_rows = one_hot(source == lax.rem(target, ny) * nx + target // ny)
    adapters = r["cols"][:, 0:1]
    load("wo")
    a_recv()
    turned = dot(turn, ab[...].astype(F32).reshape(count, 128).astype(BF16))
    for g in range(8):
        arow[gy, :, g * 128:(g + 1) * 128] = turned[g * nx:(g + 1) * nx, :].astype(BF16)
    g_start, g_recv, g_send = net.relay(arow, r["ar_s"], r["ar_z"])
    g_start()
    width = nx * 128
    pattern_row, pattern_rank = iota((128, width), 0), iota((128, width), 1) & (RANK - 1)
    pattern = one_hot(((pattern_row & (RANK - 1)) == pattern_rank) & (pattern_row < 2 * RANK))
    g_recv()
    gathered = arow[...].astype(F32).reshape(agents, 1024).astype(BF16)
    attention = dot(sort_rows, gathered).astype(BF16)
    mixed = dot_t(attention, r["md"][...])
    lane = iota((agents, 128), 1)
    base = (gy * 2).astype(F32)
    first = (adapters == base) & (lane < RANK)
    second = (adapters == base + 1.0) & (lane >= RANK) & (lane < 2 * RANK)
    r["xl_src"][...] = jnp.where(first | second, mixed, 0.0).reshape(nx, rows, 128)
    r["xl"][gx] = r["xl_src"][gx]
    x_start, x_recv, x_send = net.scatter("gx", r["xl_src"], r["xl"], r["xl_s"])
    x_start()
    r["xm_src"][...] = dot(attention, r["wo_v"][...]).reshape(nx, rows, 256)
    r["xm"][gx] = r["xm_src"][gx]
    m_start, m_recv, m_send = net.scatter("gx", r["xm_src"], r["xm"], r["xm_s"])
    m_start()
    x_recv()
    zl = r["zl"]
    zl[gy] = jnp.sum(r["xl"][...], axis=0).astype(BF16)
    z_start, z_recv, z_send = net.gather("gy", zl, r["zl_s"])
    z_start()
    own_adapter = r["cols"][pl.ds(pl.multiple_of(gx * rows, 8), rows), 0:1]
    m_recv()
    summed = jnp.sum(r["xm"][...], axis=0)
    ml_recv()
    lift_all = ml[...].reshape(width, 256)
    z_recv()
    lowmix = jnp.sum(zl[...].astype(F32), axis=0).astype(BF16)
    y = summed + ADAPTER_SCALE * dot(spread(lowmix, pattern, own_adapter), lift_all)
    ys, yb = r["ys"], r["yb"]
    for i in range(rows):
        ys[i] = y[i:i + 1, :]
    yb[gy] = ys[gy]
    y_start, y_recv, y_send = net.scatter("gy", ys, yb, r["y_s"])
    y_start()
    y_recv()
    for i in range(ny):
        y_out[:, i * 256:(i + 1) * 256] = yb[i].astype(BF16)
    return [a_send, g_send, x_send, m_send, z_send, y_send]


def make_local(nx, ny):
    agents, rows = nx * ny, ny
    nz = min(8, ny // 2)
    sem = pltpu.SemaphoreType.DMA

    def local(tokens, norm_gain, query_matrix, key_matrix, value_matrix, output_matrix, adapter_down,
              query_lift, key_value_lift, mixer_down, mixer_lift, adapter_index, suffix_lengths,
              shared_prefix_keys, shared_prefix_values, private_suffix_keys, private_suffix_values):
        arrays = dict(
            tokens=tokens, ml_in=mixer_lift.reshape(128, 256), ql=query_lift.reshape(128, 256), kvl=key_value_lift,
            idx=adapter_index.reshape(1, agents), down=adapter_down.transpose(0, 2, 1), kt=key_matrix.T,
            vt=value_matrix.T, mdt=mixer_down.transpose(0, 2, 1), gain=norm_gain.reshape(1, 1024), wq=query_matrix,
            pk=shared_prefix_keys, pv=shared_prefix_values, sk=private_suffix_keys, sv=private_suffix_values,
            wo=output_matrix)
        scratch = {name + "_v": pltpu.VMEM(a.shape, a.dtype) for name, a in arrays.items()}
        scratch.update({name: pltpu.VMEM(shape, dtype) for name, shape, dtype in [
            ("tok", (ny, nx, 1152), BF16), ("lift", (nx, 128, 384), BF16), ("cols", (agents, 128), F32),
            ("cs", (8, 128), F32), ("wc", (256, 1024), BF16), ("md", (128, 1024), BF16),
            ("rl_src", (nx, rows, 128), F32), ("rl", (nx, rows, 128), F32),
            ("rm_src", (nx, rows, 384), F32), ("rm", (nx, rows, 384), F32), ("al", (ny, rows // 2, 128), BF16),
            ("qbuf", (ny, rows, 256), BF16), ("kvs", (rows, 1, 128), F32), ("kvb", (rows, 1, 128), F32),
            ("osend", (nx + 1, rows, 8, 128), BF16), ("obuf", (ny, nx + 1, 8, 128), BF16),
            ("qp", (nx, rows, 8, 128), F32), ("att", (nx, 8, 128), BF16),
            ("ab", (nx, 8, 128), BF16), ("arow", (ny, nx, 1024), BF16), ("ml", (nx, 128, 256), BF16),
            ("xl_src", (nx, rows, 128), F32), ("xl", (nx, rows, 128), F32),
            ("xm_src", (nx, rows, 256), F32), ("xm", (nx, rows, 256), F32), ("zl", (ny, rows, 128), BF16),
            ("ys", (rows, 1, 256), F32), ("yb", (rows, 1, 256), F32)]})
        phases = ["tok", "lift", "rl", "rm", "al", "q", "kv", "o", "ab", "ar", "ml", "xl", "xm", "zl", "y"]
        scratch.update({name + "_s": sem((2,)) for name in phases})
        scratch.update({name + "_z": sem((nz,)) for name in ("tok", "q", "ar")})
        scratch["loads"] = sem((len(arrays),))
        names, extra = list(arrays), list(scratch)

        def kernel(*refs):
            r = dict(zip(names + ["len", "y_out"] + extra, refs))
            copies = {name: pltpu.make_async_copy(r[name], r[name + "_v"], r["loads"].at[i])
                      for i, name in enumerate(names)}
            net = Net(nx, ny)
            net.signal_all()
            for name in names:
                copies[name].start()
            load = lambda name: copies[name].wait()
            prepare(net, r, load)
            net.wait_all()
            kv, ml_recv, waits = project(net, r, load)
            waits = waits + attend(net, r, load, kv)
            waits = waits + project_out(net, r, load, ml_recv, r["y_out"])
            for wait in waits:
                wait()

        any_space = pl.BlockSpec(memory_space=pl.ANY)
        return pl.pallas_call(
            kernel,
            out_shape=jax.ShapeDtypeStruct((1, ny * 256), BF16),
            in_specs=[any_space] * len(names) + [pl.BlockSpec(memory_space=pltpu.SMEM)],
            out_specs=pl.BlockSpec(memory_space=pltpu.VMEM),
            scratch_shapes=[scratch[n] for n in extra],
            compiler_params=pltpu.CompilerParams(
                collective_id=0, has_side_effects=True, vmem_limit_bytes=60 * 1024 * 1024),
        )(*arrays.values(), suffix_lengths)

    return local


def solution(mesh):
    return jax.shard_map(
        make_local(mesh.shape["gx"], mesh.shape["gy"]),
        mesh=mesh,
        in_specs=(
            P("gy", "gx"),
            P("gx"),
            P("gx", "gy"),
            P("gx", "gy"),
            P("gx", "gy"),
            P("gx", "gy"),
            P("gy", "gx", None),
            P("gx", None, "gy"),
            P("gx", None, None, "gy"),
            P("gy", "gx", None),
            P("gx", None, "gy"),
            P(),
            P(("gx", "gy")),
            P("gy", None),
            P("gy", None),
            P(("gx", "gy"), None, None),
            P(("gx", "gy"), None, None),
        ),
        out_specs=P(("gx", "gy"), None),
        check_vma=False,
    )
```

```python
import math

import jax
import jax.numpy as jnp
from jax import lax
from jax.experimental import pallas as pl
from jax.experimental.pallas import tpu as pltpu
from jax.sharding import PartitionSpec as P

MODEL_WIDTH = 8192
HEAD_SIZE = 128
PREFIX_LENGTH = 16384
EPSILON = 1e-05
ADAPTER_SCALE = 2.0
ROPE_BASE = 500000.0
RANK = 16

MESH = pl.DeviceIdType.MESH
F32 = jnp.float32
BF16 = jnp.bfloat16
NEG = -1e30


def iota(shape, dim):
    return lax.broadcasted_iota(jnp.int32, shape, dim)


def one_hot(cond):
    return jnp.where(cond, 1.0, 0.0).astype(BF16)


def dot(a, b):
    return jnp.dot(a, b, preferred_element_type=F32)


def dot_t(a, b):
    return lax.dot_general(a, b, (((1,), (1,)), ((), ())), preferred_element_type=F32)


class Net:
    def __init__(self, gx_count, gy_count):
        self.nx, self.ny = gx_count, gy_count
        self.gx, self.gy = lax.axis_index("gx"), lax.axis_index("gy")
        self.nz = min(8, gy_count // 2)
        self.phases = []

    def phase(self, start, wait_recv, wait_send):
        done = dict(started=False, received=False)
        self.phases.append((done, wait_recv, wait_send))

        def begin():
            done["started"] = True
            start()

        def receive():
            done["received"] = True
            wait_recv()

        return begin, receive

    def finish(self):
        for done, wait_recv, wait_send in self.phases:
            if done["started"]:
                if not done["received"]:
                    wait_recv()
                wait_send()

    def along(self, axis):
        if axis == "gy":
            return self.gy, self.ny, lambda p: (self.gx, p)
        return self.gx, self.nx, lambda p: (p, self.gy)

    def signal_all(self):
        sem = pltpu.get_barrier_semaphore()
        for axis in ("gy", "gx"):
            me, n, dev = self.along(axis)

            def one(s, c):
                pl.semaphore_signal(sem, inc=1, device_id=dev(lax.rem(me + s, n)), device_id_type=MESH)
                return c

            lax.fori_loop(1, n, one, 0)

    def wait_all(self):
        pl.semaphore_wait(pltpu.get_barrier_semaphore(), self.nx + self.ny - 2)

    def exchange(self, axis, src_at, dst_at, sems, all_src, all_dst):
        me, n, dev = self.along(axis)

        def start():
            def one(s, c):
                peer = lax.rem(me + s, n)
                pltpu.make_async_remote_copy(
                    src_ref=src_at(peer), dst_ref=dst_at(me), send_sem=sems.at[0], recv_sem=sems.at[1],
                    device_id=dev(peer), device_id_type=MESH).start()
                return c
            lax.fori_loop(1, n, one, 0)

        def whole():
            return pltpu.make_async_remote_copy(
                src_ref=all_src, dst_ref=all_dst, send_sem=sems.at[0], recv_sem=sems.at[1],
                device_id=dev(lax.rem(me + 1, n)), device_id_type=MESH)

        return self.phase(start, lambda: whole().wait_recv(), lambda: whole().wait_send())

    def gather(self, axis, buf, sems):
        me, n, _ = self.along(axis)
        part = buf.at[pl.ds(0, n - 1)]
        return self.exchange(axis, lambda p: buf.at[me], lambda i: buf.at[i], sems, part, part)

    def scatter(self, axis, src, dst, sems):
        _, n, _ = self.along(axis)
        return self.exchange(axis, lambda p: src.at[p], lambda i: dst.at[i], sems,
                             src.at[pl.ds(0, n - 1)], dst.at[pl.ds(0, n - 1)])

    def relay(self, buf, sems, first_sems, far_sems):
        nz = self.nz
        ny = self.ny // nz
        y, z = self.gy // nz, lax.rem(self.gy, nz)

        def copy(slot, recv, device):
            return pltpu.make_async_remote_copy(
                src_ref=buf.at[slot], dst_ref=buf.at[slot], send_sem=sems.at[0], recv_sem=recv,
                device_id=(self.gx, device), device_id_type=MESH)

        def send_on(slot):
            def one(t, c):
                copy(slot, far_sems.at[y], lax.rem(y + t, ny) * nz + z).start()
                return c
            lax.fori_loop(1, ny, one, 0)

        def start():
            def one(t, c):
                copy(self.gy, first_sems.at[z], y * nz + lax.rem(z + t, nz)).start()
                return c
            lax.fori_loop(1, nz, one, 0)
            send_on(self.gy)

        def near():
            def one(t, c):
                other = lax.rem(z + nz - t, nz)
                copy(y * nz + other, first_sems.at[other], y * nz + other).wait_recv()
                send_on(y * nz + other)
                return c
            lax.fori_loop(1, nz, one, 0)

        def far(other):
            part = buf.at[pl.ds(other * nz, nz)]
            pltpu.make_async_remote_copy(
                src_ref=part, dst_ref=part, send_sem=sems.at[0], recv_sem=far_sems.at[other],
                device_id=(self.gx, other * nz + z), device_id_type=MESH).wait_recv()

        def wait_recv():
            near()
            for t in range(1, ny):
                far(lax.rem(y + t, ny))

        def wait_send():
            part = buf.at[pl.ds(0, self.ny - 1)]
            pltpu.make_async_remote_copy(
                src_ref=part, dst_ref=part, send_sem=sems.at[0], recv_sem=first_sems.at[0],
                device_id=(self.gx, y * nz + lax.rem(z + 1, nz)), device_id_type=MESH).wait_send()

        begin, receive = self.phase(start, wait_recv, wait_send)
        done = self.phases[-1][0]

        def near_then():
            done["received"] = True
            near()

        return begin, receive, near_then, far


def index_columns(idx_ref):
    count = idx_ref.shape[1]
    row = jnp.broadcast_to(idx_ref[...].astype(F32), (count, count))
    diagonal = iota((count, count), 0) == iota((count, count), 1)
    return jnp.sum(jnp.where(diagonal, row, 0.0), axis=1, keepdims=True)


def spread(low, pattern, adapter_column):
    wide = dot(low, pattern)
    owner = (iota(wide.shape, 1) // RANK).astype(F32)
    return jnp.where(owner == adapter_column, wide, 0.0).astype(BF16)


def prepare(net, r, load):
    nx, ny, gx, gy = net.nx, net.ny, net.gx, net.gy
    agents = nx * ny
    tok, lift = r["tok"], r["lift"]
    lane = iota((8, 128), 1)
    frequency = jnp.exp((lane & 63).astype(F32) * (-2.0 * math.log(ROPE_BASE) / HEAD_SIZE))
    angles = (PREFIX_LENGTH + r["len"][0]).astype(F32) * frequency
    cs = jnp.where(lane < 64, jnp.cos(angles), jnp.sin(angles))
    r["cs"][...] = cs
    high = cs.astype(BF16).astype(F32)
    mid = (cs - high).astype(BF16).astype(F32)
    row = iota((8, 128), 0)
    parts = jnp.where(row == 0, high, jnp.where(row == 1, mid, jnp.where(row == 2, cs - high - mid, 0.0)))
    load("tokens")
    tok[gy, :, 0:1024] = r["tokens_v"][...]
    tok[gy, :, 1024:1152] = parts[0:nx].astype(BF16)
    ml = r["ml"]
    load("ml_in")
    ml[gx] = r["ml_in_v"][...]
    load("ql")
    load("kvl")
    place = iota((32, 128), 1) - iota((32, 128), 0)
    kvl = r["kvl_v"][...]
    lift[gx, :, 0:256] = r["ql_v"][...]
    lift[gx, :, 256:384] = (dot(kvl[:, 0].reshape(128, 32), one_hot(place == 64))
                            + dot(kvl[:, 1].reshape(128, 32), one_hot(place == 96))).astype(BF16)
    load("idx")
    r["cols"][...] = jnp.broadcast_to(index_columns(r["idx_v"]), (agents, 128))
    wc, md = r["wc"], r["md"]
    for name in ("down", "kt", "vt", "mdt"):
        load(name)
    wc[...] = jnp.zeros(wc.shape, BF16)
    wc[0:48] = r["down_v"][0]
    wc[128:176] = r["down_v"][1]
    wc[64:96] = r["kt_v"][...]
    wc[96:128] = r["vt_v"][...]
    md[...] = jnp.zeros(md.shape, BF16)
    md[0:16] = r["mdt_v"][0]
    md[16:32] = r["mdt_v"][1]


def project(net, r, load):
    nx, ny, gx, gy = net.nx, net.ny, net.gx, net.gy
    agents = nx * ny
    tok, lift = r["tok"], r["lift"]
    t_start, t_recv, _, _ = net.relay(tok, r["tok_s"], r["tok_z"], r["tok_f"])
    l_start, l_recv = net.gather("gx", lift, r["lift_s"])
    t_start()
    l_start()
    load("gain")
    load("wq")
    t_recv()
    adapters = r["cols"][:, 0:1]
    x = tok[:, :, 0:1024].astype(F32).reshape(agents, 1024)
    scaled = (x * r["gain_v"][...]).astype(BF16)
    first = dot_t(scaled, r["wc"][...])
    squares = jnp.sum(x * x, axis=1, keepdims=True)
    lane = iota((agents, 128), 1)
    base = (gy * 2).astype(F32)
    down = jnp.where(adapters == base, first[:, 0:128],
                     jnp.where(adapters == base + 1.0, first[:, 128:256], 0.0))
    down = jnp.where(lane < 3 * RANK, down, jnp.where(lane == 3 * RANK, squares, 0.0))
    rows = agents // nx
    half = rows // 2
    down = down.reshape(nx, 2, half, 128)
    r["rl_src"][...] = down[:, 0] + pltpu.roll(down[:, 1].reshape(nx * half, 128), 64, 1).reshape(nx, half, 128)
    rl_start, rl_recv = net.scatter("gx", r["rl_src"], r["rl"], r["rl_s"])
    rl_start()
    r["rl"][gx] = r["rl_src"][gx]
    r["rm_src"][:, :, 256:384] = first[:, 0:128].reshape(nx, rows, 128)
    r["rm_src"][:, :, 0:256] = dot(scaled, r["wq_v"][...]).reshape(nx, rows, 256)
    rm_start, rm_recv = net.scatter("gx", r["rm_src"], r["rm"], r["rm_s"])
    rm_start()
    r["rm"][gx] = r["rm_src"][gx]
    rl_recv()
    low = jnp.sum(r["rl"][...], axis=0)
    al = r["al"]
    al[gy] = low.astype(BF16)
    al_start, al_recv = net.gather("gy", al, r["al_s"])
    al_start()
    width = nx * 128
    pattern_row, pattern_rank = iota((128, width), 0), iota((128, width), 1) & (RANK - 1)
    patterns = [one_hot(pattern_row == pattern_rank + part * RANK) for part in range(3)]
    square_columns = jnp.concatenate([low[:, 48:49], low[:, 112:113]], axis=0)
    factor = lax.rsqrt(square_columns / (nx * 1024) + EPSILON)
    ctab = jnp.sum(tok[:, :, 1024:1152].astype(F32), axis=1)
    turned = pltpu.roll(ctab, 64, 1)
    front = iota(ctab.shape, 1) < 64
    cosines = jnp.where(front, ctab, turned)
    sines = jnp.where(front, -turned, ctab)
    own_adapter = r["cols"][pl.ds(pl.multiple_of(gx * rows, 8), rows), 0:1]
    rm_recv()
    summed = jnp.sum(r["rm"][...], axis=0)
    l_recv()
    ml_start, ml_recv = net.gather("gx", r["ml"], r["ml_s"])
    ml_start()
    lift_all = lift[...].reshape(width, 384)
    al_recv()
    packed = jnp.sum(al[...].astype(F32), axis=0)
    lowrank = jnp.concatenate([packed, pltpu.roll(packed, 64, 1)], axis=0)
    lowrank = jnp.where(iota((rows, 128), 1) < 3 * RANK, lowrank, 0.0).astype(BF16)
    q_up = dot(spread(lowrank, patterns[0], own_adapter), lift_all[:, 0:256])
    k_up = dot(spread(lowrank, patterns[1], own_adapter), lift_all[:, 256:384])
    v_up = dot(spread(lowrank, patterns[2], own_adapter), lift_all[:, 256:384])
    q = (summed[:, 0:256] + ADAPTER_SCALE * q_up) * factor
    kv_up = jnp.where(iota((rows, 128), 1) < 96, k_up, v_up)
    kv = (summed[:, 256:384] + ADAPTER_SCALE * kv_up) * factor
    qbuf = r["qbuf"]
    for t in range(2):
        u = q[:, t * 128:(t + 1) * 128]
        qbuf[gy, :, t * 128:(t + 1) * 128] = (u * cosines + pltpu.roll(u, 64, 1) * sines).astype(BF16)
    return kv, ml_recv


def coded_stats(peak, mass, lane, shift):
    rows = peak.shape[0]
    place = (lane - shift) & 127
    value = jnp.where(place < 24, peak, mass)
    high = value.astype(BF16).astype(F32)
    mid = (value - high).astype(BF16).astype(F32)
    low = value - high - mid
    group = place >> 3
    coded = jnp.where((group == 0) | (group == 3), high, jnp.where((group == 1) | (group == 4), mid, low))
    mine = ((lane & 7) == (iota((rows, 128), 0) & 7)) & (group < 6)
    return jnp.where(mine, coded, 0.0)


def joined_stats(coded):
    peaks = coded + pltpu.roll(coded, 120, 1) + pltpu.roll(coded, 112, 1)
    return peaks, pltpu.roll(peaks, 104, 1)


def attend(net, r, load, kv):
    nx, ny, gx, gy = net.nx, net.ny, net.gx, net.gy
    rows = ny
    kv_heads = nx
    parts = ny // kv_heads
    inv_root = 1.0 / math.sqrt(HEAD_SIZE)
    qbuf, kvs, kvb, osend, obuf, qp = r["qbuf"], r["kvs"], r["kvb"], r["osend"], r["obuf"], r["qp"]
    q_start, _, q_near, q_far = net.relay(qbuf, r["q_s"], r["q_z"], r["q_f"])
    q_start()
    for i in range(rows):
        kvs[i] = kv[i:i + 1, :]

    def place(i):
        return lax.rem(i, parts) * kv_heads + i // parts

    kvb[place(gy)] = kvs[gy]
    k_start, k_recv = net.exchange("gy", lambda p: kvs.at[p], lambda i: kvb.at[place(i)], r["kv_s"],
                                   kvs.at[pl.ds(0, ny - 1)], kvb.at[pl.ds(0, ny - 1)])
    k_start()
    count = rows * 8
    target, source = iota((count, count), 0), iota((count, count), 1)
    perm = one_hot(source == (target & 7) * rows + (target >> 3))
    lanes = iota((count, 128), 1)
    shift = (gy & 15) * 8

    def out_copy(head, agent, row, column):
        return pltpu.make_async_remote_copy(
            src_ref=osend.at[head, agent, pl.ds(0, 10)], dst_ref=obuf.at[row, column, pl.ds(0, 10)],
            send_sem=r["o_s"].at[head], recv_sem=r["o_r"].at[row],
            device_id=(head, agent), device_id_type=MESH)

    def one_head(h):
        columns = pl.ds(pl.multiple_of(h * 128, 128), 128)
        blocks = [qbuf[h * parts + j, :, t * 128:(t + 1) * 128] for j in range(parts) for t in range(2)]
        qh = dot(perm, jnp.concatenate(blocks, axis=0))
        qp[h] = qh.reshape(rows, 8, 128)
        scores = dot_t(qh.astype(BF16), r["pk_v"][:, columns]) * inv_root
        peak = jnp.max(scores, axis=1, keepdims=True)
        weights = jnp.exp(scores - peak)
        mass = jnp.sum(weights, axis=1, keepdims=True)
        out = dot(weights.astype(BF16), r["pv_v"][:, columns]) / mass
        osend[h, :, 0:8, :] = out.reshape(rows, 8, 128).astype(BF16)
        coded = coded_stats(peak, mass, lanes, shift).reshape(rows, 8, 128)
        line = jnp.sum(coded, axis=1, keepdims=True)
        osend[h, :, 8:10, :] = jnp.broadcast_to(line, (rows, 2, 128)).astype(BF16)

        def send(s, c):
            out_copy(h, lax.rem(gy + s, ny), gx, gy).start()
            return c

        lax.fori_loop(jnp.where(h == gx, 1, 0), ny, send, 0)

    for name in ("pk", "pv"):
        load(name)
    nz = net.nz
    y_count, y = ny // nz, gy // nz
    y_heads = nz // parts
    q_near()
    for t in [0] + sorted(range(1, y_count), key=lambda d: min(d, y_count - d)):
        other = lax.rem(y + t, y_count)
        if t:
            q_far(other)
        for i in range(y_heads):
            one_head(other * y_heads + i)
    obuf[gx, gy, 0:10, :] = osend[gx, gy, 0:10, :]
    k_recv()
    head_row = iota((kv_heads, 128), 0)
    head_lane = iota((kv_heads, 128), 1)
    new_k = jnp.zeros((kv_heads, 128), F32)
    new_v = jnp.zeros((kv_heads, 128), F32)
    for p in range(parts):
        piece = jnp.zeros((kv_heads, 128), F32)
        for h in range(kv_heads):
            piece = jnp.where(head_row == h, kvb[p * kv_heads + h], piece)
        here = (head_lane >> 5) == p
        new_k = jnp.where(here, pltpu.roll(piece, (32 * p - 64) % 128, 1), new_k)
        new_v = jnp.where(here, pltpu.roll(piece, (32 * p - 96) % 128, 1), new_v)
    ctab = r["cs"][0:kv_heads]
    turned = pltpu.roll(ctab, 64, 1)
    front = head_lane < 64
    cosines = jnp.where(front, ctab, turned)
    sines = jnp.where(front, -turned, ctab)
    new_k = (new_k * cosines + pltpu.roll(new_k, 64, 1) * sines).astype(BF16).astype(F32)
    new_v = new_v.astype(BF16).astype(F32)
    for name in ("sk", "sv"):
        load(name)
    span = r["sk_v"].shape[1]
    live = iota((8, span), 1) < r["len"][0]
    lane = iota((8, 128), 1)
    ss, sb = r["ss"], r["sb"]
    for h in range(kv_heads):
        q_own = qp[h, gy]
        scores = dot_t(q_own.astype(BF16), r["sk_v"][0, :, h * 128:(h + 1) * 128]) * inv_root
        scores = jnp.where(live, scores, NEG)
        new_score = jnp.sum(q_own * new_k[h:h + 1, :], axis=1, keepdims=True) * inv_root
        peak = jnp.maximum(jnp.max(scores, axis=1, keepdims=True), new_score)
        weights = jnp.exp(scores - peak)
        new_weight = jnp.exp(new_score - peak)
        mass = jnp.sum(weights, axis=1, keepdims=True) + new_weight
        mixed = dot(weights.astype(BF16), r["sv_v"][0, :, h * 128:(h + 1) * 128]) + new_weight * new_v[h:h + 1, :]
        ss[h, 0:8, :] = (mixed / mass).astype(BF16)
        line = jnp.sum(coded_stats(peak, mass, lane, 0), axis=0, keepdims=True)
        ss[h, 8:10, :] = jnp.broadcast_to(line, (2, 128)).astype(BF16)
    sb[gx, 0:10, :] = ss[gx, 0:10, :]
    s_start, s_recv = net.exchange(
        "gx", lambda p: ss.at[p, pl.ds(0, 10)], lambda i: sb.at[i, pl.ds(0, 10)], r["ss_s"],
        ss.at[pl.ds(0, nx - 1), pl.ds(0, 10)], sb.at[pl.ds(0, nx - 1), pl.ds(0, 10)])
    s_start()

    def out_all(ref, t, own_row):
        row = lax.rem(gx + t, nx)
        span_rows = ref.at[row, pl.ds(0, ny - 1 if t == 0 else ny), pl.ds(0, 10)]
        return pltpu.make_async_remote_copy(
            src_ref=span_rows, dst_ref=span_rows, send_sem=r["o_s"].at[row], recv_sem=r["o_r"].at[row],
            device_id=(gx, lax.rem(gy + 1, ny)), device_id_type=MESH)

    def o_recv():
        for t in range(nx):
            out_all(obuf, t, 0).wait_recv()

    def o_send():
        for t in range(nx):
            out_all(osend, t, 0).wait_send()

    o_start, o_recv = net.phase(lambda: None, o_recv, o_send)
    o_start()
    s_recv()
    o_recv()
    sub = iota((8, 128), 0)
    line_row, line_lane = iota((ny, 128), 0), iota((ny, 128), 1)
    here = (line_lane >> 3) == (line_row & 15)
    zero = jnp.zeros((nx, 128), F32)
    halves = max(1, ny // 16)
    size = ny // halves
    agent_row = iota((nx, 128), 0)
    peaks, masses = [jnp.full((nx, 128), NEG, F32)] * halves, [zero] * halves
    own = zero
    for i in range(nx):
        coded = obuf[i, :, 8:10, :].astype(F32)[:, 0, :]
        peak, mass = joined_stats(coded)
        peak, mass = jnp.where(here, peak, 0.0), jnp.where(here, mass, 0.0)
        for k in range(halves):
            part = slice(k * size, (k + 1) * size)
            peaks[k] = jnp.where(agent_row == i, jnp.sum(peak[part], axis=0, keepdims=True), peaks[k])
            masses[k] = jnp.where(agent_row == i, jnp.sum(mass[part], axis=0, keepdims=True), masses[k])
        own = jnp.where(agent_row == i, sb[i, 8:10, :].astype(F32)[0:1, :], own)
    if size < 16:
        there = iota((nx, 128), 1) < size * 8
        peaks = [jnp.where(there, p, NEG) for p in peaks]
    own_peak, own_mass = joined_stats(own)
    first = iota((nx, 128), 1) < 8
    own_peak, own_mass = jnp.where(first, own_peak, 0.0), jnp.where(first, own_mass, 0.0)
    for step in (8, 16, 32, 64):
        own_peak = own_peak + pltpu.roll(own_peak, step, 1)
        own_mass = own_mass + pltpu.roll(own_mass, step, 1)
    top = peaks[0]
    for p in peaks[1:]:
        top = jnp.maximum(top, p)
    for step in (8, 16, 32, 64):
        top = jnp.maximum(top, pltpu.roll(top, step, 1))
    top = jnp.maximum(top, own_peak)
    shares = [m * jnp.exp(p - top) for m, p in zip(masses, peaks)]
    own_share = own_mass * jnp.exp(own_peak - top)
    whole = shares[0]
    for share in shares[1:]:
        whole = whole + share
    for step in (8, 16, 32, 64):
        whole = whole + pltpu.roll(whole, step, 1)
    inverse = 1.0 / (whole + own_share)
    diagonal = (lane & 7) == sub
    att = r["att"]
    for i in range(nx):
        wide = jnp.concatenate(
            [jnp.where(diagonal, share[i:i + 1, :] * inverse[i:i + 1, :], 0.0) for share in shares], axis=1)
        wide = wide[:, 0:ny * 8]
        high = wide.astype(BF16)
        both = jnp.concatenate([high.astype(F32), wide - high.astype(F32)], axis=0).astype(BF16)
        values = obuf[i, :, 0:8, :].astype(F32).reshape(ny * 8, 128).astype(BF16)
        mixed = dot(both, values)
        column = jnp.sum(jnp.where(lane == sub, own_share[i:i + 1, :] * inverse[i:i + 1, :], 0.0),
                         axis=1, keepdims=True)
        att[i] = mixed[0:8] + mixed[8:16] + column * sb[i, 0:8, :].astype(F32)


def project_out(net, r, load, ml_recv, y_out):
    nx, ny, gx, gy = net.nx, net.ny, net.gx, net.gy
    agents, rows = nx * ny, ny
    arow, ml = r["arow"], r["ml"]
    count = nx * 8
    target, source = iota((count, count), 0), iota((count, count), 1)
    turn = one_hot(source == lax.rem(target, nx) * 8 + target // nx)
    target, source = iota((agents, agents), 0), iota((agents, agents), 1)
    sort_rows = one_hot(source == lax.rem(target, ny) * nx + target // ny)
    adapters = r["cols"][:, 0:1]
    load("wo")
    turned = dot(turn, r["att"][...].reshape(count, 128).astype(BF16))
    for g in range(8):
        arow[gy, :, g * 128:(g + 1) * 128] = turned[g * nx:(g + 1) * nx, :].astype(BF16)
    g_start, g_recv, _, _ = net.relay(arow, r["ar_s"], r["ar_z"], r["ar_f"])
    g_start()
    width = nx * 128
    pattern_row, pattern_rank = iota((128, width), 0), iota((128, width), 1) & (RANK - 1)
    pattern = one_hot(((pattern_row & (RANK - 1)) == pattern_rank) & (pattern_row < 2 * RANK))
    g_recv()
    gathered = arow[...].astype(F32).reshape(agents, 1024).astype(BF16)
    attention = dot(sort_rows, gathered).astype(BF16)
    mixed = dot_t(attention, r["md"][...])
    lane = iota((agents, 128), 1)
    base = (gy * 2).astype(F32)
    first = (adapters == base) & (lane < RANK)
    second = (adapters == base + 1.0) & (lane >= RANK) & (lane < 2 * RANK)
    quarter = rows // 4
    mixed = jnp.where(first | second, mixed, 0.0).reshape(nx, 4, quarter, 128)
    packed = mixed[:, 0]
    for k in range(1, 4):
        turned = pltpu.roll(mixed[:, k].reshape(nx * quarter, 128), 32 * k, 1)
        packed = packed + turned.reshape(nx, quarter, 128)
    r["xl_src"][...] = packed
    r["xl"][gx] = r["xl_src"][gx]
    x_start, x_recv = net.scatter("gx", r["xl_src"], r["xl"], r["xl_s"])
    x_start()
    r["xm_src"][...] = dot(attention, r["wo_v"][...]).reshape(nx, rows, 256)
    r["xm"][gx] = r["xm_src"][gx]
    m_start, m_recv = net.scatter("gx", r["xm_src"], r["xm"], r["xm_s"])
    m_start()
    x_recv()
    zl = r["zl"]
    zl[gy] = jnp.sum(r["xl"][...], axis=0).astype(BF16)
    z_start, z_recv = net.gather("gy", zl, r["zl_s"])
    z_start()
    own_adapter = r["cols"][pl.ds(pl.multiple_of(gx * rows, 8), rows), 0:1]
    m_recv()
    summed = jnp.sum(r["xm"][...], axis=0)
    ml_recv()
    lift_all = ml[...].reshape(width, 256)
    z_recv()
    packed = jnp.sum(zl[...].astype(F32), axis=0)
    lowmix = jnp.concatenate([packed] + [pltpu.roll(packed, 128 - 32 * k, 1) for k in range(1, 4)], axis=0)
    lowmix = jnp.where(iota((rows, 128), 1) < 2 * RANK, lowmix, 0.0).astype(BF16)
    y = summed + ADAPTER_SCALE * dot(spread(lowmix, pattern, own_adapter), lift_all)
    ys, yb = r["ys"], r["yb"]
    for i in range(rows):
        ys[i] = y[i:i + 1, :]
    yb[gy] = ys[gy]
    y_start, y_recv = net.scatter("gy", ys, yb, r["y_s"])
    y_start()
    y_recv()
    for i in range(ny):
        y_out[:, i * 256:(i + 1) * 256] = yb[i].astype(BF16)


def make_local(nx, ny):
    agents, rows = nx * ny, ny
    nz = min(8, ny // 2)
    sem = pltpu.SemaphoreType.DMA

    def local(tokens, norm_gain, query_matrix, key_matrix, value_matrix, output_matrix, adapter_down,
              query_lift, key_value_lift, mixer_down, mixer_lift, adapter_index, suffix_lengths,
              shared_prefix_keys, shared_prefix_values, private_suffix_keys, private_suffix_values):
        arrays = dict(
            tokens=tokens, ml_in=mixer_lift.reshape(128, 256), ql=query_lift.reshape(128, 256), kvl=key_value_lift,
            idx=adapter_index.reshape(1, agents), down=adapter_down.transpose(0, 2, 1), kt=key_matrix.T,
            vt=value_matrix.T, mdt=mixer_down.transpose(0, 2, 1), gain=norm_gain.reshape(1, 1024), wq=query_matrix,
            pk=shared_prefix_keys, pv=shared_prefix_values, sk=private_suffix_keys, sv=private_suffix_values,
            wo=output_matrix)
        scratch = {name + "_v": pltpu.VMEM(a.shape, a.dtype) for name, a in arrays.items()}
        scratch.update({name: pltpu.VMEM(shape, dtype) for name, shape, dtype in [
            ("tok", (ny, nx, 1152), BF16), ("lift", (nx, 128, 384), BF16), ("cols", (agents, 128), F32),
            ("cs", (8, 128), F32), ("wc", (256, 1024), BF16), ("md", (128, 1024), BF16),
            ("rl_src", (nx, rows // 2, 128), F32), ("rl", (nx, rows // 2, 128), F32),
            ("rm_src", (nx, rows, 384), F32), ("rm", (nx, rows, 384), F32), ("al", (ny, rows // 2, 128), BF16),
            ("qbuf", (ny, rows, 256), BF16), ("kvs", (rows, 1, 128), F32), ("kvb", (rows, 1, 128), F32),
            ("osend", (nx, rows, 16, 128), BF16), ("obuf", (nx, ny, 16, 128), BF16),
            ("ss", (nx, 16, 128), BF16), ("sb", (nx, 16, 128), BF16),
            ("qp", (nx, rows, 8, 128), F32), ("att", (nx, 8, 128), F32),
            ("arow", (ny, nx, 1024), BF16), ("ml", (nx, 128, 256), BF16),
            ("xl_src", (nx, rows // 4, 128), F32), ("xl", (nx, rows // 4, 128), F32),
            ("xm_src", (nx, rows, 256), F32), ("xm", (nx, rows, 256), F32), ("zl", (ny, rows // 4, 128), BF16),
            ("ys", (rows, 1, 256), F32), ("yb", (rows, 1, 256), F32)]})
        phases = ["tok", "lift", "rl", "rm", "al", "q", "kv", "ss", "ar", "ml", "xl", "xm", "zl", "y"]
        scratch.update({name + "_s": sem((2,)) for name in phases})
        scratch.update({name + "_z": sem((nz,)) for name in ("tok", "q", "ar")})
        scratch.update({name + "_f": sem((ny // nz,)) for name in ("tok", "q", "ar")})
        scratch.update(o_s=sem((nx,)), o_r=sem((nx,)))
        scratch["loads"] = sem((len(arrays),))
        names, extra = list(arrays), list(scratch)

        def kernel(*refs):
            r = dict(zip(names + ["len", "y_out"] + extra, refs))
            copies = {name: pltpu.make_async_copy(r[name], r[name + "_v"], r["loads"].at[i])
                      for i, name in enumerate(names)}
            net = Net(nx, ny)
            net.signal_all()
            for name in names:
                copies[name].start()
            load = lambda name: copies[name].wait()
            prepare(net, r, load)
            net.wait_all()
            kv, ml_recv = project(net, r, load)
            attend(net, r, load, kv)
            project_out(net, r, load, ml_recv, r["y_out"])
            net.finish()

        any_space = pl.BlockSpec(memory_space=pl.ANY)
        return pl.pallas_call(
            kernel,
            out_shape=jax.ShapeDtypeStruct((1, ny * 256), BF16),
            in_specs=[any_space] * len(names) + [pl.BlockSpec(memory_space=pltpu.SMEM)],
            out_specs=pl.BlockSpec(memory_space=pltpu.VMEM),
            scratch_shapes=[scratch[n] for n in extra],
            compiler_params=pltpu.CompilerParams(
                collective_id=0, has_side_effects=True, vmem_limit_bytes=60 * 1024 * 1024),
        )(*arrays.values(), suffix_lengths)

    return local


def solution(mesh):
    return jax.shard_map(
        make_local(mesh.shape["gx"], mesh.shape["gy"]),
        mesh=mesh,
        in_specs=(
            P("gy", "gx"),
            P("gx"),
            P("gx", "gy"),
            P("gx", "gy"),
            P("gx", "gy"),
            P("gx", "gy"),
            P("gy", "gx", None),
            P("gx", None, "gy"),
            P("gx", None, None, "gy"),
            P("gy", "gx", None),
            P("gx", None, "gy"),
            P(),
            P(("gx", "gy")),
            P("gy", None),
            P("gy", None),
            P(("gx", "gy"), None, None),
            P(("gx", "gy"), None, None),
        ),
        out_specs=P(("gx", "gy"), None),
        check_vma=False,
    )
```

```python
import math

import jax
import jax.numpy as jnp
from jax import lax
from jax.experimental import pallas as pl
from jax.experimental.pallas import tpu as pltpu
from jax.sharding import PartitionSpec as P

MODEL_WIDTH = 8192
HEAD_SIZE = 128
PREFIX_LENGTH = 16384
EPSILON = 1e-05
ADAPTER_SCALE = 2.0
ROPE_BASE = 500000.0
RANK = 16

MESH = pl.DeviceIdType.MESH
F32 = jnp.float32
BF16 = jnp.bfloat16
NEG = -1e30


def iota(shape, dim):
    return lax.broadcasted_iota(jnp.int32, shape, dim)


def one_hot(cond):
    return jnp.where(cond, 1.0, 0.0).astype(BF16)


def dot(a, b):
    return jnp.dot(a, b, preferred_element_type=F32)


def dot_t(a, b):
    return lax.dot_general(a, b, (((1,), (1,)), ((), ())), preferred_element_type=F32)


class Net:
    def __init__(self, gx_count, gy_count):
        self.nx, self.ny = gx_count, gy_count
        self.gx, self.gy = lax.axis_index("gx"), lax.axis_index("gy")
        self.nz = min(8, gy_count // 2)
        self.y, self.z = self.gy // self.nz, lax.rem(self.gy, self.nz)
        self.phases = []

    def phase(self, start, wait_recv, wait_send):
        done = dict(started=False, received=False)
        self.phases.append((done, wait_recv, wait_send))

        def begin():
            done["started"] = True
            start()

        def receive():
            done["received"] = True
            wait_recv()

        return begin, receive

    def finish(self):
        for done, wait_recv, wait_send in self.phases:
            if done["started"]:
                if not done["received"]:
                    wait_recv()
                wait_send()

    def along(self, axis):
        if axis == "gy":
            return self.gy, self.ny, lambda p: (self.gx, p)
        if axis == "z":
            return self.z, self.nz, lambda p: (self.gx, self.y * self.nz + p)
        if axis == "y":
            return self.y, self.ny // self.nz, lambda p: (self.gx, p * self.nz + self.z)
        return self.gx, self.nx, lambda p: (p, self.gy)

    def signal_all(self):
        sem = pltpu.get_barrier_semaphore()
        for axis in ("gy", "gx"):
            me, n, dev = self.along(axis)

            def one(s, c):
                pl.semaphore_signal(sem, inc=1, device_id=dev(lax.rem(me + s, n)), device_id_type=MESH)
                return c

            lax.fori_loop(1, n, one, 0)

    def wait_all(self):
        pl.semaphore_wait(pltpu.get_barrier_semaphore(), self.nx + self.ny - 2)

    def exchange(self, axis, src_at, dst_at, sems, all_src, all_dst):
        me, n, dev = self.along(axis)

        def start():
            def one(s, c):
                peer = lax.rem(me + s, n)
                pltpu.make_async_remote_copy(
                    src_ref=src_at(peer), dst_ref=dst_at(me), send_sem=sems.at[0], recv_sem=sems.at[1],
                    device_id=dev(peer), device_id_type=MESH).start()
                return c
            lax.fori_loop(1, n, one, 0)

        def whole():
            return pltpu.make_async_remote_copy(
                src_ref=all_src, dst_ref=all_dst, send_sem=sems.at[0], recv_sem=sems.at[1],
                device_id=dev(lax.rem(me + 1, n)), device_id_type=MESH)

        return self.phase(start, lambda: whole().wait_recv(), lambda: whole().wait_send())

    def gather(self, axis, buf, sems):
        me, n, _ = self.along(axis)
        part = buf.at[pl.ds(0, n - 1)]
        return self.exchange(axis, lambda p: buf.at[me], lambda i: buf.at[i], sems, part, part)

    def scatter(self, axis, src, dst, sems):
        _, n, _ = self.along(axis)
        return self.exchange(axis, lambda p: src.at[p], lambda i: dst.at[i], sems,
                             src.at[pl.ds(0, n - 1)], dst.at[pl.ds(0, n - 1)])

    def relay(self, buf, sems, first_sems, far_sems):
        nz = self.nz
        ny = self.ny // nz
        y, z = self.gy // nz, lax.rem(self.gy, nz)

        def copy(slot, recv, device):
            return pltpu.make_async_remote_copy(
                src_ref=buf.at[slot], dst_ref=buf.at[slot], send_sem=sems.at[0], recv_sem=recv,
                device_id=(self.gx, device), device_id_type=MESH)

        def send_on(slot):
            def one(t, c):
                copy(slot, far_sems.at[y], lax.rem(y + t, ny) * nz + z).start()
                return c
            lax.fori_loop(1, ny, one, 0)

        def start():
            def one(t, c):
                copy(self.gy, first_sems.at[z], y * nz + lax.rem(z + t, nz)).start()
                return c
            lax.fori_loop(1, nz, one, 0)
            send_on(self.gy)

        def near():
            def one(t, c):
                other = lax.rem(z + nz - t, nz)
                copy(y * nz + other, first_sems.at[other], y * nz + other).wait_recv()
                send_on(y * nz + other)
                return c
            lax.fori_loop(1, nz, one, 0)

        def far(other):
            part = buf.at[pl.ds(other * nz, nz)]
            pltpu.make_async_remote_copy(
                src_ref=part, dst_ref=part, send_sem=sems.at[0], recv_sem=far_sems.at[other],
                device_id=(self.gx, other * nz + z), device_id_type=MESH).wait_recv()

        def wait_recv():
            near()
            for t in range(1, ny):
                far(lax.rem(y + t, ny))

        def wait_send():
            part = buf.at[pl.ds(0, self.ny - 1)]
            pltpu.make_async_remote_copy(
                src_ref=part, dst_ref=part, send_sem=sems.at[0], recv_sem=first_sems.at[0],
                device_id=(self.gx, y * nz + lax.rem(z + 1, nz)), device_id_type=MESH).wait_send()

        begin, receive = self.phase(start, wait_recv, wait_send)
        done = self.phases[-1][0]

        def near_then():
            done["received"] = True
            near()

        return begin, receive, near_then, far


def index_columns(idx_ref):
    count = idx_ref.shape[1]
    row = jnp.broadcast_to(idx_ref[...].astype(F32), (count, count))
    diagonal = iota((count, count), 0) == iota((count, count), 1)
    return jnp.sum(jnp.where(diagonal, row, 0.0), axis=1, keepdims=True)


def spread(low, pattern, adapter_column):
    wide = dot(low, pattern)
    owner = (iota(wide.shape, 1) // RANK).astype(F32)
    return jnp.where(owner == adapter_column, wide, 0.0).astype(BF16)


def prepare(net, r, load):
    nx, ny, gx, gy = net.nx, net.ny, net.gx, net.gy
    agents = nx * ny
    tok, lift = r["tok"], r["lift"]
    lane = iota((8, 128), 1)
    frequency = jnp.exp((lane & 63).astype(F32) * (-2.0 * math.log(ROPE_BASE) / HEAD_SIZE))
    angles = (PREFIX_LENGTH + r["len"][0]).astype(F32) * frequency
    cs = jnp.where(lane < 64, jnp.cos(angles), jnp.sin(angles))
    r["cs"][...] = cs
    high = cs.astype(BF16).astype(F32)
    mid = (cs - high).astype(BF16).astype(F32)
    row = iota((8, 128), 0)
    parts = jnp.where(row == 0, high, jnp.where(row == 1, mid, jnp.where(row == 2, cs - high - mid, 0.0)))
    load("tokens")
    tok[gy, :, 0:1024] = r["tokens_v"][...]
    tok[gy, :, 1024:1152] = parts[0:nx].astype(BF16)
    ml = r["ml"]
    load("ml_in")
    ml[gx] = r["ml_in_v"][...]
    load("ql")
    load("kvl")
    place = iota((32, 128), 1) - iota((32, 128), 0)
    kvl = r["kvl_v"][...]
    lift[gx, :, 0:256] = r["ql_v"][...]
    lift[gx, :, 256:384] = (dot(kvl[:, 0].reshape(128, 32), one_hot(place == 64))
                            + dot(kvl[:, 1].reshape(128, 32), one_hot(place == 96))).astype(BF16)
    load("idx")
    r["cols"][...] = jnp.broadcast_to(index_columns(r["idx_v"]), (agents, 128))
    wc, md = r["wc"], r["md"]
    for name in ("down", "kt", "vt", "mdt"):
        load(name)
    wc[...] = jnp.zeros(wc.shape, BF16)
    wc[0:48] = r["down_v"][0]
    wc[128:176] = r["down_v"][1]
    wc[64:96] = r["kt_v"][...]
    wc[96:128] = r["vt_v"][...]
    md[...] = jnp.zeros(md.shape, BF16)
    md[0:16] = r["mdt_v"][0]
    md[16:32] = r["mdt_v"][1]


def swap_blocks(net, r, name):
    source, target = r[name + "_v"], r[name + "_all"]
    width = target.shape[2]
    count = target.shape[0]
    columns = lambda i: pl.ds(pl.multiple_of(i * width, 128), width)
    part = target.at[pl.ds(0, count - 1)]
    return net.exchange("y", lambda p: source.at[:, columns(p)], lambda i: target.at[i], r[name + "_s"], part, part)


def project(net, r, load):
    nx, ny, gx, gy = net.nx, net.ny, net.gx, net.gy
    agents = nx * ny
    tok, lift = r["tok"], r["lift"]
    t_start, t_recv, _, _ = net.relay(tok, r["tok_s"], r["tok_z"], r["tok_f"])
    l_start, l_recv = net.gather("gx", lift, r["lift_s"])
    t_start()
    l_start()
    load("gain")
    load("wq")
    for name in ("pk", "pv"):
        load(name)
    t_recv()
    swaps = [swap_blocks(net, r, name) for name in ("pk", "pv")]
    for swap_start, _ in swaps:
        swap_start()
    adapters = r["cols"][:, 0:1]
    x = tok[:, :, 0:1024].astype(F32).reshape(agents, 1024)
    scaled = (x * r["gain_v"][...]).astype(BF16)
    first = dot_t(scaled, r["wc"][...])
    squares = jnp.sum(x * x, axis=1, keepdims=True)
    lane = iota((agents, 128), 1)
    base = (gy * 2).astype(F32)
    down = jnp.where(adapters == base, first[:, 0:128],
                     jnp.where(adapters == base + 1.0, first[:, 128:256], 0.0))
    down = jnp.where(lane < 3 * RANK, down, jnp.where(lane == 3 * RANK, squares, 0.0))
    rows = agents // nx
    half = rows // 2
    down = down.reshape(nx, 2, half, 128)
    r["rl_src"][...] = down[:, 0] + pltpu.roll(down[:, 1].reshape(nx * half, 128), 64, 1).reshape(nx, half, 128)
    rl_start, rl_recv = net.scatter("gx", r["rl_src"], r["rl"], r["rl_s"])
    rl_start()
    r["rl"][gx] = r["rl_src"][gx]
    r["rm_src"][:, :, 256:384] = first[:, 0:128].reshape(nx, rows, 128)
    r["rm_src"][:, :, 0:256] = dot(scaled, r["wq_v"][...]).reshape(nx, rows, 256)
    rm_start, rm_recv = net.scatter("gx", r["rm_src"], r["rm"], r["rm_s"])
    rm_start()
    r["rm"][gx] = r["rm_src"][gx]
    rl_recv()
    low = jnp.sum(r["rl"][...], axis=0)
    al = r["al"]
    al[gy] = low.astype(BF16)
    al_start, al_recv = net.gather("gy", al, r["al_s"])
    al_start()
    width = nx * 128
    pattern_row, pattern_rank = iota((128, width), 0), iota((128, width), 1) & (RANK - 1)
    patterns = [one_hot(pattern_row == pattern_rank + part * RANK) for part in range(3)]
    square_columns = jnp.concatenate([low[:, 48:49], low[:, 112:113]], axis=0)
    factor = lax.rsqrt(square_columns / (nx * 1024) + EPSILON)
    ctab = jnp.sum(tok[:, :, 1024:1152].astype(F32), axis=1)
    turned = pltpu.roll(ctab, 64, 1)
    front = iota(ctab.shape, 1) < 64
    cosines = jnp.where(front, ctab, turned)
    sines = jnp.where(front, -turned, ctab)
    own_adapter = r["cols"][pl.ds(pl.multiple_of(gx * rows, 8), rows), 0:1]
    rm_recv()
    summed = jnp.sum(r["rm"][...], axis=0)
    l_recv()
    ml_start, ml_recv = net.gather("gx", r["ml"], r["ml_s"])
    ml_start()
    lift_all = lift[...].reshape(width, 384)
    al_recv()
    packed = jnp.sum(al[...].astype(F32), axis=0)
    lowrank = jnp.concatenate([packed, pltpu.roll(packed, 64, 1)], axis=0)
    lowrank = jnp.where(iota((rows, 128), 1) < 3 * RANK, lowrank, 0.0).astype(BF16)
    q_up = dot(spread(lowrank, patterns[0], own_adapter), lift_all[:, 0:256])
    k_up = dot(spread(lowrank, patterns[1], own_adapter), lift_all[:, 256:384])
    v_up = dot(spread(lowrank, patterns[2], own_adapter), lift_all[:, 256:384])
    q = (summed[:, 0:256] + ADAPTER_SCALE * q_up) * factor
    kv_up = jnp.where(iota((rows, 128), 1) < 96, k_up, v_up)
    kv = (summed[:, 256:384] + ADAPTER_SCALE * kv_up) * factor
    qbuf = r["qbuf"]
    heads = []
    for t in range(2):
        u = q[:, t * 128:(t + 1) * 128]
        heads.append((u * cosines + pltpu.roll(u, 64, 1) * sines).astype(BF16))
        qbuf[net.z, :, t * 128:(t + 1) * 128] = heads[t]
    return jnp.concatenate([h.astype(F32) for h in heads] + [kv], axis=1), ml_recv, swaps


def coded_stats(peak, mass, lane, shift):
    rows = peak.shape[0]
    place = (lane - shift) & 127
    value = jnp.where(place < 24, peak, mass)
    high = value.astype(BF16).astype(F32)
    mid = (value - high).astype(BF16).astype(F32)
    low = value - high - mid
    group = place >> 3
    coded = jnp.where((group == 0) | (group == 3), high, jnp.where((group == 1) | (group == 4), mid, low))
    mine = ((lane & 7) == (iota((rows, 128), 0) & 7)) & (group < 6)
    return jnp.where(mine, coded, 0.0)


def joined_stats(coded):
    peaks = coded + pltpu.roll(coded, 120, 1) + pltpu.roll(coded, 112, 1)
    return peaks, pltpu.roll(peaks, 104, 1)


def attend(net, r, load, qkv, swaps):
    nx, ny, gx, gy = net.nx, net.ny, net.gx, net.gy
    nz, y, z = net.nz, net.y, net.z
    rows = ny
    kv_heads = nx
    parts = ny // kv_heads
    y_heads = nz // parts
    inv_root = 1.0 / math.sqrt(HEAD_SIZE)
    qbuf, kvs, kvb, osend, obuf = r["qbuf"], r["kvs"], r["kvb"], r["osend"], r["obuf"]
    q_start, q_recv = net.gather("z", qbuf, r["q_s"])
    q_start()
    for i in range(rows):
        kvs[i] = qkv[i:i + 1, :]

    def place(i):
        return lax.rem(i, parts) * kv_heads + i // parts

    kvb[place(gy)] = kvs[gy]
    k_start, k_recv = net.exchange("gy", lambda p: kvs.at[p], lambda i: kvb.at[place(i)], r["kv_s"],
                                   kvs.at[pl.ds(0, ny - 1)], kvb.at[pl.ds(0, ny - 1)])
    k_start()
    count = rows * 8
    target, source = iota((count, count), 0), iota((count, count), 1)
    perm = one_hot(source == (target & 7) * rows + (target >> 3))
    lanes = iota((count, 128), 1)
    shift = z * 8

    def out_copy(head, t, agent, sent):
        arrived = r["o_r"].at[jnp.where(head == gx, nx + z, gx)]
        return pltpu.make_async_remote_copy(
            src_ref=osend.at[t, agent, pl.ds(0, 10)], dst_ref=obuf.at[gx, z, pl.ds(0, 10)],
            send_sem=r["o_s"].at[sent], recv_sem=arrived, device_id=(head, agent), device_id_type=MESH)

    def one_head(t):
        h = y * y_heads + t
        blocks = [qbuf[t * parts + j, :, k * 128:(k + 1) * 128] for j in range(parts) for k in range(2)]
        qh = dot(perm, jnp.concatenate(blocks, axis=0)).astype(BF16)
        keys = r["pk_all"][:, :, t * 128:(t + 1) * 128].reshape(-1, 128)
        scores = dot_t(qh, keys) * inv_root
        peak = jnp.max(scores, axis=1, keepdims=True)
        weights = jnp.exp(scores - peak)
        mass = jnp.sum(weights, axis=1, keepdims=True)
        if t == 0:
            swaps[1][1]()
        values = r["pv_all"][:, :, t * 128:(t + 1) * 128].reshape(-1, 128)
        out = dot(weights.astype(BF16), values) / mass
        osend[t, :, 0:8, :] = out.reshape(rows, 8, 128).astype(BF16)
        coded = coded_stats(peak, mass, lanes, shift).reshape(rows, 8, 128)
        line = jnp.sum(coded, axis=1, keepdims=True)
        osend[t, :, 8:10, :] = jnp.broadcast_to(line, (rows, 2, 128)).astype(BF16)

        def own(s, c):
            out_copy(h, t, gy, y_heads + t).start()
            return c

        def send(s, c):
            out_copy(h, t, lax.rem(gy + s, ny), t).start()
            return c

        lax.fori_loop(jnp.where(h == gx, 1, 0), 1, own, 0)
        lax.fori_loop(1, ny, send, 0)

    def o_send():
        for t in range(y_heads):
            part = osend.at[t, pl.ds(0, ny - 1), pl.ds(0, 10)]
            pltpu.make_async_remote_copy(
                src_ref=part, dst_ref=part, send_sem=r["o_s"].at[t], recv_sem=r["o_r"].at[0],
                device_id=(gx, lax.rem(gy + 1, ny)), device_id_type=MESH).wait_send()

            def own(s, c):
                out_copy(y * y_heads + t, t, gy, y_heads + t).wait_send()
                return c

            lax.fori_loop(jnp.where(y * y_heads + t == gx, 1, 0), 1, own, 0)

    def o_recv():
        for t in range(1, nx):
            row = lax.rem(gx + t, nx)
            part = obuf.at[row, :, pl.ds(0, 10)]
            pltpu.make_async_remote_copy(
                src_ref=part, dst_ref=part, send_sem=r["o_s"].at[0], recv_sem=r["o_r"].at[row],
                device_id=(gx, lax.rem(gy + 1, ny)), device_id_type=MESH).wait_recv()

        def own(s, c):
            other = lax.rem(z + s, nz)
            part = obuf.at[gx, other, pl.ds(0, 10)]
            pltpu.make_async_remote_copy(
                src_ref=part, dst_ref=part, send_sem=r["o_s"].at[0], recv_sem=r["o_r"].at[nx + other],
                device_id=(gx, lax.rem(gy + 1, ny)), device_id_type=MESH).wait_recv()
            return c

        lax.fori_loop(jnp.where(gx // y_heads == y, 1, 0), nz, own, 0)

    o_start, o_recv = net.phase(lambda: None, o_recv, o_send)
    o_start()
    width = y_heads * 128
    own_columns = pl.ds(pl.multiple_of(y * width, 128), width)
    r["pk_all"][y] = r["pk_v"][:, own_columns]
    r["pv_all"][y] = r["pv_v"][:, own_columns]
    q_recv()
    swaps[0][1]()
    for t in range(y_heads):
        one_head(t)

    def keep(s, c):
        obuf[gx, z, 0:10, :] = osend[lax.rem(gx, y_heads), gy, 0:10, :]
        return c

    lax.fori_loop(jnp.where(gx // y_heads == y, 0, 1), 1, keep, 0)
    k_recv()
    head_row = iota((kv_heads, 128), 0)
    head_lane = iota((kv_heads, 128), 1)
    new_k = jnp.zeros((kv_heads, 128), F32)
    new_v = jnp.zeros((kv_heads, 128), F32)
    for p in range(parts):
        piece = jnp.zeros((kv_heads, 128), F32)
        for h in range(kv_heads):
            piece = jnp.where(head_row == h, kvb[p * kv_heads + h, :, 256:384], piece)
        here = (head_lane >> 5) == p
        new_k = jnp.where(here, pltpu.roll(piece, (32 * p - 64) % 128, 1), new_k)
        new_v = jnp.where(here, pltpu.roll(piece, (32 * p - 96) % 128, 1), new_v)
    ctab = r["cs"][0:kv_heads]
    turned = pltpu.roll(ctab, 64, 1)
    front = head_lane < 64
    cosines = jnp.where(front, ctab, turned)
    sines = jnp.where(front, -turned, ctab)
    new_k = (new_k * cosines + pltpu.roll(new_k, 64, 1) * sines).astype(BF16).astype(F32)
    new_v = new_v.astype(BF16).astype(F32)
    for name in ("sk", "sv"):
        load(name)
    span = r["sk_v"].shape[1]
    live = iota((8, span), 1) < r["len"][0]
    lane = iota((8, 128), 1)
    row8 = iota((8, 128), 0)
    ss, sb = r["ss"], r["sb"]
    for h in range(kv_heads):
        q_own = jnp.zeros((8, 128), F32)
        for g in range(8):
            line = kvb[(g // 2) * kv_heads + h, :, (g % 2) * 128:(g % 2 + 1) * 128]
            q_own = jnp.where(row8 == g, line, q_own)
        scores = dot_t(q_own.astype(BF16), r["sk_v"][0, :, h * 128:(h + 1) * 128]) * inv_root
        scores = jnp.where(live, scores, NEG)
        new_score = jnp.sum(q_own * new_k[h:h + 1, :], axis=1, keepdims=True) * inv_root
        peak = jnp.maximum(jnp.max(scores, axis=1, keepdims=True), new_score)
        weights = jnp.exp(scores - peak)
        new_weight = jnp.exp(new_score - peak)
        mass = jnp.sum(weights, axis=1, keepdims=True) + new_weight
        mixed = dot(weights.astype(BF16), r["sv_v"][0, :, h * 128:(h + 1) * 128]) + new_weight * new_v[h:h + 1, :]
        ss[h, 0:8, :] = (mixed / mass).astype(BF16)
        line = jnp.sum(coded_stats(peak, mass, lane, 0), axis=0, keepdims=True)
        ss[h, 8:10, :] = jnp.broadcast_to(line, (2, 128)).astype(BF16)
    sb[gx, 0:10, :] = ss[gx, 0:10, :]
    s_start, s_recv = net.exchange(
        "gx", lambda p: ss.at[p, pl.ds(0, 10)], lambda i: sb.at[i, pl.ds(0, 10)], r["ss_s"],
        ss.at[pl.ds(0, nx - 1), pl.ds(0, 10)], sb.at[pl.ds(0, nx - 1), pl.ds(0, 10)])
    s_start()

    s_recv()
    o_recv()
    sub = iota((8, 128), 0)
    line_row, line_lane = iota((nz, 128), 0), iota((nz, 128), 1)
    here = (line_lane >> 3) == (line_row & 15)
    zero = jnp.zeros((nx, 128), F32)
    agent_row = iota((nx, 128), 0)
    peaks, masses = zero, zero
    own = zero
    for i in range(nx):
        coded = obuf[i, :, 8:10, :].astype(F32)[:, 0, :]
        peak, mass = joined_stats(coded)
        peak, mass = jnp.where(here, peak, 0.0), jnp.where(here, mass, 0.0)
        peaks = jnp.where(agent_row == i, jnp.sum(peak, axis=0, keepdims=True), peaks)
        masses = jnp.where(agent_row == i, jnp.sum(mass, axis=0, keepdims=True), masses)
        own = jnp.where(agent_row == i, sb[i, 8:10, :].astype(F32)[0:1, :], own)
    peaks = jnp.where(iota((nx, 128), 1) < nz * 8, peaks, NEG)
    own_peak, own_mass = joined_stats(own)
    first = iota((nx, 128), 1) < 8
    own_peak, own_mass = jnp.where(first, own_peak, 0.0), jnp.where(first, own_mass, 0.0)
    for step in (8, 16, 32, 64):
        own_peak = own_peak + pltpu.roll(own_peak, step, 1)
        own_mass = own_mass + pltpu.roll(own_mass, step, 1)
    top = peaks
    for step in (8, 16, 32, 64):
        top = jnp.maximum(top, pltpu.roll(top, step, 1))
    top = jnp.maximum(top, own_peak)
    share = masses * jnp.exp(peaks - top)
    own_share = own_mass * jnp.exp(own_peak - top)
    whole = share
    for step in (8, 16, 32, 64):
        whole = whole + pltpu.roll(whole, step, 1)
    inverse = 1.0 / (whole + own_share)
    diagonal = (lane & 7) == sub
    att = r["att"]
    for i in range(nx):
        wide = jnp.where(diagonal, share[i:i + 1, :] * inverse[i:i + 1, :], 0.0)[:, 0:nz * 8]
        high = wide.astype(BF16)
        both = jnp.concatenate([high.astype(F32), wide - high.astype(F32)], axis=0).astype(BF16)
        values = obuf[i, :, 0:8, :].astype(F32).reshape(nz * 8, 128).astype(BF16)
        mixed = dot(both, values)
        column = jnp.sum(jnp.where(lane == sub, own_share[i:i + 1, :] * inverse[i:i + 1, :], 0.0),
                         axis=1, keepdims=True)
        att[i] = mixed[0:8] + mixed[8:16] + column * sb[i, 0:8, :].astype(F32)


def project_out(net, r, load, ml_recv, y_out):
    nx, ny, gx, gy = net.nx, net.ny, net.gx, net.gy
    agents, rows = nx * ny, ny
    arow, ml = r["arow"], r["ml"]
    count = nx * 8
    target, source = iota((count, count), 0), iota((count, count), 1)
    turn = one_hot(source == lax.rem(target, nx) * 8 + target // nx)
    target, source = iota((agents, agents), 0), iota((agents, agents), 1)
    sort_rows = one_hot(source == lax.rem(target, ny) * nx + target // ny)
    adapters = r["cols"][:, 0:1]
    load("wo")
    turned = dot(turn, r["att"][...].reshape(count, 128).astype(BF16))
    for g in range(8):
        arow[gy, :, g * 128:(g + 1) * 128] = turned[g * nx:(g + 1) * nx, :].astype(BF16)
    g_start, g_recv, _, _ = net.relay(arow, r["ar_s"], r["ar_z"], r["ar_f"])
    g_start()
    width = nx * 128
    pattern_row, pattern_rank = iota((128, width), 0), iota((128, width), 1) & (RANK - 1)
    pattern = one_hot(((pattern_row & (RANK - 1)) == pattern_rank) & (pattern_row < 2 * RANK))
    g_recv()
    gathered = arow[...].astype(F32).reshape(agents, 1024).astype(BF16)
    attention = dot(sort_rows, gathered).astype(BF16)
    mixed = dot_t(attention, r["md"][...])
    lane = iota((agents, 128), 1)
    base = (gy * 2).astype(F32)
    first = (adapters == base) & (lane < RANK)
    second = (adapters == base + 1.0) & (lane >= RANK) & (lane < 2 * RANK)
    quarter = rows // 4
    mixed = jnp.where(first | second, mixed, 0.0).reshape(nx, 4, quarter, 128)
    packed = mixed[:, 0]
    for k in range(1, 4):
        turned = pltpu.roll(mixed[:, k].reshape(nx * quarter, 128), 32 * k, 1)
        packed = packed + turned.reshape(nx, quarter, 128)
    r["xl_src"][...] = packed
    r["xl"][gx] = r["xl_src"][gx]
    x_start, x_recv = net.scatter("gx", r["xl_src"], r["xl"], r["xl_s"])
    x_start()
    r["xm_src"][...] = dot(attention, r["wo_v"][...]).reshape(nx, rows, 256)
    r["xm"][gx] = r["xm_src"][gx]
    m_start, m_recv = net.scatter("gx", r["xm_src"], r["xm"], r["xm_s"])
    m_start()
    x_recv()
    zl = r["zl"]
    zl[gy] = jnp.sum(r["xl"][...], axis=0).astype(BF16)
    z_start, z_recv = net.gather("gy", zl, r["zl_s"])
    z_start()
    own_adapter = r["cols"][pl.ds(pl.multiple_of(gx * rows, 8), rows), 0:1]
    m_recv()
    summed = jnp.sum(r["xm"][...], axis=0)
    ml_recv()
    lift_all = ml[...].reshape(width, 256)
    z_recv()
    packed = jnp.sum(zl[...].astype(F32), axis=0)
    lowmix = jnp.concatenate([packed] + [pltpu.roll(packed, 128 - 32 * k, 1) for k in range(1, 4)], axis=0)
    lowmix = jnp.where(iota((rows, 128), 1) < 2 * RANK, lowmix, 0.0).astype(BF16)
    y = summed + ADAPTER_SCALE * dot(spread(lowmix, pattern, own_adapter), lift_all)
    ys, yb = r["ys"], r["yb"]
    for i in range(rows):
        ys[i] = y[i:i + 1, :]
    yb[gy] = ys[gy]
    y_start, y_recv = net.scatter("gy", ys, yb, r["y_s"])
    y_start()
    y_recv()
    for i in range(ny):
        y_out[:, i * 256:(i + 1) * 256] = yb[i].astype(BF16)


def make_local(nx, ny):
    agents, rows = nx * ny, ny
    nz = min(8, ny // 2)
    sem = pltpu.SemaphoreType.DMA

    def local(tokens, norm_gain, query_matrix, key_matrix, value_matrix, output_matrix, adapter_down,
              query_lift, key_value_lift, mixer_down, mixer_lift, adapter_index, suffix_lengths,
              shared_prefix_keys, shared_prefix_values, private_suffix_keys, private_suffix_values):
        block, heads = shared_prefix_keys.shape[0], nx // (ny // nz)
        arrays = dict(
            tokens=tokens, ml_in=mixer_lift.reshape(128, 256), ql=query_lift.reshape(128, 256), kvl=key_value_lift,
            idx=adapter_index.reshape(1, agents), down=adapter_down.transpose(0, 2, 1), kt=key_matrix.T,
            vt=value_matrix.T, mdt=mixer_down.transpose(0, 2, 1), gain=norm_gain.reshape(1, 1024), wq=query_matrix,
            pk=shared_prefix_keys, pv=shared_prefix_values, sk=private_suffix_keys, sv=private_suffix_values,
            wo=output_matrix)
        scratch = {name + "_v": pltpu.VMEM(a.shape, a.dtype) for name, a in arrays.items()}
        scratch.update({name: pltpu.VMEM(shape, dtype) for name, shape, dtype in [
            ("tok", (ny, nx, 1152), BF16), ("lift", (nx, 128, 384), BF16), ("cols", (agents, 128), F32),
            ("cs", (8, 128), F32), ("wc", (256, 1024), BF16), ("md", (128, 1024), BF16),
            ("rl_src", (nx, rows // 2, 128), F32), ("rl", (nx, rows // 2, 128), F32),
            ("rm_src", (nx, rows, 384), F32), ("rm", (nx, rows, 384), F32), ("al", (ny, rows // 2, 128), BF16),
            ("qbuf", (nz, rows, 256), BF16), ("kvs", (rows, 1, 384), F32), ("kvb", (rows, 1, 384), F32),
            ("pk_all", (ny // nz, block, heads * 128), BF16), ("pv_all", (ny // nz, block, heads * 128), BF16),
            ("osend", (heads, rows, 16, 128), BF16), ("obuf", (nx, nz, 16, 128), BF16),
            ("ss", (nx, 16, 128), BF16), ("sb", (nx, 16, 128), BF16),
            ("att", (nx, 8, 128), F32),
            ("arow", (ny, nx, 1024), BF16), ("ml", (nx, 128, 256), BF16),
            ("xl_src", (nx, rows // 4, 128), F32), ("xl", (nx, rows // 4, 128), F32),
            ("xm_src", (nx, rows, 256), F32), ("xm", (nx, rows, 256), F32), ("zl", (ny, rows // 4, 128), BF16),
            ("ys", (rows, 1, 256), F32), ("yb", (rows, 1, 256), F32)]})
        phases = ["tok", "lift", "rl", "rm", "al", "q", "kv", "ss", "ar", "pk", "pv", "ml", "xl", "xm", "zl", "y"]
        scratch.update({name + "_s": sem((2,)) for name in phases})
        scratch.update({name + "_z": sem((nz,)) for name in ("tok", "ar")})
        scratch.update({name + "_f": sem((ny // nz,)) for name in ("tok", "ar")})
        scratch.update(o_s=sem((2 * heads,)), o_r=sem((nx + nz,)))
        scratch["loads"] = sem((len(arrays),))
        names, extra = list(arrays), list(scratch)

        def kernel(*refs):
            r = dict(zip(names + ["len", "y_out"] + extra, refs))
            copies = {name: pltpu.make_async_copy(r[name], r[name + "_v"], r["loads"].at[i])
                      for i, name in enumerate(names)}
            net = Net(nx, ny)
            net.signal_all()
            for name in names:
                copies[name].start()
            load = lambda name: copies[name].wait()
            prepare(net, r, load)
            net.wait_all()
            qkv, ml_recv, swaps = project(net, r, load)
            attend(net, r, load, qkv, swaps)
            project_out(net, r, load, ml_recv, r["y_out"])
            net.finish()

        any_space = pl.BlockSpec(memory_space=pl.ANY)
        return pl.pallas_call(
            kernel,
            out_shape=jax.ShapeDtypeStruct((1, ny * 256), BF16),
            in_specs=[any_space] * len(names) + [pl.BlockSpec(memory_space=pltpu.SMEM)],
            out_specs=pl.BlockSpec(memory_space=pltpu.VMEM),
            scratch_shapes=[scratch[n] for n in extra],
            compiler_params=pltpu.CompilerParams(
                collective_id=0, has_side_effects=True, vmem_limit_bytes=60 * 1024 * 1024),
        )(*arrays.values(), suffix_lengths)

    return local


def solution(mesh):
    return jax.shard_map(
        make_local(mesh.shape["gx"], mesh.shape["gy"]),
        mesh=mesh,
        in_specs=(
            P("gy", "gx"),
            P("gx"),
            P("gx", "gy"),
            P("gx", "gy"),
            P("gx", "gy"),
            P("gx", "gy"),
            P("gy", "gx", None),
            P("gx", None, "gy"),
            P("gx", None, None, "gy"),
            P("gy", "gx", None),
            P("gx", None, "gy"),
            P(),
            P(("gx", "gy")),
            P("gy", None),
            P("gy", None),
            P(("gx", "gy"), None, None),
            P(("gx", "gy"), None, None),
        ),
        out_specs=P(("gx", "gy"), None),
        check_vma=False,
    )
```

```python
import math

import jax
import jax.numpy as jnp
from jax import lax
from jax.experimental import pallas as pl
from jax.experimental.pallas import tpu as pltpu
from jax.sharding import PartitionSpec as P

MODEL_WIDTH = 8192
HEAD_SIZE = 128
PREFIX_LENGTH = 16384
EPSILON = 1e-05
ADAPTER_SCALE = 2.0
ROPE_BASE = 500000.0
RANK = 16

MESH = pl.DeviceIdType.MESH
F32 = jnp.float32
BF16 = jnp.bfloat16
NEG = -1e30


def iota(shape, dim):
    return lax.broadcasted_iota(jnp.int32, shape, dim)


def one_hot(cond):
    return jnp.where(cond, 1.0, 0.0).astype(BF16)


def dot(a, b):
    return jnp.dot(a, b, preferred_element_type=F32)


def dot_t(a, b):
    return lax.dot_general(a, b, (((1,), (1,)), ((), ())), preferred_element_type=F32)


class Net:
    def __init__(self, gx_count, gy_count):
        self.nx, self.ny = gx_count, gy_count
        self.gx, self.gy = lax.axis_index("gx"), lax.axis_index("gy")
        self.nz = min(8, gy_count // 2)
        self.y, self.z = self.gy // self.nz, lax.rem(self.gy, self.nz)
        self.x, self.core = self.gx // 2, lax.rem(self.gx, 2)
        self.phases = []

    def phase(self, start, wait_recv, wait_send):
        done = dict(started=False, received=False)
        self.phases.append((done, wait_recv, wait_send))

        def begin():
            done["started"] = True
            start()

        def receive():
            done["received"] = True
            wait_recv()

        return begin, receive

    def finish(self):
        for done, wait_recv, wait_send in self.phases:
            if done["started"]:
                if not done["received"]:
                    wait_recv()
                wait_send()

    def along(self, axis):
        if axis == "gy":
            return self.gy, self.ny, lambda p: (self.gx, p)
        if axis == "z":
            return self.z, self.nz, lambda p: (self.gx, self.y * self.nz + p)
        if axis == "y":
            return self.y, self.ny // self.nz, lambda p: (self.gx, p * self.nz + self.z)
        return self.gx, self.nx, lambda p: (p, self.gy)

    def signal_all(self):
        sem = pltpu.get_barrier_semaphore()
        for axis in ("gy", "gx"):
            me, n, dev = self.along(axis)

            def one(s, c):
                pl.semaphore_signal(sem, inc=1, device_id=dev(lax.rem(me + s, n)), device_id_type=MESH)
                return c

            lax.fori_loop(1, n, one, 0)

    def wait_all(self):
        pl.semaphore_wait(pltpu.get_barrier_semaphore(), self.nx + self.ny - 2)

    def exchange(self, axis, src_at, dst_at, sems, all_src, all_dst):
        me, n, dev = self.along(axis)

        def start():
            def one(s, c):
                peer = lax.rem(me + s, n)
                pltpu.make_async_remote_copy(
                    src_ref=src_at(peer), dst_ref=dst_at(me), send_sem=sems.at[0], recv_sem=sems.at[1],
                    device_id=dev(peer), device_id_type=MESH).start()
                return c
            lax.fori_loop(1, n, one, 0)

        def whole():
            return pltpu.make_async_remote_copy(
                src_ref=all_src, dst_ref=all_dst, send_sem=sems.at[0], recv_sem=sems.at[1],
                device_id=dev(lax.rem(me + 1, n)), device_id_type=MESH)

        return self.phase(start, lambda: whole().wait_recv(), lambda: whole().wait_send())

    def gather(self, axis, buf, sems):
        me, n, _ = self.along(axis)
        part = buf.at[pl.ds(0, n - 1)]
        return self.exchange(axis, lambda p: buf.at[me], lambda i: buf.at[i], sems, part, part)

    def scatter(self, axis, src, dst, sems):
        _, n, _ = self.along(axis)
        return self.exchange(axis, lambda p: src.at[p], lambda i: dst.at[i], sems,
                             src.at[pl.ds(0, n - 1)], dst.at[pl.ds(0, n - 1)])

    def relay(self, buf, sems, first_sems, far_sems):
        nz = self.nz
        ny = self.ny // nz
        y, z = self.gy // nz, lax.rem(self.gy, nz)

        def copy(slot, recv, device):
            return pltpu.make_async_remote_copy(
                src_ref=buf.at[slot], dst_ref=buf.at[slot], send_sem=sems.at[0], recv_sem=recv,
                device_id=(self.gx, device), device_id_type=MESH)

        def send_on(slot):
            def one(t, c):
                copy(slot, far_sems.at[y], lax.rem(y + t, ny) * nz + z).start()
                return c
            lax.fori_loop(1, ny, one, 0)

        def start():
            def one(t, c):
                copy(self.gy, first_sems.at[z], y * nz + lax.rem(z + t, nz)).start()
                return c
            lax.fori_loop(1, nz, one, 0)
            send_on(self.gy)

        def near():
            def one(t, c):
                other = lax.rem(z + nz - t, nz)
                copy(y * nz + other, first_sems.at[other], y * nz + other).wait_recv()
                send_on(y * nz + other)
                return c
            lax.fori_loop(1, nz, one, 0)

        def far(other):
            part = buf.at[pl.ds(other * nz, nz)]
            pltpu.make_async_remote_copy(
                src_ref=part, dst_ref=part, send_sem=sems.at[0], recv_sem=far_sems.at[other],
                device_id=(self.gx, other * nz + z), device_id_type=MESH).wait_recv()

        def wait_recv():
            near()
            for t in range(1, ny):
                far(lax.rem(y + t, ny))

        def wait_send():
            part = buf.at[pl.ds(0, self.ny - 1)]
            pltpu.make_async_remote_copy(
                src_ref=part, dst_ref=part, send_sem=sems.at[0], recv_sem=first_sems.at[0],
                device_id=(self.gx, y * nz + lax.rem(z + 1, nz)), device_id_type=MESH).wait_send()

        begin, receive = self.phase(start, wait_recv, wait_send)
        done = self.phases[-1][0]

        def near_then():
            done["received"] = True
            near()

        return begin, receive, near_then, far


def index_columns(idx_ref):
    count = idx_ref.shape[1]
    row = jnp.broadcast_to(idx_ref[...].astype(F32), (count, count))
    diagonal = iota((count, count), 0) == iota((count, count), 1)
    return jnp.sum(jnp.where(diagonal, row, 0.0), axis=1, keepdims=True)


def spread(low, pattern, adapter_column):
    wide = dot(low, pattern)
    owner = (iota(wide.shape, 1) // RANK).astype(F32)
    return jnp.where(owner == adapter_column, wide, 0.0).astype(BF16)


def prepare(net, r, load):
    nx, ny, gx, gy = net.nx, net.ny, net.gx, net.gy
    agents = nx * ny
    tok, lift = r["tok"], r["lift"]
    lane = iota((8, 128), 1)
    frequency = jnp.exp((lane & 63).astype(F32) * (-2.0 * math.log(ROPE_BASE) / HEAD_SIZE))
    angles = (PREFIX_LENGTH + r["len"][0]).astype(F32) * frequency
    cs = jnp.where(lane < 64, jnp.cos(angles), jnp.sin(angles))
    r["cs"][...] = cs
    high = cs.astype(BF16).astype(F32)
    mid = (cs - high).astype(BF16).astype(F32)
    row = iota((8, 128), 0)
    parts = jnp.where(row == 0, high, jnp.where(row == 1, mid, jnp.where(row == 2, cs - high - mid, 0.0)))
    load("tokens")
    tok[gy, :, 0:1024] = r["tokens_v"][...]
    tok[gy, :, 1024:1152] = parts[0:nx].astype(BF16)
    ml = r["ml"]
    load("ml_in")
    ml[gx] = r["ml_in_v"][...]
    load("ql")
    load("kvl")
    place = iota((32, 128), 1) - iota((32, 128), 0)
    kvl = r["kvl_v"][...]
    lift[gx, :, 0:256] = r["ql_v"][...]
    lift[gx, :, 256:384] = (dot(kvl[:, 0].reshape(128, 32), one_hot(place == 64))
                            + dot(kvl[:, 1].reshape(128, 32), one_hot(place == 96))).astype(BF16)
    load("idx")
    r["cols"][...] = jnp.broadcast_to(index_columns(r["idx_v"]), (agents, 128))
    wc, md = r["wc"], r["md"]
    for name in ("down", "kt", "vt", "mdt"):
        load(name)
    wc[...] = jnp.zeros(wc.shape, BF16)
    wc[0:48] = r["down_v"][0]
    wc[128:176] = r["down_v"][1]
    wc[64:96] = r["kt_v"][...]
    wc[96:128] = r["vt_v"][...]
    md[...] = jnp.zeros(md.shape, BF16)
    md[0:16] = r["mdt_v"][0]
    md[16:32] = r["mdt_v"][1]


def swap_blocks(net, r, name):
    source, target = r[name + "_v"], r[name + "_all"]
    width = target.shape[2]
    count = target.shape[0]
    columns = lambda i: pl.ds(pl.multiple_of((i * 2 + net.core) * width, 128), width)
    part = target.at[pl.ds(0, count - 1)]
    return net.exchange("y", lambda p: source.at[:, columns(p)], lambda i: target.at[i], r[name + "_s"], part, part)


def project(net, r, load):
    nx, ny, gx, gy = net.nx, net.ny, net.gx, net.gy
    agents = nx * ny
    tok, lift = r["tok"], r["lift"]
    t_start, t_recv, _, _ = net.relay(tok, r["tok_s"], r["tok_z"], r["tok_f"])
    l_start, l_recv = net.gather("gx", lift, r["lift_s"])
    t_start()
    l_start()
    load("gain")
    load("wq")
    for name in ("pk", "pv"):
        load(name)
    swaps = [swap_blocks(net, r, name) for name in ("pk", "pv")]
    swaps[0][0]()
    t_recv()
    swaps[1][0]()
    adapters = r["cols"][:, 0:1]
    x = tok[:, :, 0:1024].astype(F32).reshape(agents, 1024)
    scaled = (x * r["gain_v"][...]).astype(BF16)
    first = dot_t(scaled, r["wc"][...])
    squares = jnp.sum(x * x, axis=1, keepdims=True)
    lane = iota((agents, 128), 1)
    base = (gy * 2).astype(F32)
    down = jnp.where(adapters == base, first[:, 0:128],
                     jnp.where(adapters == base + 1.0, first[:, 128:256], 0.0))
    down = jnp.where(lane < 3 * RANK, down, jnp.where(lane == 3 * RANK, squares, 0.0))
    rows = agents // nx
    half = rows // 2
    down = down.reshape(nx, 2, half, 128)
    r["rl_src"][...] = down[:, 0] + pltpu.roll(down[:, 1].reshape(nx * half, 128), 64, 1).reshape(nx, half, 128)
    rl_start, rl_recv = net.scatter("gx", r["rl_src"], r["rl"], r["rl_s"])
    rl_start()
    r["rl"][gx] = r["rl_src"][gx]
    r["rm_src"][:, :, 256:384] = first[:, 0:128].reshape(nx, rows, 128)
    r["rm_src"][:, :, 0:256] = dot(scaled, r["wq_v"][...]).reshape(nx, rows, 256)
    rm_start, rm_recv = net.scatter("gx", r["rm_src"], r["rm"], r["rm_s"])
    rm_start()
    r["rm"][gx] = r["rm_src"][gx]
    rl_recv()
    low = jnp.sum(r["rl"][...], axis=0)
    al = r["al"]
    al[gy] = low.astype(BF16)
    al_start, al_recv = net.gather("gy", al, r["al_s"])
    al_start()
    width = nx * 128
    pattern_row, pattern_rank = iota((128, width), 0), iota((128, width), 1) & (RANK - 1)
    patterns = [one_hot(pattern_row == pattern_rank + part * RANK) for part in range(3)]
    square_columns = jnp.concatenate([low[:, 48:49], low[:, 112:113]], axis=0)
    factor = lax.rsqrt(square_columns / (nx * 1024) + EPSILON)
    ctab = jnp.sum(tok[:, :, 1024:1152].astype(F32), axis=1)
    turned = pltpu.roll(ctab, 64, 1)
    front = iota(ctab.shape, 1) < 64
    cosines = jnp.where(front, ctab, turned)
    sines = jnp.where(front, -turned, ctab)
    own_adapter = r["cols"][pl.ds(pl.multiple_of(gx * rows, 8), rows), 0:1]
    rm_recv()
    summed = jnp.sum(r["rm"][...], axis=0)
    l_recv()
    ml_start, ml_recv = net.gather("gx", r["ml"], r["ml_s"])
    ml_start()
    lift_all = lift[...].reshape(width, 384)
    al_recv()
    packed = jnp.sum(al[...].astype(F32), axis=0)
    lowrank = jnp.concatenate([packed, pltpu.roll(packed, 64, 1)], axis=0)
    lowrank = jnp.where(iota((rows, 128), 1) < 3 * RANK, lowrank, 0.0).astype(BF16)
    q_up = dot(spread(lowrank, patterns[0], own_adapter), lift_all[:, 0:256])
    k_up = dot(spread(lowrank, patterns[1], own_adapter), lift_all[:, 256:384])
    v_up = dot(spread(lowrank, patterns[2], own_adapter), lift_all[:, 256:384])
    q = (summed[:, 0:256] + ADAPTER_SCALE * q_up) * factor
    kv_up = jnp.where(iota((rows, 128), 1) < 96, k_up, v_up)
    kv = (summed[:, 256:384] + ADAPTER_SCALE * kv_up) * factor
    heads = []
    for t in range(2):
        u = q[:, t * 128:(t + 1) * 128]
        heads.append((u * cosines + pltpu.roll(u, 64, 1) * sines).astype(BF16))
        r["qown"][:, t * 128:(t + 1) * 128] = heads[t]
    return jnp.concatenate([h.astype(F32) for h in heads] + [kv], axis=1), ml_recv, swaps


def coded_stats(peak, mass, lane, shift):
    rows = peak.shape[0]
    place = (lane - shift) & 127
    value = jnp.where(place < 24, peak, mass)
    high = value.astype(BF16).astype(F32)
    mid = (value - high).astype(BF16).astype(F32)
    low = value - high - mid
    group = place >> 3
    coded = jnp.where((group == 0) | (group == 3), high, jnp.where((group == 1) | (group == 4), mid, low))
    mine = ((lane & 7) == (iota((rows, 128), 0) & 7)) & (group < 6)
    return jnp.where(mine, coded, 0.0)


def joined_stats(coded):
    peaks = coded + pltpu.roll(coded, 120, 1) + pltpu.roll(coded, 112, 1)
    return peaks, pltpu.roll(peaks, 104, 1)


def attend(net, r, load, qkv, swaps):
    nx, ny, gx, gy = net.nx, net.ny, net.gx, net.gy
    nz, y, z = net.nz, net.y, net.z
    rows = ny
    kv_heads = nx
    parts = ny // kv_heads
    assert nz == 2 * parts
    x, core = net.x, net.core
    inv_root = 1.0 / math.sqrt(HEAD_SIZE)
    qbuf, kvs, kvb, osend, obuf = r["qbuf"], r["kvs"], r["kvb"], r["osend"], r["obuf"]
    q_core, q_part = z // parts, lax.rem(z, parts)
    q_same = q_core == core

    def q_copy(s):
        arrived = r["q_r"].at[jnp.where(q_same, q_part, parts)]
        return pltpu.make_async_remote_copy(
            src_ref=r["qown"], dst_ref=qbuf.at[core * parts + q_part], send_sem=r["q_s"].at[jnp.minimum(s, 1)],
            recv_sem=arrived, device_id=(x * 2 + q_core, y * nz + lax.rem(z + s, nz)), device_id_type=MESH)

    def q_wait(part, sent, arrived):
        return pltpu.make_async_remote_copy(
            src_ref=part, dst_ref=part, send_sem=r["q_s"].at[sent], recv_sem=r["q_r"].at[arrived],
            device_id=(gx, y * nz + lax.rem(z + 1, nz)), device_id_type=MESH)

    def q_begin():
        def one(s, c):
            q_copy(s).start()
            return c

        lax.fori_loop(jnp.where(q_same, 1, 0), nz, one, 0)

        def keep(s, c):
            qbuf[core * parts + q_part] = r["qown"][...]
            return c

        lax.fori_loop(jnp.where(q_same, 0, 1), 1, keep, 0)

    def q_receive():
        q_wait(qbuf.at[pl.ds((1 - core) * parts, parts)], 0, parts).wait_recv()

        def one(s, c):
            other = lax.rem(z + s, parts)
            q_wait(qbuf.at[core * parts + other], 0, other).wait_recv()
            return c

        lax.fori_loop(jnp.where(q_same, 1, 0), parts, one, 0)

    def q_sent():
        q_wait(qbuf.at[pl.ds(0, nz - 1)], 1, 0).wait_send()

        def one(s, c):
            q_copy(s).wait_send()
            return c

        lax.fori_loop(jnp.where(q_same, 1, 0), 1, one, 0)

    q_start, q_recv = net.phase(q_begin, q_receive, q_sent)
    q_start()
    for i in range(rows):
        kvs[i] = qkv[i:i + 1, :]

    def place(i):
        return lax.rem(i, parts) * kv_heads + i // parts

    kvb[place(gy)] = kvs[gy]
    k_start, k_recv = net.exchange("gy", lambda p: kvs.at[p], lambda i: kvb.at[place(i)], r["kv_s"],
                                   kvs.at[pl.ds(0, ny - 1)], kvb.at[pl.ds(0, ny - 1)])
    k_start()
    count = rows * 8
    target, source = iota((count, count), 0), iota((count, count), 1)
    perm = one_hot(source == (target & 7) * rows + (target >> 3))
    lanes = iota((count, 128), 1)
    shift = z * 8

    h = y * 2 + core
    mine = h == gx

    def out_copy(k, agent, sent):
        row = x * 2 + k
        arrived = r["o_r"].at[jnp.where(h // 2 == x, nx + k * nz + z, row)]
        return pltpu.make_async_remote_copy(
            src_ref=osend.at[k, agent, pl.ds(0, 10)], dst_ref=obuf.at[row, z, pl.ds(0, 10)],
            send_sem=r["o_s"].at[sent], recv_sem=arrived, device_id=(h, agent), device_id_type=MESH)

    def out_wait(part, sent, arrived):
        return pltpu.make_async_remote_copy(
            src_ref=part, dst_ref=part, send_sem=r["o_s"].at[sent], recv_sem=r["o_r"].at[arrived],
            device_id=(gx, lax.rem(gy + 1, ny)), device_id_type=MESH)

    def one_row(k):
        blocks = [qbuf[k * parts + j, :, t * 128:(t + 1) * 128] for j in range(parts) for t in range(2)]
        qh = dot(perm, jnp.concatenate(blocks, axis=0)).astype(BF16)
        scores = dot_t(qh, r["pk_all"][...].reshape(-1, 128)) * inv_root
        peak = jnp.max(scores, axis=1, keepdims=True)
        weights = jnp.exp(scores - peak)
        mass = jnp.sum(weights, axis=1, keepdims=True)
        if k == 0:
            swaps[1][1]()
        out = dot(weights.astype(BF16), r["pv_all"][...].reshape(-1, 128)) / mass
        osend[k, :, 0:8, :] = out.reshape(rows, 8, 128).astype(BF16)
        coded = coded_stats(peak, mass, lanes, shift).reshape(rows, 8, 128)
        line = jnp.sum(coded, axis=1, keepdims=True)
        osend[k, :, 8:10, :] = jnp.broadcast_to(line, (rows, 2, 128)).astype(BF16)

        def own(s, c):
            out_copy(k, gy, 2 + k).start()
            return c

        def send(s, c):
            out_copy(k, lax.rem(gy + s, ny), k).start()
            return c

        lax.fori_loop(jnp.where(mine, 1, 0), 1, own, 0)
        lax.fori_loop(1, ny, send, 0)

    def o_send():
        for k in range(2):
            out_wait(osend.at[k, pl.ds(0, ny - 1), pl.ds(0, 10)], k, 0).wait_send()

            def own(s, c):
                out_copy(k, gy, 2 + k).wait_send()
                return c

            lax.fori_loop(jnp.where(mine, 1, 0), 1, own, 0)

    def o_recv():
        for k in range(2):
            for t in range(1, nx // 2):
                row = lax.rem(x + t, nx // 2) * 2 + k
                out_wait(obuf.at[row, :, pl.ds(0, 10)], 0, row).wait_recv()

            def own(s, c):
                other = lax.rem(z + s, nz)
                out_wait(obuf.at[x * 2 + k, other, pl.ds(0, 10)], 0, nx + k * nz + other).wait_recv()
                return c

            lax.fori_loop(jnp.where(x == y, 1, 0), nz, own, 0)

    o_start, o_recv = net.phase(lambda: None, o_recv, o_send)
    o_start()
    own_columns = pl.ds(pl.multiple_of(h * 128, 128), 128)
    r["pk_all"][y] = r["pk_v"][:, own_columns]
    r["pv_all"][y] = r["pv_v"][:, own_columns]
    q_recv()
    swaps[0][1]()
    for k in range(2):
        one_row(k)

    def keep(s, c):
        for k in range(2):
            obuf[x * 2 + k, z, 0:10, :] = osend[k, gy, 0:10, :]
        return c

    lax.fori_loop(jnp.where(mine, 0, 1), 1, keep, 0)
    k_recv()
    head_row = iota((kv_heads, 128), 0)
    head_lane = iota((kv_heads, 128), 1)
    new_k = jnp.zeros((kv_heads, 128), F32)
    new_v = jnp.zeros((kv_heads, 128), F32)
    for p in range(parts):
        piece = jnp.zeros((kv_heads, 128), F32)
        for h in range(kv_heads):
            piece = jnp.where(head_row == h, kvb[p * kv_heads + h, :, 256:384], piece)
        here = (head_lane >> 5) == p
        new_k = jnp.where(here, pltpu.roll(piece, (32 * p - 64) % 128, 1), new_k)
        new_v = jnp.where(here, pltpu.roll(piece, (32 * p - 96) % 128, 1), new_v)
    ctab = r["cs"][0:kv_heads]
    turned = pltpu.roll(ctab, 64, 1)
    front = head_lane < 64
    cosines = jnp.where(front, ctab, turned)
    sines = jnp.where(front, -turned, ctab)
    new_k = (new_k * cosines + pltpu.roll(new_k, 64, 1) * sines).astype(BF16).astype(F32)
    new_v = new_v.astype(BF16).astype(F32)
    for name in ("sk", "sv"):
        load(name)
    span = r["sk_v"].shape[1]
    live = iota((8, span), 1) < r["len"][0]
    lane = iota((8, 128), 1)
    row8 = iota((8, 128), 0)
    ss, sb = r["ss"], r["sb"]
    for h in range(kv_heads):
        q_own = jnp.zeros((8, 128), F32)
        for g in range(8):
            line = kvb[(g // 2) * kv_heads + h, :, (g % 2) * 128:(g % 2 + 1) * 128]
            q_own = jnp.where(row8 == g, line, q_own)
        scores = dot_t(q_own.astype(BF16), r["sk_v"][0, :, h * 128:(h + 1) * 128]) * inv_root
        scores = jnp.where(live, scores, NEG)
        new_score = jnp.sum(q_own * new_k[h:h + 1, :], axis=1, keepdims=True) * inv_root
        peak = jnp.maximum(jnp.max(scores, axis=1, keepdims=True), new_score)
        weights = jnp.exp(scores - peak)
        new_weight = jnp.exp(new_score - peak)
        mass = jnp.sum(weights, axis=1, keepdims=True) + new_weight
        mixed = dot(weights.astype(BF16), r["sv_v"][0, :, h * 128:(h + 1) * 128]) + new_weight * new_v[h:h + 1, :]
        ss[h, 0:8, :] = (mixed / mass).astype(BF16)
        line = jnp.sum(coded_stats(peak, mass, lane, 0), axis=0, keepdims=True)
        ss[h, 8:10, :] = jnp.broadcast_to(line, (2, 128)).astype(BF16)
    sb[gx, 0:10, :] = ss[gx, 0:10, :]
    s_start, s_recv = net.exchange(
        "gx", lambda p: ss.at[p, pl.ds(0, 10)], lambda i: sb.at[i, pl.ds(0, 10)], r["ss_s"],
        ss.at[pl.ds(0, nx - 1), pl.ds(0, 10)], sb.at[pl.ds(0, nx - 1), pl.ds(0, 10)])
    s_start()

    s_recv()
    o_recv()
    sub = iota((8, 128), 0)
    line_row, line_lane = iota((nz, 128), 0), iota((nz, 128), 1)
    here = (line_lane >> 3) == (line_row & 15)
    zero = jnp.zeros((nx, 128), F32)
    agent_row = iota((nx, 128), 0)
    peaks, masses = zero, zero
    own = zero
    for i in range(nx):
        coded = obuf[i, :, 8:10, :].astype(F32)[:, 0, :]
        peak, mass = joined_stats(coded)
        peak, mass = jnp.where(here, peak, 0.0), jnp.where(here, mass, 0.0)
        peaks = jnp.where(agent_row == i, jnp.sum(peak, axis=0, keepdims=True), peaks)
        masses = jnp.where(agent_row == i, jnp.sum(mass, axis=0, keepdims=True), masses)
        own = jnp.where(agent_row == i, sb[i, 8:10, :].astype(F32)[0:1, :], own)
    peaks = jnp.where(iota((nx, 128), 1) < nz * 8, peaks, NEG)
    own_peak, own_mass = joined_stats(own)
    first = iota((nx, 128), 1) < 8
    own_peak, own_mass = jnp.where(first, own_peak, 0.0), jnp.where(first, own_mass, 0.0)
    for step in (8, 16, 32, 64):
        own_peak = own_peak + pltpu.roll(own_peak, step, 1)
        own_mass = own_mass + pltpu.roll(own_mass, step, 1)
    top = peaks
    for step in (8, 16, 32, 64):
        top = jnp.maximum(top, pltpu.roll(top, step, 1))
    top = jnp.maximum(top, own_peak)
    share = masses * jnp.exp(peaks - top)
    own_share = own_mass * jnp.exp(own_peak - top)
    whole = share
    for step in (8, 16, 32, 64):
        whole = whole + pltpu.roll(whole, step, 1)
    inverse = 1.0 / (whole + own_share)
    diagonal = (lane & 7) == sub
    att = r["att"]
    for i in range(nx):
        wide = jnp.where(diagonal, share[i:i + 1, :] * inverse[i:i + 1, :], 0.0)[:, 0:nz * 8]
        high = wide.astype(BF16)
        both = jnp.concatenate([high.astype(F32), wide - high.astype(F32)], axis=0).astype(BF16)
        values = obuf[i, :, 0:8, :].astype(F32).reshape(nz * 8, 128).astype(BF16)
        mixed = dot(both, values)
        column = jnp.sum(jnp.where(lane == sub, own_share[i:i + 1, :] * inverse[i:i + 1, :], 0.0),
                         axis=1, keepdims=True)
        att[i] = mixed[0:8] + mixed[8:16] + column * sb[i, 0:8, :].astype(F32)


def project_out(net, r, load, ml_recv, y_out):
    nx, ny, gx, gy = net.nx, net.ny, net.gx, net.gy
    agents, rows = nx * ny, ny
    arow, ml = r["arow"], r["ml"]
    count = nx * 8
    target, source = iota((count, count), 0), iota((count, count), 1)
    turn = one_hot(source == lax.rem(target, nx) * 8 + target // nx)
    target, source = iota((agents, agents), 0), iota((agents, agents), 1)
    sort_rows = one_hot(source == lax.rem(target, ny) * nx + target // ny)
    adapters = r["cols"][:, 0:1]
    load("wo")
    turned = dot(turn, r["att"][...].reshape(count, 128).astype(BF16))
    for g in range(8):
        arow[gy, :, g * 128:(g + 1) * 128] = turned[g * nx:(g + 1) * nx, :].astype(BF16)
    g_start, g_recv, _, _ = net.relay(arow, r["ar_s"], r["ar_z"], r["ar_f"])
    g_start()
    width = nx * 128
    pattern_row, pattern_rank = iota((128, width), 0), iota((128, width), 1) & (RANK - 1)
    pattern = one_hot(((pattern_row & (RANK - 1)) == pattern_rank) & (pattern_row < 2 * RANK))
    g_recv()
    gathered = arow[...].astype(F32).reshape(agents, 1024).astype(BF16)
    attention = dot(sort_rows, gathered).astype(BF16)
    mixed = dot_t(attention, r["md"][...])
    lane = iota((agents, 128), 1)
    base = (gy * 2).astype(F32)
    first = (adapters == base) & (lane < RANK)
    second = (adapters == base + 1.0) & (lane >= RANK) & (lane < 2 * RANK)
    quarter = rows // 4
    mixed = jnp.where(first | second, mixed, 0.0).reshape(nx, 4, quarter, 128)
    packed = mixed[:, 0]
    for k in range(1, 4):
        turned = pltpu.roll(mixed[:, k].reshape(nx * quarter, 128), 32 * k, 1)
        packed = packed + turned.reshape(nx, quarter, 128)
    r["xl_src"][...] = packed
    r["xl"][gx] = r["xl_src"][gx]
    x_start, x_recv = net.scatter("gx", r["xl_src"], r["xl"], r["xl_s"])
    x_start()
    r["xm_src"][...] = dot(attention, r["wo_v"][...]).reshape(nx, rows, 256)
    r["xm"][gx] = r["xm_src"][gx]
    m_start, m_recv = net.scatter("gx", r["xm_src"], r["xm"], r["xm_s"])
    m_start()
    x_recv()
    zl = r["zl"]
    zl[gy] = jnp.sum(r["xl"][...], axis=0).astype(BF16)
    z_start, z_recv = net.gather("gy", zl, r["zl_s"])
    z_start()
    own_adapter = r["cols"][pl.ds(pl.multiple_of(gx * rows, 8), rows), 0:1]
    m_recv()
    summed = jnp.sum(r["xm"][...], axis=0)
    ml_recv()
    lift_all = ml[...].reshape(width, 256)
    z_recv()
    packed = jnp.sum(zl[...].astype(F32), axis=0)
    lowmix = jnp.concatenate([packed] + [pltpu.roll(packed, 128 - 32 * k, 1) for k in range(1, 4)], axis=0)
    lowmix = jnp.where(iota((rows, 128), 1) < 2 * RANK, lowmix, 0.0).astype(BF16)
    y = summed + ADAPTER_SCALE * dot(spread(lowmix, pattern, own_adapter), lift_all)
    ys, yb = r["ys"], r["yb"]
    for i in range(rows):
        ys[i] = y[i:i + 1, :]
    yb[gy] = ys[gy]
    y_start, y_recv = net.scatter("gy", ys, yb, r["y_s"])
    y_start()
    y_recv()
    for i in range(ny):
        y_out[:, i * 256:(i + 1) * 256] = yb[i].astype(BF16)


def make_local(nx, ny):
    agents, rows = nx * ny, ny
    nz = min(8, ny // 2)
    sem = pltpu.SemaphoreType.DMA

    def local(tokens, norm_gain, query_matrix, key_matrix, value_matrix, output_matrix, adapter_down,
              query_lift, key_value_lift, mixer_down, mixer_lift, adapter_index, suffix_lengths,
              shared_prefix_keys, shared_prefix_values, private_suffix_keys, private_suffix_values):
        block = shared_prefix_keys.shape[0]
        arrays = dict(
            tokens=tokens, ml_in=mixer_lift.reshape(128, 256), ql=query_lift.reshape(128, 256), kvl=key_value_lift,
            idx=adapter_index.reshape(1, agents), down=adapter_down.transpose(0, 2, 1), kt=key_matrix.T,
            vt=value_matrix.T, mdt=mixer_down.transpose(0, 2, 1), gain=norm_gain.reshape(1, 1024), wq=query_matrix,
            pk=shared_prefix_keys, pv=shared_prefix_values, sk=private_suffix_keys, sv=private_suffix_values,
            wo=output_matrix)
        scratch = {name + "_v": pltpu.VMEM(a.shape, a.dtype) for name, a in arrays.items()}
        scratch.update({name: pltpu.VMEM(shape, dtype) for name, shape, dtype in [
            ("tok", (ny, nx, 1152), BF16), ("lift", (nx, 128, 384), BF16), ("cols", (agents, 128), F32),
            ("cs", (8, 128), F32), ("wc", (256, 1024), BF16), ("md", (128, 1024), BF16),
            ("rl_src", (nx, rows // 2, 128), F32), ("rl", (nx, rows // 2, 128), F32),
            ("rm_src", (nx, rows, 384), F32), ("rm", (nx, rows, 384), F32), ("al", (ny, rows // 2, 128), BF16),
            ("qbuf", (nz, rows, 256), BF16), ("qown", (rows, 256), BF16), ("kvs", (rows, 1, 384), F32), ("kvb", (rows, 1, 384), F32),
            ("pk_all", (ny // nz, block, 128), BF16), ("pv_all", (ny // nz, block, 128), BF16),
            ("osend", (2, rows, 16, 128), BF16), ("obuf", (nx, nz, 16, 128), BF16),
            ("ss", (nx, 16, 128), BF16), ("sb", (nx, 16, 128), BF16),
            ("att", (nx, 8, 128), F32),
            ("arow", (ny, nx, 1024), BF16), ("ml", (nx, 128, 256), BF16),
            ("xl_src", (nx, rows // 4, 128), F32), ("xl", (nx, rows // 4, 128), F32),
            ("xm_src", (nx, rows, 256), F32), ("xm", (nx, rows, 256), F32), ("zl", (ny, rows // 4, 128), BF16),
            ("ys", (rows, 1, 256), F32), ("yb", (rows, 1, 256), F32)]})
        phases = ["tok", "lift", "rl", "rm", "al", "q", "kv", "ss", "ar", "pk", "pv", "ml", "xl", "xm", "zl", "y"]
        scratch.update({name + "_s": sem((2,)) for name in phases})
        scratch.update({name + "_z": sem((nz,)) for name in ("tok", "ar")})
        scratch.update({name + "_f": sem((ny // nz,)) for name in ("tok", "ar")})
        scratch.update(o_s=sem((4,)), o_r=sem((nx + 2 * nz,)), q_r=sem((nz,)))
        scratch["loads"] = sem((len(arrays),))
        names, extra = list(arrays), list(scratch)

        def kernel(*refs):
            r = dict(zip(names + ["len", "y_out"] + extra, refs))
            copies = {name: pltpu.make_async_copy(r[name], r[name + "_v"], r["loads"].at[i])
                      for i, name in enumerate(names)}
            net = Net(nx, ny)
            net.signal_all()
            for name in names:
                copies[name].start()
            load = lambda name: copies[name].wait()
            prepare(net, r, load)
            net.wait_all()
            qkv, ml_recv, swaps = project(net, r, load)
            attend(net, r, load, qkv, swaps)
            project_out(net, r, load, ml_recv, r["y_out"])
            net.finish()

        any_space = pl.BlockSpec(memory_space=pl.ANY)
        return pl.pallas_call(
            kernel,
            out_shape=jax.ShapeDtypeStruct((1, ny * 256), BF16),
            in_specs=[any_space] * len(names) + [pl.BlockSpec(memory_space=pltpu.SMEM)],
            out_specs=pl.BlockSpec(memory_space=pltpu.VMEM),
            scratch_shapes=[scratch[n] for n in extra],
            compiler_params=pltpu.CompilerParams(
                collective_id=0, has_side_effects=True, vmem_limit_bytes=60 * 1024 * 1024),
        )(*arrays.values(), suffix_lengths)

    return local


def solution(mesh):
    return jax.shard_map(
        make_local(mesh.shape["gx"], mesh.shape["gy"]),
        mesh=mesh,
        in_specs=(
            P("gy", "gx"),
            P("gx"),
            P("gx", "gy"),
            P("gx", "gy"),
            P("gx", "gy"),
            P("gx", "gy"),
            P("gy", "gx", None),
            P("gx", None, "gy"),
            P("gx", None, None, "gy"),
            P("gy", "gx", None),
            P("gx", None, "gy"),
            P(),
            P(("gx", "gy")),
            P("gy", None),
            P("gy", None),
            P(("gx", "gy"), None, None),
            P(("gx", "gy"), None, None),
        ),
        out_specs=P(("gx", "gy"), None),
        check_vma=False,
    )
```

```python
import math

import jax
import jax.numpy as jnp
from jax import lax
from jax.experimental import pallas as pl
from jax.experimental.pallas import tpu as pltpu
from jax.sharding import PartitionSpec as P

MODEL_WIDTH = 8192
HEAD_SIZE = 128
PREFIX_LENGTH = 16384
EPSILON = 1e-05
ADAPTER_SCALE = 2.0
ROPE_BASE = 500000.0
RANK = 16

MESH = pl.DeviceIdType.MESH
F32 = jnp.float32
BF16 = jnp.bfloat16
NEG = -1e30


def iota(shape, dim):
    return lax.broadcasted_iota(jnp.int32, shape, dim)


def one_hot(cond):
    return jnp.where(cond, 1.0, 0.0).astype(BF16)


def dot(a, b):
    return jnp.dot(a, b, preferred_element_type=F32)


def dot_t(a, b):
    return lax.dot_general(a, b, (((1,), (1,)), ((), ())), preferred_element_type=F32)


class Net:
    def __init__(self, gx_count, gy_count):
        self.nx, self.ny = gx_count, gy_count
        self.gx, self.gy = lax.axis_index("gx"), lax.axis_index("gy")
        self.nz = min(8, gy_count // 2)
        self.y, self.z = self.gy // self.nz, lax.rem(self.gy, self.nz)
        self.x, self.core = self.gx // 2, lax.rem(self.gx, 2)
        self.phases = []

    def phase(self, start, wait_recv, wait_send):
        done = dict(started=False, received=False)
        self.phases.append((done, wait_recv, wait_send))

        def begin():
            done["started"] = True
            start()

        def receive():
            done["received"] = True
            wait_recv()

        return begin, receive

    def finish(self):
        for done, wait_recv, wait_send in self.phases:
            if done["started"]:
                if not done["received"]:
                    wait_recv()
                wait_send()

    def along(self, axis):
        if axis == "gy":
            return self.gy, self.ny, lambda p: (self.gx, p)
        if axis == "z":
            return self.z, self.nz, lambda p: (self.gx, self.y * self.nz + p)
        if axis == "y":
            return self.y, self.ny // self.nz, lambda p: (self.gx, p * self.nz + self.z)
        return self.gx, self.nx, lambda p: (p, self.gy)

    def signal_all(self):
        sem = pltpu.get_barrier_semaphore()
        for axis in ("gy", "gx"):
            me, n, dev = self.along(axis)

            def one(s, c):
                pl.semaphore_signal(sem, inc=1, device_id=dev(lax.rem(me + s, n)), device_id_type=MESH)
                return c

            lax.fori_loop(1, n, one, 0)

    def wait_all(self):
        pl.semaphore_wait(pltpu.get_barrier_semaphore(), self.nx + self.ny - 2)

    def exchange(self, axis, src_at, dst_at, sems, all_src, all_dst):
        me, n, dev = self.along(axis)

        def start():
            def one(s, c):
                peer = lax.rem(me + s, n)
                pltpu.make_async_remote_copy(
                    src_ref=src_at(peer), dst_ref=dst_at(me), send_sem=sems.at[0], recv_sem=sems.at[1],
                    device_id=dev(peer), device_id_type=MESH).start()
                return c
            lax.fori_loop(1, n, one, 0)

        def whole():
            return pltpu.make_async_remote_copy(
                src_ref=all_src, dst_ref=all_dst, send_sem=sems.at[0], recv_sem=sems.at[1],
                device_id=dev(lax.rem(me + 1, n)), device_id_type=MESH)

        return self.phase(start, lambda: whole().wait_recv(), lambda: whole().wait_send())

    def gather(self, axis, buf, sems):
        me, n, _ = self.along(axis)
        part = buf.at[pl.ds(0, n - 1)]
        return self.exchange(axis, lambda p: buf.at[me], lambda i: buf.at[i], sems, part, part)

    def scatter(self, axis, src, dst, sems):
        _, n, _ = self.along(axis)
        return self.exchange(axis, lambda p: src.at[p], lambda i: dst.at[i], sems,
                             src.at[pl.ds(0, n - 1)], dst.at[pl.ds(0, n - 1)])

    def relay(self, buf, sems, first_sems, far_sems):
        nz = self.nz
        ny = self.ny // nz
        y, z = self.gy // nz, lax.rem(self.gy, nz)

        def copy(slot, recv, device):
            return pltpu.make_async_remote_copy(
                src_ref=buf.at[slot], dst_ref=buf.at[slot], send_sem=sems.at[0], recv_sem=recv,
                device_id=(self.gx, device), device_id_type=MESH)

        def send_on(slot):
            def one(t, c):
                copy(slot, far_sems.at[y], lax.rem(y + t, ny) * nz + z).start()
                return c
            lax.fori_loop(1, ny, one, 0)

        def start():
            def one(t, c):
                copy(self.gy, first_sems.at[z], y * nz + lax.rem(z + t, nz)).start()
                return c
            lax.fori_loop(1, nz, one, 0)
            send_on(self.gy)

        def near():
            def one(t, c):
                other = lax.rem(z + nz - t, nz)
                copy(y * nz + other, first_sems.at[other], y * nz + other).wait_recv()
                send_on(y * nz + other)
                return c
            lax.fori_loop(1, nz, one, 0)

        def far(other):
            part = buf.at[pl.ds(other * nz, nz)]
            pltpu.make_async_remote_copy(
                src_ref=part, dst_ref=part, send_sem=sems.at[0], recv_sem=far_sems.at[other],
                device_id=(self.gx, other * nz + z), device_id_type=MESH).wait_recv()

        def wait_recv():
            near()
            for t in range(1, ny):
                far(lax.rem(y + t, ny))

        def wait_send():
            part = buf.at[pl.ds(0, self.ny - 1)]
            pltpu.make_async_remote_copy(
                src_ref=part, dst_ref=part, send_sem=sems.at[0], recv_sem=first_sems.at[0],
                device_id=(self.gx, y * nz + lax.rem(z + 1, nz)), device_id_type=MESH).wait_send()

        begin, receive = self.phase(start, wait_recv, wait_send)
        done = self.phases[-1][0]

        def near_then():
            done["received"] = True
            near()

        return begin, receive, near_then, far


def index_columns(idx_ref):
    count = idx_ref.shape[1]
    row = jnp.broadcast_to(idx_ref[...].astype(F32), (count, count))
    diagonal = iota((count, count), 0) == iota((count, count), 1)
    return jnp.sum(jnp.where(diagonal, row, 0.0), axis=1, keepdims=True)


def spread(low, pattern, adapter_column):
    wide = dot(low, pattern)
    owner = (iota(wide.shape, 1) // RANK).astype(F32)
    return jnp.where(owner == adapter_column, wide, 0.0).astype(BF16)


def prepare(net, r, load):
    nx, ny, gx, gy = net.nx, net.ny, net.gx, net.gy
    agents = nx * ny
    tok, lift = r["tok"], r["lift"]
    lane = iota((8, 128), 1)
    frequency = jnp.exp((lane & 63).astype(F32) * (-2.0 * math.log(ROPE_BASE) / HEAD_SIZE))
    angles = (PREFIX_LENGTH + r["len"][0]).astype(F32) * frequency
    cs = jnp.where(lane < 64, jnp.cos(angles), jnp.sin(angles))
    r["cs"][...] = cs
    high = cs.astype(BF16).astype(F32)
    mid = (cs - high).astype(BF16).astype(F32)
    row = iota((8, 128), 0)
    parts = jnp.where(row == 0, high, jnp.where(row == 1, mid, jnp.where(row == 2, cs - high - mid, 0.0)))
    load("tokens")
    tok[gy, :, 0:1024] = r["tokens_v"][...]
    tok[gy, :, 1024:1152] = parts[0:nx].astype(BF16)
    ml = r["ml"]
    load("ml_in")
    ml[gx] = r["ml_in_v"][...]
    load("ql")
    load("kvl")
    place = iota((32, 128), 1) - iota((32, 128), 0)
    kvl = r["kvl_v"][...]
    lift[gx, :, 0:256] = r["ql_v"][...]
    lift[gx, :, 256:384] = (dot(kvl[:, 0].reshape(128, 32), one_hot(place == 64))
                            + dot(kvl[:, 1].reshape(128, 32), one_hot(place == 96))).astype(BF16)
    load("idx")
    r["cols"][...] = jnp.broadcast_to(index_columns(r["idx_v"]), (agents, 128))
    wc, md = r["wc"], r["md"]
    for name in ("down", "kt", "vt", "mdt"):
        load(name)
    wc[...] = jnp.zeros(wc.shape, BF16)
    wc[0:48] = r["down_v"][0]
    wc[128:176] = r["down_v"][1]
    wc[64:96] = r["kt_v"][...]
    wc[96:128] = r["vt_v"][...]
    md[...] = jnp.zeros(md.shape, BF16)
    md[0:16] = r["mdt_v"][0]
    md[16:32] = r["mdt_v"][1]


def swap_blocks(net, r, name):
    source, target = r[name + "_v"], r[name + "_all"]
    width = target.shape[2]
    count = target.shape[0]
    columns = lambda i: pl.ds(pl.multiple_of((i * 2 + net.core) * width, 128), width)
    part = target.at[pl.ds(0, count - 1)]
    return net.exchange("y", lambda p: source.at[:, columns(p)], lambda i: target.at[i], r[name + "_s"], part, part)


def project(net, r, load):
    nx, ny, gx, gy = net.nx, net.ny, net.gx, net.gy
    agents = nx * ny
    tok, lift = r["tok"], r["lift"]
    t_start, t_recv, _, _ = net.relay(tok, r["tok_s"], r["tok_z"], r["tok_f"])
    l_start, l_recv = net.gather("gx", lift, r["lift_s"])
    t_start()
    l_start()
    load("gain")
    load("wq")
    for name in ("pk", "pv"):
        load(name)
    swaps = [swap_blocks(net, r, name) for name in ("pk", "pv")]
    t_recv()
    swaps[0][0]()
    adapters = r["cols"][:, 0:1]
    x = tok[:, :, 0:1024].astype(F32).reshape(agents, 1024)
    scaled = (x * r["gain_v"][...]).astype(BF16)
    first = dot_t(scaled, r["wc"][...])
    squares = jnp.sum(x * x, axis=1, keepdims=True)
    lane = iota((agents, 128), 1)
    base = (gy * 2).astype(F32)
    down = jnp.where(adapters == base, first[:, 0:128],
                     jnp.where(adapters == base + 1.0, first[:, 128:256], 0.0))
    down = jnp.where(lane < 3 * RANK, down, jnp.where(lane == 3 * RANK, squares, 0.0))
    rows = agents // nx
    half = rows // 2
    down = down.reshape(nx, 2, half, 128)
    r["rl_src"][...] = down[:, 0] + pltpu.roll(down[:, 1].reshape(nx * half, 128), 64, 1).reshape(nx, half, 128)
    rl_start, rl_recv = net.scatter("gx", r["rl_src"], r["rl"], r["rl_s"])
    rl_start()
    r["rl"][gx] = r["rl_src"][gx]
    r["rm_src"][:, :, 256:384] = first[:, 0:128].reshape(nx, rows, 128)
    r["rm_src"][:, :, 0:256] = dot(scaled, r["wq_v"][...]).reshape(nx, rows, 256)
    rm_start, rm_recv = net.scatter("gx", r["rm_src"], r["rm"], r["rm_s"])
    rm_start()
    r["rm"][gx] = r["rm_src"][gx]
    rl_recv()
    low = jnp.sum(r["rl"][...], axis=0)
    al = r["al"]
    al[gy] = low.astype(BF16)
    al_start, al_recv = net.gather("gy", al, r["al_s"])
    al_start()
    width = nx * 128
    pattern_row, pattern_rank = iota((128, width), 0), iota((128, width), 1) & (RANK - 1)
    patterns = [one_hot(pattern_row == pattern_rank + part * RANK) for part in range(3)]
    square_columns = jnp.concatenate([low[:, 48:49], low[:, 112:113]], axis=0)
    factor = lax.rsqrt(square_columns / (nx * 1024) + EPSILON)
    ctab = jnp.sum(tok[:, :, 1024:1152].astype(F32), axis=1)
    turned = pltpu.roll(ctab, 64, 1)
    front = iota(ctab.shape, 1) < 64
    cosines = jnp.where(front, ctab, turned)
    sines = jnp.where(front, -turned, ctab)
    own_adapter = r["cols"][pl.ds(pl.multiple_of(gx * rows, 8), rows), 0:1]
    rm_recv()
    summed = jnp.sum(r["rm"][...], axis=0)
    l_recv()
    ml_start, ml_recv = net.gather("gx", r["ml"], r["ml_s"])
    ml_start()
    lift_all = lift[...].reshape(width, 384)
    al_recv()
    swaps[1][0]()
    packed = jnp.sum(al[...].astype(F32), axis=0)
    lowrank = jnp.concatenate([packed, pltpu.roll(packed, 64, 1)], axis=0)
    lowrank = jnp.where(iota((rows, 128), 1) < 3 * RANK, lowrank, 0.0).astype(BF16)
    q_up = dot(spread(lowrank, patterns[0], own_adapter), lift_all[:, 0:256])
    k_up = dot(spread(lowrank, patterns[1], own_adapter), lift_all[:, 256:384])
    v_up = dot(spread(lowrank, patterns[2], own_adapter), lift_all[:, 256:384])
    q = (summed[:, 0:256] + ADAPTER_SCALE * q_up) * factor
    kv_up = jnp.where(iota((rows, 128), 1) < 96, k_up, v_up)
    kv = (summed[:, 256:384] + ADAPTER_SCALE * kv_up) * factor
    heads = []
    for t in range(2):
        u = q[:, t * 128:(t + 1) * 128]
        heads.append((u * cosines + pltpu.roll(u, 64, 1) * sines).astype(BF16))
        r["qown"][:, t * 128:(t + 1) * 128] = heads[t]
    return jnp.concatenate([h.astype(F32) for h in heads] + [kv], axis=1), ml_recv, swaps


def coded_stats(peak, mass, lane, shift):
    rows = peak.shape[0]
    place = (lane - shift) & 127
    value = jnp.where(place < 24, peak, mass)
    high = value.astype(BF16).astype(F32)
    mid = (value - high).astype(BF16).astype(F32)
    low = value - high - mid
    group = place >> 3
    coded = jnp.where((group == 0) | (group == 3), high, jnp.where((group == 1) | (group == 4), mid, low))
    mine = ((lane & 7) == (iota((rows, 128), 0) & 7)) & (group < 6)
    return jnp.where(mine, coded, 0.0)


def joined_stats(coded):
    peaks = coded + pltpu.roll(coded, 120, 1) + pltpu.roll(coded, 112, 1)
    return peaks, pltpu.roll(peaks, 104, 1)


def attend(net, r, load, qkv, swaps):
    nx, ny, gx, gy = net.nx, net.ny, net.gx, net.gy
    nz, y, z = net.nz, net.y, net.z
    rows = ny
    kv_heads = nx
    parts = ny // kv_heads
    assert nz == 2 * parts
    x, core = net.x, net.core
    inv_root = 1.0 / math.sqrt(HEAD_SIZE)
    qbuf, kvs, kvb, osend, obuf = r["qbuf"], r["kvs"], r["kvb"], r["osend"], r["obuf"]
    q_core, q_part = z // parts, lax.rem(z, parts)
    q_same = q_core == core

    def q_copy(s):
        arrived = r["q_r"].at[jnp.where(q_same, q_part, parts)]
        return pltpu.make_async_remote_copy(
            src_ref=r["qown"], dst_ref=qbuf.at[core * parts + q_part], send_sem=r["q_s"].at[jnp.minimum(s, 1)],
            recv_sem=arrived, device_id=(x * 2 + q_core, y * nz + lax.rem(z + s, nz)), device_id_type=MESH)

    def q_wait(part, sent, arrived):
        return pltpu.make_async_remote_copy(
            src_ref=part, dst_ref=part, send_sem=r["q_s"].at[sent], recv_sem=r["q_r"].at[arrived],
            device_id=(gx, y * nz + lax.rem(z + 1, nz)), device_id_type=MESH)

    def q_begin():
        def one(s, c):
            q_copy(s).start()
            return c

        lax.fori_loop(jnp.where(q_same, 1, 0), nz, one, 0)

        def keep(s, c):
            qbuf[core * parts + q_part] = r["qown"][...]
            return c

        lax.fori_loop(jnp.where(q_same, 0, 1), 1, keep, 0)

    def q_receive():
        q_wait(qbuf.at[pl.ds((1 - core) * parts, parts)], 0, parts).wait_recv()

        def one(s, c):
            other = lax.rem(z + s, parts)
            q_wait(qbuf.at[core * parts + other], 0, other).wait_recv()
            return c

        lax.fori_loop(jnp.where(q_same, 1, 0), parts, one, 0)

    def q_sent():
        q_wait(qbuf.at[pl.ds(0, nz - 1)], 1, 0).wait_send()

        def one(s, c):
            q_copy(s).wait_send()
            return c

        lax.fori_loop(jnp.where(q_same, 1, 0), 1, one, 0)

    q_start, q_recv = net.phase(q_begin, q_receive, q_sent)
    q_start()
    for i in range(rows):
        kvs[i] = qkv[i:i + 1, :]

    def place(i):
        return lax.rem(i, parts) * kv_heads + i // parts

    kvb[place(gy)] = kvs[gy]
    k_start, k_recv = net.exchange("gy", lambda p: kvs.at[p], lambda i: kvb.at[place(i)], r["kv_s"],
                                   kvs.at[pl.ds(0, ny - 1)], kvb.at[pl.ds(0, ny - 1)])
    k_start()
    count = rows * 8
    target, source = iota((count, count), 0), iota((count, count), 1)
    perm = one_hot(source == (target & 7) * rows + (target >> 3))
    lanes = iota((count, 128), 1)
    shift = z * 8

    h = y * 2 + core
    mine = h == gx

    def out_copy(k, agent, sent):
        row = x * 2 + k
        arrived = r["o_r"].at[jnp.where(h // 2 == x, nx + k * nz + z, row)]
        return pltpu.make_async_remote_copy(
            src_ref=osend.at[k, agent, pl.ds(0, 10)], dst_ref=obuf.at[row, z, pl.ds(0, 10)],
            send_sem=r["o_s"].at[sent], recv_sem=arrived, device_id=(h, agent), device_id_type=MESH)

    def out_wait(part, sent, arrived):
        return pltpu.make_async_remote_copy(
            src_ref=part, dst_ref=part, send_sem=r["o_s"].at[sent], recv_sem=r["o_r"].at[arrived],
            device_id=(gx, lax.rem(gy + 1, ny)), device_id_type=MESH)

    def one_row(k):
        blocks = [qbuf[k * parts + j, :, t * 128:(t + 1) * 128] for j in range(parts) for t in range(2)]
        qh = dot(perm, jnp.concatenate(blocks, axis=0)).astype(BF16)
        scores = dot_t(qh, r["pk_all"][...].reshape(-1, 128)) * inv_root
        peak = jnp.max(scores, axis=1, keepdims=True)
        weights = jnp.exp(scores - peak)
        mass = jnp.sum(weights, axis=1, keepdims=True)
        if k == 0:
            swaps[1][1]()
        out = dot(weights.astype(BF16), r["pv_all"][...].reshape(-1, 128)) / mass
        osend[k, :, 0:8, :] = out.reshape(rows, 8, 128).astype(BF16)
        coded = coded_stats(peak, mass, lanes, shift).reshape(rows, 8, 128)
        line = jnp.sum(coded, axis=1, keepdims=True)
        osend[k, :, 8:10, :] = jnp.broadcast_to(line, (rows, 2, 128)).astype(BF16)

        def own(s, c):
            out_copy(k, gy, 2 + k).start()
            return c

        def send(s, c):
            out_copy(k, lax.rem(gy + s, ny), k).start()
            return c

        lax.fori_loop(jnp.where(mine, 1, 0), 1, own, 0)
        lax.fori_loop(1, ny, send, 0)

    def o_send():
        for k in range(2):
            out_wait(osend.at[k, pl.ds(0, ny - 1), pl.ds(0, 10)], k, 0).wait_send()

            def own(s, c):
                out_copy(k, gy, 2 + k).wait_send()
                return c

            lax.fori_loop(jnp.where(mine, 1, 0), 1, own, 0)

    def o_recv():
        for k in range(2):
            for t in range(1, nx // 2):
                row = lax.rem(x + t, nx // 2) * 2 + k
                out_wait(obuf.at[row, :, pl.ds(0, 10)], 0, row).wait_recv()

            def own(s, c):
                other = lax.rem(z + s, nz)
                out_wait(obuf.at[x * 2 + k, other, pl.ds(0, 10)], 0, nx + k * nz + other).wait_recv()
                return c

            lax.fori_loop(jnp.where(x == y, 1, 0), nz, own, 0)

    o_start, o_recv = net.phase(lambda: None, o_recv, o_send)
    o_start()
    own_columns = pl.ds(pl.multiple_of(h * 128, 128), 128)
    r["pk_all"][y] = r["pk_v"][:, own_columns]
    r["pv_all"][y] = r["pv_v"][:, own_columns]
    q_recv()
    swaps[0][1]()
    for k in range(2):
        one_row(k)

    def keep(s, c):
        for k in range(2):
            obuf[x * 2 + k, z, 0:10, :] = osend[k, gy, 0:10, :]
        return c

    lax.fori_loop(jnp.where(mine, 0, 1), 1, keep, 0)
    k_recv()
    head_row = iota((kv_heads, 128), 0)
    head_lane = iota((kv_heads, 128), 1)
    new_k = jnp.zeros((kv_heads, 128), F32)
    new_v = jnp.zeros((kv_heads, 128), F32)
    for p in range(parts):
        piece = jnp.zeros((kv_heads, 128), F32)
        for h in range(kv_heads):
            piece = jnp.where(head_row == h, kvb[p * kv_heads + h, :, 256:384], piece)
        here = (head_lane >> 5) == p
        new_k = jnp.where(here, pltpu.roll(piece, (32 * p - 64) % 128, 1), new_k)
        new_v = jnp.where(here, pltpu.roll(piece, (32 * p - 96) % 128, 1), new_v)
    ctab = r["cs"][0:kv_heads]
    turned = pltpu.roll(ctab, 64, 1)
    front = head_lane < 64
    cosines = jnp.where(front, ctab, turned)
    sines = jnp.where(front, -turned, ctab)
    new_k = (new_k * cosines + pltpu.roll(new_k, 64, 1) * sines).astype(BF16).astype(F32)
    new_v = new_v.astype(BF16).astype(F32)
    for name in ("sk", "sv"):
        load(name)
    span = r["sk_v"].shape[1]
    live = iota((8, span), 1) < r["len"][0]
    lane = iota((8, 128), 1)
    row8 = iota((8, 128), 0)
    ss, sb = r["ss"], r["sb"]
    for h in range(kv_heads):
        q_own = jnp.zeros((8, 128), F32)
        for g in range(8):
            line = kvb[(g // 2) * kv_heads + h, :, (g % 2) * 128:(g % 2 + 1) * 128]
            q_own = jnp.where(row8 == g, line, q_own)
        scores = dot_t(q_own.astype(BF16), r["sk_v"][0, :, h * 128:(h + 1) * 128]) * inv_root
        scores = jnp.where(live, scores, NEG)
        new_score = jnp.sum(q_own * new_k[h:h + 1, :], axis=1, keepdims=True) * inv_root
        peak = jnp.maximum(jnp.max(scores, axis=1, keepdims=True), new_score)
        weights = jnp.exp(scores - peak)
        new_weight = jnp.exp(new_score - peak)
        mass = jnp.sum(weights, axis=1, keepdims=True) + new_weight
        mixed = dot(weights.astype(BF16), r["sv_v"][0, :, h * 128:(h + 1) * 128]) + new_weight * new_v[h:h + 1, :]
        ss[h, 0:8, :] = (mixed / mass).astype(BF16)
        line = jnp.sum(coded_stats(peak, mass, lane, 0), axis=0, keepdims=True)
        ss[h, 8:10, :] = jnp.broadcast_to(line, (2, 128)).astype(BF16)
    sb[gx, 0:10, :] = ss[gx, 0:10, :]
    s_start, s_recv = net.exchange(
        "gx", lambda p: ss.at[p, pl.ds(0, 10)], lambda i: sb.at[i, pl.ds(0, 10)], r["ss_s"],
        ss.at[pl.ds(0, nx - 1), pl.ds(0, 10)], sb.at[pl.ds(0, nx - 1), pl.ds(0, 10)])
    s_start()

    s_recv()
    o_recv()
    sub = iota((8, 128), 0)
    line_row, line_lane = iota((nz, 128), 0), iota((nz, 128), 1)
    here = (line_lane >> 3) == (line_row & 15)
    zero = jnp.zeros((nx, 128), F32)
    agent_row = iota((nx, 128), 0)
    peaks, masses = zero, zero
    own = zero
    for i in range(nx):
        coded = obuf[i, :, 8:10, :].astype(F32)[:, 0, :]
        peak, mass = joined_stats(coded)
        peak, mass = jnp.where(here, peak, 0.0), jnp.where(here, mass, 0.0)
        peaks = jnp.where(agent_row == i, jnp.sum(peak, axis=0, keepdims=True), peaks)
        masses = jnp.where(agent_row == i, jnp.sum(mass, axis=0, keepdims=True), masses)
        own = jnp.where(agent_row == i, sb[i, 8:10, :].astype(F32)[0:1, :], own)
    peaks = jnp.where(iota((nx, 128), 1) < nz * 8, peaks, NEG)
    own_peak, own_mass = joined_stats(own)
    first = iota((nx, 128), 1) < 8
    own_peak, own_mass = jnp.where(first, own_peak, 0.0), jnp.where(first, own_mass, 0.0)
    for step in (8, 16, 32, 64):
        own_peak = own_peak + pltpu.roll(own_peak, step, 1)
        own_mass = own_mass + pltpu.roll(own_mass, step, 1)
    top = peaks
    for step in (8, 16, 32, 64):
        top = jnp.maximum(top, pltpu.roll(top, step, 1))
    top = jnp.maximum(top, own_peak)
    share = masses * jnp.exp(peaks - top)
    own_share = own_mass * jnp.exp(own_peak - top)
    whole = share
    for step in (8, 16, 32, 64):
        whole = whole + pltpu.roll(whole, step, 1)
    inverse = 1.0 / (whole + own_share)
    diagonal = (lane & 7) == sub
    att = r["att"]
    for i in range(nx):
        wide = jnp.where(diagonal, share[i:i + 1, :] * inverse[i:i + 1, :], 0.0)[:, 0:nz * 8]
        high = wide.astype(BF16)
        both = jnp.concatenate([high.astype(F32), wide - high.astype(F32)], axis=0).astype(BF16)
        values = obuf[i, :, 0:8, :].astype(F32).reshape(nz * 8, 128).astype(BF16)
        mixed = dot(both, values)
        column = jnp.sum(jnp.where(lane == sub, own_share[i:i + 1, :] * inverse[i:i + 1, :], 0.0),
                         axis=1, keepdims=True)
        att[i] = mixed[0:8] + mixed[8:16] + column * sb[i, 0:8, :].astype(F32)


def project_out(net, r, load, ml_recv, y_out):
    nx, ny, gx, gy = net.nx, net.ny, net.gx, net.gy
    agents, rows = nx * ny, ny
    arow, ml = r["arow"], r["ml"]
    count = nx * 8
    target, source = iota((count, count), 0), iota((count, count), 1)
    turn = one_hot(source == lax.rem(target, nx) * 8 + target // nx)
    target, source = iota((agents, agents), 0), iota((agents, agents), 1)
    sort_rows = one_hot(source == lax.rem(target, ny) * nx + target // ny)
    adapters = r["cols"][:, 0:1]
    load("wo")
    turned = dot(turn, r["att"][...].reshape(count, 128).astype(BF16))
    for g in range(8):
        arow[gy, :, g * 128:(g + 1) * 128] = turned[g * nx:(g + 1) * nx, :].astype(BF16)
    g_start, g_recv, _, _ = net.relay(arow, r["ar_s"], r["ar_z"], r["ar_f"])
    g_start()
    width = nx * 128
    pattern_row, pattern_rank = iota((128, width), 0), iota((128, width), 1) & (RANK - 1)
    pattern = one_hot(((pattern_row & (RANK - 1)) == pattern_rank) & (pattern_row < 2 * RANK))
    g_recv()
    gathered = arow[...].astype(F32).reshape(agents, 1024).astype(BF16)
    attention = dot(sort_rows, gathered).astype(BF16)
    mixed = dot_t(attention, r["md"][...])
    lane = iota((agents, 128), 1)
    base = (gy * 2).astype(F32)
    first = (adapters == base) & (lane < RANK)
    second = (adapters == base + 1.0) & (lane >= RANK) & (lane < 2 * RANK)
    quarter = rows // 4
    mixed = jnp.where(first | second, mixed, 0.0).reshape(nx, 4, quarter, 128)
    packed = mixed[:, 0]
    for k in range(1, 4):
        turned = pltpu.roll(mixed[:, k].reshape(nx * quarter, 128), 32 * k, 1)
        packed = packed + turned.reshape(nx, quarter, 128)
    r["xl_src"][...] = packed
    r["xl"][gx] = r["xl_src"][gx]
    x_start, x_recv = net.scatter("gx", r["xl_src"], r["xl"], r["xl_s"])
    x_start()
    r["xm_src"][...] = dot(attention, r["wo_v"][...]).reshape(nx, rows, 256)
    r["xm"][gx] = r["xm_src"][gx]
    m_start, m_recv = net.scatter("gx", r["xm_src"], r["xm"], r["xm_s"])
    m_start()
    x_recv()
    zl = r["zl"]
    zl[gy] = jnp.sum(r["xl"][...], axis=0).astype(BF16)
    z_start, z_recv = net.gather("gy", zl, r["zl_s"])
    z_start()
    own_adapter = r["cols"][pl.ds(pl.multiple_of(gx * rows, 8), rows), 0:1]
    m_recv()
    summed = jnp.sum(r["xm"][...], axis=0)
    ml_recv()
    lift_all = ml[...].reshape(width, 256)
    z_recv()
    packed = jnp.sum(zl[...].astype(F32), axis=0)
    lowmix = jnp.concatenate([packed] + [pltpu.roll(packed, 128 - 32 * k, 1) for k in range(1, 4)], axis=0)
    lowmix = jnp.where(iota((rows, 128), 1) < 2 * RANK, lowmix, 0.0).astype(BF16)
    y = summed + ADAPTER_SCALE * dot(spread(lowmix, pattern, own_adapter), lift_all)
    ys, yb = r["ys"], r["yb"]
    for i in range(rows):
        ys[i] = y[i:i + 1, :]
    yb[gy] = ys[gy]
    y_start, y_recv = net.scatter("gy", ys, yb, r["y_s"])
    y_start()
    y_recv()
    for i in range(ny):
        y_out[:, i * 256:(i + 1) * 256] = yb[i].astype(BF16)


def make_local(nx, ny):
    agents, rows = nx * ny, ny
    nz = min(8, ny // 2)
    sem = pltpu.SemaphoreType.DMA

    def local(tokens, norm_gain, query_matrix, key_matrix, value_matrix, output_matrix, adapter_down,
              query_lift, key_value_lift, mixer_down, mixer_lift, adapter_index, suffix_lengths,
              shared_prefix_keys, shared_prefix_values, private_suffix_keys, private_suffix_values):
        block = shared_prefix_keys.shape[0]
        arrays = dict(
            tokens=tokens, ml_in=mixer_lift.reshape(128, 256), ql=query_lift.reshape(128, 256), kvl=key_value_lift,
            idx=adapter_index.reshape(1, agents), down=adapter_down.transpose(0, 2, 1), kt=key_matrix.T,
            vt=value_matrix.T, mdt=mixer_down.transpose(0, 2, 1), gain=norm_gain.reshape(1, 1024), wq=query_matrix,
            pk=shared_prefix_keys, pv=shared_prefix_values, sk=private_suffix_keys, sv=private_suffix_values,
            wo=output_matrix)
        scratch = {name + "_v": pltpu.VMEM(a.shape, a.dtype) for name, a in arrays.items()}
        scratch.update({name: pltpu.VMEM(shape, dtype) for name, shape, dtype in [
            ("tok", (ny, nx, 1152), BF16), ("lift", (nx, 128, 384), BF16), ("cols", (agents, 128), F32),
            ("cs", (8, 128), F32), ("wc", (256, 1024), BF16), ("md", (128, 1024), BF16),
            ("rl_src", (nx, rows // 2, 128), F32), ("rl", (nx, rows // 2, 128), F32),
            ("rm_src", (nx, rows, 384), F32), ("rm", (nx, rows, 384), F32), ("al", (ny, rows // 2, 128), BF16),
            ("qbuf", (nz, rows, 256), BF16), ("qown", (rows, 256), BF16), ("kvs", (rows, 1, 384), F32), ("kvb", (rows, 1, 384), F32),
            ("pk_all", (ny // nz, block, 128), BF16), ("pv_all", (ny // nz, block, 128), BF16),
            ("osend", (2, rows, 16, 128), BF16), ("obuf", (nx, nz, 16, 128), BF16),
            ("ss", (nx, 16, 128), BF16), ("sb", (nx, 16, 128), BF16),
            ("att", (nx, 8, 128), F32),
            ("arow", (ny, nx, 1024), BF16), ("ml", (nx, 128, 256), BF16),
            ("xl_src", (nx, rows // 4, 128), F32), ("xl", (nx, rows // 4, 128), F32),
            ("xm_src", (nx, rows, 256), F32), ("xm", (nx, rows, 256), F32), ("zl", (ny, rows // 4, 128), BF16),
            ("ys", (rows, 1, 256), F32), ("yb", (rows, 1, 256), F32)]})
        phases = ["tok", "lift", "rl", "rm", "al", "q", "kv", "ss", "ar", "pk", "pv", "ml", "xl", "xm", "zl", "y"]
        scratch.update({name + "_s": sem((2,)) for name in phases})
        scratch.update({name + "_z": sem((nz,)) for name in ("tok", "ar")})
        scratch.update({name + "_f": sem((ny // nz,)) for name in ("tok", "ar")})
        scratch.update(o_s=sem((4,)), o_r=sem((nx + 2 * nz,)), q_r=sem((nz,)))
        scratch["loads"] = sem((len(arrays),))
        names, extra = list(arrays), list(scratch)

        def kernel(*refs):
            r = dict(zip(names + ["len", "y_out"] + extra, refs))
            copies = {name: pltpu.make_async_copy(r[name], r[name + "_v"], r["loads"].at[i])
                      for i, name in enumerate(names)}
            net = Net(nx, ny)
            net.signal_all()
            for name in names:
                copies[name].start()
            load = lambda name: copies[name].wait()
            prepare(net, r, load)
            net.wait_all()
            qkv, ml_recv, swaps = project(net, r, load)
            attend(net, r, load, qkv, swaps)
            project_out(net, r, load, ml_recv, r["y_out"])
            net.finish()

        any_space = pl.BlockSpec(memory_space=pl.ANY)
        return pl.pallas_call(
            kernel,
            out_shape=jax.ShapeDtypeStruct((1, ny * 256), BF16),
            in_specs=[any_space] * len(names) + [pl.BlockSpec(memory_space=pltpu.SMEM)],
            out_specs=pl.BlockSpec(memory_space=pltpu.VMEM),
            scratch_shapes=[scratch[n] for n in extra],
            compiler_params=pltpu.CompilerParams(
                collective_id=0, has_side_effects=True, vmem_limit_bytes=60 * 1024 * 1024),
        )(*arrays.values(), suffix_lengths)

    return local


def solution(mesh):
    return jax.shard_map(
        make_local(mesh.shape["gx"], mesh.shape["gy"]),
        mesh=mesh,
        in_specs=(
            P("gy", "gx"),
            P("gx"),
            P("gx", "gy"),
            P("gx", "gy"),
            P("gx", "gy"),
            P("gx", "gy"),
            P("gy", "gx", None),
            P("gx", None, "gy"),
            P("gx", None, None, "gy"),
            P("gy", "gx", None),
            P("gx", None, "gy"),
            P(),
            P(("gx", "gy")),
            P("gy", None),
            P("gy", None),
            P(("gx", "gy"), None, None),
            P(("gx", "gy"), None, None),
        ),
        out_specs=P(("gx", "gy"), None),
        check_vma=False,
    )
```
